32 devices in a mesh: tm: 16 (over z, y, x), seq: 2 (over core).
Axes of the slice: x: 2, y: 2, z: 4, core: 2. Of those that a mesh axis runs over, the one named last changes fastest.
Arguments:
- gains: float32 [128, 128, 128], P(('seq', 'tm')), parts along dimension 0, may hold values from -1 to 1
- offsets: float32 [128, 128], P(('seq', 'tm')), parts along dimension 0, may hold values from -8 to 8
- cov_terms: float32 [128, 128, 128], P(('seq', 'tm')), parts along dimension 0, as said below
Outputs:
- smoothed_means: float32 [128, 128], P(('seq', 'tm')), parts along dimension 0
- smoothed_covs: float32 [128, 128, 128], P(('seq', 'tm')), parts along dimension 0
- moments: float32 [256, 128], P('seq'), parts along dimension 0
The draws below stay inside these ranges and needn't reach their ends.
There are 2 independent parts, one for each index of `seq`. The reference program is written for one: setup_inputs(seed, part) draws one part's arguments, and reference() takes and returns one part's arrays. A program takes and returns all parts, laid end to end along the dimension named above; each array names one. Nothing has to cross between parts.
Inputs may be any that keep to these rules, and one draw needn't show every extreme that they name: `cov_terms`: each step's covariance term is symmetric positive definite.
All inputs are finite; a program needn't handle non-finite values.
Results may differ from the reference program's by a relative error of at most 0.00014.
Values sent between devices are 32-bit elements; how exact they have to be, the bound alone decides.
A program may use at most 128 MiB of HBM per device.

```python
import jax
import jax.numpy as jnp
from jax import lax

STATE = 128
WINDOW_COUNT = 64


def rate_table(key):
    starting_element = jax.random.fold_in(key, 7)
    order = jax.random.permutation(jax.random.fold_in(starting_element, 1), STATE)
    slow_count = STATE // 2
    ranking = jnp.argsort(order)
    lagging_indicator = ranking < slow_count
    fast_span = jax.random.uniform(jax.random.fold_in(starting_element, 2), (WINDOW_COUNT, STATE), minval=20.0, maxval=50.0)
    brisk_frequency = jnp.exp(-1.0 / fast_span)
    slow_span = jax.random.uniform(jax.random.fold_in(starting_element, 3), (WINDOW_COUNT, STATE), minval=0.5, maxval=1.0)
    lagging_frequency = jnp.exp(jnp.log(0.5) / WINDOW_COUNT * slow_span)
    recorded_moments = jax.random.randint(jax.random.fold_in(starting_element, 4), (4,), 0, WINDOW_COUNT)
    consecutive_run_span = jnp.where(jnp.any(jnp.arange(WINDOW_COUNT)[:, None] == recorded_moments[None, :], axis=1), 0.6, 1.0)
    measurement_frequency = jnp.where(lagging_indicator[None, :], lagging_frequency * consecutive_run_span[:, None], brisk_frequency)
    return measurement_frequency.astype(jnp.float32)


def frame_table(key):
    raw = jax.random.normal(jax.random.fold_in(key, 11), (WINDOW_COUNT + 1, STATE, STATE), dtype=jnp.float32)

    def one_frame(matrix):
        basis, upper = jnp.linalg.qr(matrix)
        signs = jnp.where(jnp.diagonal(upper) >= 0.0, 1.0, -1.0)
        return basis * signs[None, :]
    return lax.map(one_frame, raw)


def draw_gains(key, part):
    measurement_frequency = rate_table(key)
    snapshot_table = frame_table(key)
    scaled = snapshot_table[:WINDOW_COUNT] * measurement_frequency[:, None, :]
    gain = jnp.einsum('tij,tkj->tik', scaled, snapshot_table[1:], precision=lax.Precision.HIGHEST)
    return gain.astype(jnp.float32)


def draw_offsets(key, part):
    measurement_frequency = rate_table(key)
    snapshot_table = frame_table(key)
    noise = jax.random.truncated_normal(jax.random.fold_in(key, 31), -4.0, 4.0, (WINDOW_COUNT, STATE))
    inner = 2.0 * noise * jnp.sqrt(1.0 - measurement_frequency * measurement_frequency)
    outer = jnp.einsum('tij,tj->ti', snapshot_table[:WINDOW_COUNT], inner, precision=lax.Precision.HIGHEST)
    return jnp.clip(outer, -8.0, 8.0).astype(jnp.float32)


def draw_cov_terms(key, part):
    measurement_frequency = rate_table(key)
    snapshot_table = frame_table(key)
    top_level = 4.0
    level = jnp.exp(jax.random.uniform(jax.random.fold_in(key, 41), (STATE,), minval=jnp.log(0.5), maxval=jnp.log(top_level)))
    jitter = jnp.exp(jax.random.uniform(jax.random.fold_in(key, 42), (WINDOW_COUNT, STATE), minval=jnp.log(0.7), maxval=jnp.log(1.4)))
    diag_part = (1.0 - measurement_frequency * measurement_frequency) * level[None, :] * jitter
    location_list = jax.random.uniform(jax.random.fold_in(key, 43), (WINDOW_COUNT, STATE))
    kernel = jnp.exp(-(location_list[:, :, None] - location_list[:, None, :]) ** 2 / 0.02)
    root = jnp.sqrt(diag_part)
    unit = jnp.eye(STATE, dtype=jnp.float32)
    inner = root[:, :, None] * root[:, None, :] * (0.5 * unit[None] + 0.5 * kernel)
    rotated = jnp.einsum('tij,tjk->tik', snapshot_table[:WINDOW_COUNT], inner, precision=lax.Precision.HIGHEST)
    full = jnp.einsum('tik,tlk->til', rotated, snapshot_table[:WINDOW_COUNT], precision=lax.Precision.HIGHEST)
    full = 0.5 * (full + jnp.swapaxes(full, 1, 2))
    return full.astype(jnp.float32)


def setup_inputs(seed: int = 0, part: int = 0) -> dict:
    key_list = jax.random.split(jax.random.key(seed), 4)
    own_keys = jax.random.split(jax.random.fold_in(key_list[3], part), 4)
    gains = draw_gains(jax.random.fold_in(jax.random.fold_in(key_list[3], part), 71), part)
    offsets = draw_offsets(jax.random.fold_in(jax.random.fold_in(key_list[3], part), 71), part)
    cov_terms = draw_cov_terms(jax.random.fold_in(jax.random.fold_in(key_list[3], part), 71), part)
    return dict(gains=gains, offsets=offsets, cov_terms=cov_terms)


def product(left, right):
    return jnp.dot(left.astype(jnp.float32), right.astype(jnp.float32), precision=lax.Precision.HIGHEST, preferred_element_type=jnp.float32)

def reference(gains, offsets, cov_terms):
    gains = gains.at[WINDOW_COUNT - 1].set(jnp.zeros_like(gains[0]))

    def walk(state_pair, element):
        upcoming_average, cov_next = state_pair
        gain, offset, covariance = element
        mean_now = offset + product(gain, upcoming_average)
        cov_now = covariance + product(product(gain, cov_next), gain.T)
        return ((mean_now, cov_now), (mean_now, cov_now))
    start = (jnp.zeros((STATE,), jnp.float32), jnp.zeros((STATE, STATE), jnp.float32))
    final_pair, outputs = lax.scan(walk, start, (gains, offsets, cov_terms), reverse=True)
    means, covs = outputs
    moments = (jnp.sum(covs, axis=0) + product(means.T, means)) / WINDOW_COUNT
    return (means, covs, moments)
```

```python
import functools

import jax
import jax.numpy as jnp
from jax import lax
from jax.experimental import pallas as pl
from jax.experimental.pallas import tpu as pltpu
from jax.sharding import PartitionSpec as P

F32 = jnp.float32
BF16 = jnp.bfloat16
PAD = 8
GROUP = 16


def split(x):
    hi = x.astype(BF16)
    return hi, (x - hi.astype(F32)).astype(BF16)


def left(x):
    hi, lo = split(x)
    return hi, jnp.concatenate([hi, lo], axis=1)


def right(w):
    hi, lo = split(w)
    return jnp.concatenate([hi, hi], axis=0), lo


def mul(x, w):
    hi, both = x
    w_hi, w_lo = w
    return jnp.dot(both, w_hi, preferred_element_type=F32) + jnp.dot(
        hi, w_lo, preferred_element_type=F32
    )


def kernel(
    n, gains, offsets, covs, means_out, covs_out, mom_out,
    own, ring, suf, z_snd, z_near, top_snd, top_rcv,
    mom, rs_buf, bf_snd, bf_rcv, red, mom_all, mean_rows,
    ring_s, ring_r, z_s, z_r, rs_s, rs_r, bf_s, bf_r, ag_s, ag_r, out_s,
):
    steps, width = gains.shape[0], gains.shape[1]
    lean = width + PAD
    me = lax.axis_index("tm")
    levels = (n.bit_length() - 1) // 2
    quarter = n // 4
    rows = width // GROUP
    place = lax.rem(me, GROUP)
    base = me - place

    def flip(step):
        return me + step * (1 - 2 * lax.rem(lax.div(me, step), 2))

    def digit_of(stride):
        return lax.rem(lax.div(me, stride), 4)

    def peer(stride, j):
        digit = digit_of(stride)
        return me + stride * (lax.rem(digit + j, 4) - digit)

    peers = [base + lax.rem(place + j, GROUP) for j in range(1, GROUP)]
    peers += [peer(4**l, j) for l in range(2, levels) for j in (1, 2, 3)]
    barrier = pltpu.get_barrier_semaphore()
    for to in peers:
        pl.semaphore_signal(barrier, inc=1, device_id={"tm": to}, device_id_type=pl.DeviceIdType.MESH)

    def send(src, dst, s, r, to):
        return pltpu.make_async_remote_copy(
            src_ref=src, dst_ref=dst, send_sem=s, recv_sem=r,
            device_id={"tm": to}, device_id_type=pl.DeviceIdType.MESH,
        )

    def compose(e, f):
        e_psi = e[lean:]
        x = mul(left(f), right(e_psi))
        p = e[:width] + mul(left(e_psi.T), right(x[:width]))
        out = [p, e[width:lean] + x[width:lean]]
        if f.shape[0] > lean:
            out.append(x[lean:])
        return jnp.concatenate(out, axis=0)

    for t in reversed(range(steps)):
        gain = gains[t]
        if t == steps - 1:
            gain = jnp.where(me == n - 1, jnp.zeros_like(gain), gain)
        offset = jnp.broadcast_to(offsets[t : t + 1, :], (PAD, width))
        element = jnp.concatenate([covs[t], offset, gain.T], axis=0)
        own[t] = element if t == steps - 1 else compose(element, own[t + 1])

    def absorb(f):
        for t in range(steps):
            own[t, : f.shape[0]] = compose(own[t], f)

    pl.semaphore_wait(barrier, len(peers))

    def deferred(l):
        digit = digit_of(4**l)

        @pl.when(digit == 0)
        def _():
            suf[...] = compose(ring[l, 1], suf[...])

        @pl.when(digit == 2)
        def _():
            suf[...] = ring[l, 3]

        @pl.when(digit < 3)
        def _():
            absorb(suf[...])

    sends = []
    total = own[0]
    for l in range(levels - 1):
        digit = digit_of(4**l)
        ring[l, digit] = total
        started = []
        for j in (2, 1, 3):
            c = send(
                ring.at[l, digit], ring.at[l, digit], ring_s.at[l, j - 1], ring_r.at[l, j - 1], peer(4**l, j)
            )
            c.start()
            started.append(c)
        if l:
            deferred(l - 1)
        for j in (1, 2, 3):
            came = lax.rem(digit + 4 - j, 4)
            send(
                ring.at[l, came], ring.at[l, came], ring_s.at[l, j - 1], ring_r.at[l, j - 1], peer(4**l, j)
            ).wait_recv()
        sends += started
        high = compose(ring[l, 2], ring[l, 3])
        total = compose(compose(ring[l, 0], ring[l, 1]), high)
        suf[...] = high
    z_snd[...] = total

    q = lax.div(me, quarter)
    down, down2 = lax.rem(me + n - quarter, n), lax.rem(me + n - 2 * quarter, n)
    part = pl.ds(0, lean)
    near_full = send(z_snd, z_near, z_s.at[0], z_r.at[0], down)
    near_lean = send(z_snd.at[part], z_near.at[part], z_s.at[0], z_r.at[0], down)
    top_far = send(top_snd, top_rcv, z_s.at[1], z_r.at[1], down2)
    top_near = send(top_snd, top_rcv, z_s.at[2], z_r.at[1], down)

    @pl.when(q == 3)
    def _():
        near_lean.start()

    @pl.when(q == 1)
    def _():
        near_full.start()

    deferred(levels - 2)

    @pl.when(q == 3)
    def _():
        near_lean.wait_send()

    @pl.when(q == 2)
    def _():
        near_lean.wait_recv()
        top_snd[...] = compose(z_snd[...], z_near[part, :])
        top_far.start()
        top_near.start()
        absorb(z_near[part, :])
        top_far.wait_send()
        top_near.wait_send()

    @pl.when(q == 0)
    def _():
        near_full.wait_recv()
        absorb(z_near[...])

    @pl.when(q < 2)
    def _():
        top_near.wait_recv()
        absorb(top_rcv[...])

    @pl.when(q == 1)
    def _():
        near_full.wait_send()

    out_copies = []
    for t in range(steps):
        out_copies.append(pltpu.make_async_copy(own.at[t, pl.ds(0, width)], covs_out.at[t], out_s.at[t]))
    means = jnp.concatenate([own[t, width : width + 1] for t in range(steps)], axis=0)
    mean_rows[...] = means
    out_copies.append(pltpu.make_async_copy(mean_rows, means_out, out_s.at[steps]))
    sums = own[0, :width]
    for t in range(1, steps):
        sums = sums + own[t, :width]
    m_hi, m_lo = split(means)
    outer = lambda u, v: lax.dot_general(u, v, (((0,), (0,)), ((), ())), preferred_element_type=F32)
    sums = sums + (outer(m_hi, m_hi) + (outer(m_hi, m_lo) + outer(m_lo, m_hi)))
    mom[...] = sums * (1.0 / (steps * n))

    def group_rows(k):
        return pl.ds(pl.multiple_of(k * rows, rows), rows)

    for j in range(1, GROUP):
        to = lax.rem(place + j, GROUP)
        c = send(mom.at[group_rows(to)], rs_buf.at[j - 1], rs_s.at[j - 1], rs_r.at[j - 1], base + to)
        c.start()
        sends.append(c)
    for c in out_copies:
        c.start()
    acc = mom[group_rows(place), :]
    for c, j in zip(sends[1 - GROUP :], range(1, GROUP)):
        c.wait_recv()
        acc = acc + rs_buf[j - 1]
    k = 0
    while GROUP << k < n:
        bf_snd[k] = acc
        c = send(bf_snd.at[k], bf_rcv.at[k], bf_s.at[k], bf_r.at[k], flip(GROUP << k))
        c.start()
        c.wait()
        acc = acc + bf_rcv[k]
        k += 1
    red[...] = acc
    gather = []
    for j in range(1, GROUP):
        to = lax.rem(place + j, GROUP)
        c = send(red, mom_all.at[group_rows(place)], ag_s.at[j - 1], ag_r.at[j - 1], base + to)
        c.start()
        gather.append(c)
    mom_all[group_rows(place), :] = acc
    for c in sends + gather:
        c.wait_send()
    for c in out_copies:
        c.wait()
    for c in gather:
        c.wait_recv()
    last = pltpu.make_async_copy(mom_all, mom_out, out_s.at[steps + 1])
    last.start()
    last.wait()


def hand_over(a, b, c, a_out, b_out, c_out, sems):
    copies = [
        pltpu.make_async_copy(x, y, sems.at[i])
        for i, (x, y) in enumerate(((b, b_out), (c, c_out), (a, a_out)))
    ]
    for copy in copies:
        copy.start()
    for copy in copies:
        copy.wait()


def local(n, gains, offsets, cov_terms):
    steps, width = gains.shape[0], gains.shape[1]
    levels = (n.bit_length() - 1) // 2
    assert n == 4**levels and levels > 1
    slab, lean, rows = 2 * width + PAD, width + PAD, width // GROUP
    far = max(1, (n // GROUP).bit_length() - 1)
    dma = pltpu.SemaphoreType.DMA
    vmem = pl.BlockSpec(memory_space=pltpu.VMEM)
    any_space = pl.BlockSpec(memory_space=pl.ANY)
    shapes = (
        jax.ShapeDtypeStruct((steps, width), F32),
        jax.ShapeDtypeStruct((steps, width, width), F32),
        jax.ShapeDtypeStruct((width, width), F32),
    )
    results = pl.pallas_call(
        functools.partial(kernel, n),
        out_shape=shapes,
        in_specs=[vmem] * 3,
        out_specs=(any_space,) * 3,
        scratch_shapes=[
            pltpu.VMEM((steps, slab, width), F32),
            pltpu.VMEM((levels - 1, 4, slab, width), F32),
            pltpu.VMEM((slab, width), F32),
            pltpu.VMEM((slab, width), F32),
            pltpu.VMEM((slab, width), F32),
            pltpu.VMEM((lean, width), F32),
            pltpu.VMEM((lean, width), F32),
            pltpu.VMEM((width, width), F32),
            pltpu.VMEM((GROUP - 1, rows, width), F32),
            pltpu.VMEM((far, rows, width), F32),
            pltpu.VMEM((far, rows, width), F32),
            pltpu.VMEM((rows, width), F32),
            pltpu.VMEM((width, width), F32),
            pltpu.VMEM((steps, width), F32),
            dma((levels - 1, 3)), dma((levels - 1, 3)),
            dma((3,)), dma((2,)),
            dma((GROUP - 1,)), dma((GROUP - 1,)),
            dma((far,)), dma((far,)),
            dma((GROUP - 1,)), dma((GROUP - 1,)),
            dma((steps + 2,)),
        ],
        compiler_params=pltpu.CompilerParams(collective_id=0, has_side_effects=True),
    )(gains, offsets, cov_terms)
    return pl.pallas_call(
        hand_over,
        out_shape=shapes,
        in_specs=[vmem] * 3,
        out_specs=(any_space,) * 3,
        scratch_shapes=[dma((3,))],
    )(*results)


def kernel16(
    gains, offsets, covs, means_out, covs_out, mom_out,
    own, ring, suf, z_snd, z_near, top_snd, top_rcv, mom, rs_buf, red,
    ring_s, ring_r, z_s, z_r, rs_s, rs_r, ag_s, ag_r,
):
    steps, width = gains.shape[0], gains.shape[1]
    lean = width + PAD
    n = 16
    me, core = lax.axis_index("tm"), lax.axis_index("seq")
    digit, q = lax.rem(me, 4), lax.div(me, 4)
    rows = width // 4
    hosts = [4 + i for i in range(4)]

    def at(tm, seq):
        return {"tm": tm, "seq": seq}

    barrier = pltpu.get_barrier_semaphore()
    for j in range(2 * n - 1):
        to = at(lax.rem(me + 1 + j, n), core) if j < n - 1 else at(lax.rem(me + j, n), 1 - core)
        pl.semaphore_signal(barrier, inc=1, device_id=to, device_id_type=pl.DeviceIdType.MESH)

    def send(src, dst, s, r, to):
        return pltpu.make_async_remote_copy(
            src_ref=src, dst_ref=dst, send_sem=s, recv_sem=r,
            device_id=to, device_id_type=pl.DeviceIdType.MESH,
        )

    def landed(ref, sem):
        send(ref, ref, sem, sem, at(lax.rem(me + 1, n), core)).wait_recv()

    def compose(e, f):
        e_psi = e[lean:]
        x = mul(left(f), right(e_psi))
        p = e[:width] + mul(left(e_psi.T), right(x[:width]))
        out = [p, e[width:lean] + x[width:lean]]
        if f.shape[0] > lean:
            out.append(x[lean:])
        return jnp.concatenate(out, axis=0)

    for t in reversed(range(steps)):
        gain = gains[t]
        if t == steps - 1:
            gain = jnp.where(me == n - 1, jnp.zeros_like(gain), gain)
        offset = jnp.broadcast_to(offsets[t : t + 1, :], (PAD, width))
        element = jnp.concatenate([covs[t], offset, gain.T], axis=0)
        own[t] = element if t == steps - 1 else compose(element, own[t + 1])

    def absorb(f):
        for t in range(steps):
            own[t, : f.shape[0]] = compose(own[t], f)

    pl.semaphore_wait(barrier, 2 * n - 1)

    ring[0] = own[0]
    for j in (2, 1, 3):
        peer = me - digit + lax.rem(digit + j, 4)
        send(ring.at[0], ring.at[4 - j], ring_s, ring_r, at(peer, core)).start()
    landed(ring.at[pl.ds(1, 3)], ring_r)

    def total_of(d):
        return ring[lax.rem(d + 4 - digit, 4)]

    high = compose(total_of(2), total_of(3))
    z_snd[...] = compose(compose(total_of(0), total_of(1)), high)

    down, down2 = lax.rem(me + n - 4, n), lax.rem(me + n - 8, n)
    part = pl.ds(0, lean)
    near_full = send(z_snd, z_near, z_s, z_r.at[0], at(down, core))
    near_lean = send(z_snd.at[part], z_near.at[part], z_s, z_r.at[0], at(down, core))
    top_far = send(top_snd, top_rcv, z_s, z_r.at[1], at(down2, core))
    top_near = send(top_snd, top_rcv, z_s, z_r.at[1], at(down, core))

    @pl.when(q == 3)
    def _():
        near_lean.start()

    @pl.when(q == 1)
    def _():
        near_full.start()

    suf[...] = high

    @pl.when(digit == 0)
    def _():
        suf[...] = compose(total_of(1), suf[...])

    @pl.when(digit == 2)
    def _():
        suf[...] = total_of(3)

    @pl.when(digit < 3)
    def _():
        absorb(suf[...])

    @pl.when(q == 2)
    def _():
        near_lean.wait_recv()
        top_snd[...] = compose(z_snd[...], z_near[part, :])
        top_far.start()
        top_near.start()
        absorb(z_near[part, :])

    @pl.when(q == 0)
    def _():
        near_full.wait_recv()
        absorb(z_near[...])

    @pl.when(q < 2)
    def _():
        top_near.wait_recv()
        absorb(top_rcv[...])

    means = jnp.concatenate([own[t, width : width + 1] for t in range(steps)], axis=0)
    sums = own[0, :width]
    for t in range(1, steps):
        sums = sums + own[t, :width]
    m_hi, m_lo = split(means)
    outer = lambda u, v: lax.dot_general(u, v, (((0,), (0,)), ((), ())), preferred_element_type=F32)
    sums = sums + (outer(m_hi, m_hi) + (outer(m_hi, m_lo) + outer(m_lo, m_hi)))
    mom[...] = sums * (1.0 / (steps * n))

    for i, host in enumerate(hosts):
        block = mom.at[pl.ds(i * rows, rows)]
        slot = rs_buf.at[core, lax.rem(me + n - host, n)]
        scatter = send(block, slot, rs_s, rs_r.at[core], at(host, 1))

        @pl.when(jnp.logical_or(me != host, core == 0))
        def _():
            scatter.start()

    means_out[...] = means
    for t in range(steps):
        covs_out[t] = own[t, :width]

    is_host = jnp.logical_and(q == 1, core == 1)

    @pl.when(is_host)
    def _():
        mine = pl.ds(pl.multiple_of(digit * rows, rows), rows)
        for p in (1, 0):
            first = p
            landed(rs_buf.at[p, pl.ds(first, n - first)], rs_r.at[p])
            acc = rs_buf[p, 1] if p == 0 else rs_buf[p, 1] + mom[mine, :]
            for j in (0, *range(2, n)) if p == 0 else range(2, n):
                acc = acc + rs_buf[p, j]
            red[p] = acc
            for to in range(n):
                gather = send(red.at[p], mom_out.at[mine], ag_s, ag_r, at(to, p))
                if p == 0:
                    gather.start()
                else:
                    pl.when(me != to)(gather.start)
            if p == 1:
                mom_out[mine, :] = acc
        landed(mom_out.at[pl.ds(0, 3 * rows)], ag_r)
        whole = rs_buf.at[0]
        most = rs_buf.at[1, pl.ds(1, n - 1)]
        send(whole, whole, ag_s, ag_r, at(0, 0)).wait_send()
        send(most, most, ag_s, ag_r, at(0, 0)).wait_send()
        three = mom.at[pl.ds(0, 3 * rows)]
        send(three, three, rs_s, ag_r, at(0, 0)).wait_send()

    @pl.when(jnp.logical_not(is_host))
    def _():
        landed(mom_out, ag_r)
        send(mom, mom, rs_s, ag_r, at(4, 1)).wait_send()

    sent = ring.at[pl.ds(1, 3)]
    send(sent, sent, ring_s, ring_r, at(down, core)).wait_send()

    @pl.when(q == 3)
    def _():
        near_lean.wait_send()

    @pl.when(q == 1)
    def _():
        near_full.wait_send()

    @pl.when(q == 2)
    def _():
        top_far.wait_send()
        top_near.wait_send()


def write_out(a, b, c, a_out, b_out, c_out, sems):
    copies = [
        pltpu.make_async_copy(x, y, sems.at[i])
        for i, (x, y) in enumerate(((b, b_out), (c, c_out), (a, a_out)))
    ]
    for copy in copies:
        copy.start()
    for copy in copies:
        copy.wait()


def local16(gains, offsets, cov_terms):
    steps, width = gains.shape[0], gains.shape[1]
    slab, lean, rows = 2 * width + PAD, width + PAD, width // 4
    dma = pltpu.SemaphoreType.DMA
    vmem = pl.BlockSpec(memory_space=pltpu.VMEM)
    shapes = ((steps, width), (steps, width, width), (width, width))
    results = pl.pallas_call(
        kernel16,
        out_shape=tuple(pltpu.VMEM(s, F32) for s in shapes),
        in_specs=[vmem] * 3,
        out_specs=(vmem,) * 3,
        scratch_shapes=[
            pltpu.VMEM((steps, slab, width), F32),
            pltpu.VMEM((4, slab, width), F32),
            pltpu.VMEM((slab, width), F32),
            pltpu.VMEM((slab, width), F32),
            pltpu.VMEM((slab, width), F32),
            pltpu.VMEM((lean, width), F32),
            pltpu.VMEM((lean, width), F32),
            pltpu.VMEM((width, width), F32),
            pltpu.VMEM((2, 16, rows, width), F32),
            pltpu.VMEM((2, rows, width), F32),
            dma, dma, dma, dma((2,)), dma, dma((2,)), dma, dma,
        ],
        compiler_params=pltpu.CompilerParams(collective_id=0, has_side_effects=True),
    )(gains, offsets, cov_terms)
    results = [pltpu.with_memory_space_constraint(r, pltpu.VMEM) for r in results]
    return pl.pallas_call(
        write_out,
        out_shape=tuple(jax.ShapeDtypeStruct(s, F32) for s in shapes),
        in_specs=[vmem] * 3,
        out_specs=(pl.BlockSpec(memory_space=pl.ANY),) * 3,
        scratch_shapes=[dma((3,))],
    )(*results)


def solution(mesh):
    n = mesh.shape["tm"]
    in_specs = (P(("seq", "tm"), None, None), P(("seq", "tm"), None), P(("seq", "tm"), None, None))
    out_specs = (P(("seq", "tm"), None), P(("seq", "tm"), None, None), P("seq", None))
    return jax.shard_map(
        local16 if n == 16 and mesh.shape["seq"] == 2 else functools.partial(local, n), mesh=mesh, in_specs=in_specs, out_specs=out_specs, check_vma=False
    )
```

```python
import functools

import jax
import jax.numpy as jnp
from jax import lax
from jax.experimental import pallas as pl
from jax.experimental.pallas import tpu as pltpu
from jax.sharding import PartitionSpec as P

F32 = jnp.float32
BF16 = jnp.bfloat16
PAD = 8
GROUP = 16


def split(x):
    hi = x.astype(BF16)
    return hi, (x - hi.astype(F32)).astype(BF16)


def left(x):
    hi, lo = split(x)
    return hi, jnp.concatenate([hi, lo], axis=1)


def right(w):
    hi, lo = split(w)
    return jnp.concatenate([hi, hi], axis=0), lo


def mul(x, w):
    hi, both = x
    w_hi, w_lo = w
    return jnp.dot(both, w_hi, preferred_element_type=F32) + jnp.dot(
        hi, w_lo, preferred_element_type=F32
    )


def kernel(
    n, gains, offsets, covs, means_out, covs_out, mom_out,
    own, ring, suf, z_snd, z_near, top_snd, top_rcv,
    mom, rs_buf, bf_snd, bf_rcv, red, mom_all, mean_rows,
    ring_s, ring_r, z_s, z_r, rs_s, rs_r, bf_s, bf_r, ag_s, ag_r, out_s,
):
    steps, width = gains.shape[0], gains.shape[1]
    lean = width + PAD
    me = lax.axis_index("tm")
    levels = (n.bit_length() - 1) // 2
    quarter = n // 4
    rows = width // GROUP
    place = lax.rem(me, GROUP)
    base = me - place

    def flip(step):
        return me + step * (1 - 2 * lax.rem(lax.div(me, step), 2))

    def digit_of(stride):
        return lax.rem(lax.div(me, stride), 4)

    def peer(stride, j):
        digit = digit_of(stride)
        return me + stride * (lax.rem(digit + j, 4) - digit)

    peers = [base + lax.rem(place + j, GROUP) for j in range(1, GROUP)]
    peers += [peer(4**l, j) for l in range(2, levels) for j in (1, 2, 3)]
    barrier = pltpu.get_barrier_semaphore()
    for to in peers:
        pl.semaphore_signal(barrier, inc=1, device_id={"tm": to}, device_id_type=pl.DeviceIdType.MESH)

    def send(src, dst, s, r, to):
        return pltpu.make_async_remote_copy(
            src_ref=src, dst_ref=dst, send_sem=s, recv_sem=r,
            device_id={"tm": to}, device_id_type=pl.DeviceIdType.MESH,
        )

    def compose(e, f):
        e_psi = e[lean:]
        x = mul(left(f), right(e_psi))
        p = e[:width] + mul(left(e_psi.T), right(x[:width]))
        out = [p, e[width:lean] + x[width:lean]]
        if f.shape[0] > lean:
            out.append(x[lean:])
        return jnp.concatenate(out, axis=0)

    for t in reversed(range(steps)):
        gain = gains[t]
        if t == steps - 1:
            gain = jnp.where(me == n - 1, jnp.zeros_like(gain), gain)
        offset = jnp.broadcast_to(offsets[t : t + 1, :], (PAD, width))
        element = jnp.concatenate([covs[t], offset, gain.T], axis=0)
        own[t] = element if t == steps - 1 else compose(element, own[t + 1])

    def absorb(f):
        for t in range(steps):
            own[t, : f.shape[0]] = compose(own[t], f)

    pl.semaphore_wait(barrier, len(peers))

    def deferred(l):
        digit = digit_of(4**l)

        @pl.when(digit == 0)
        def _():
            suf[...] = compose(ring[l, 1], suf[...])

        @pl.when(digit == 2)
        def _():
            suf[...] = ring[l, 3]

        @pl.when(digit < 3)
        def _():
            absorb(suf[...])

    sends = []
    total = own[0]
    for l in range(levels - 1):
        digit = digit_of(4**l)
        ring[l, digit] = total
        started = []
        for j in (2, 1, 3):
            c = send(
                ring.at[l, digit], ring.at[l, digit], ring_s.at[l, j - 1], ring_r.at[l, j - 1], peer(4**l, j)
            )
            c.start()
            started.append(c)
        if l:
            deferred(l - 1)
        for j in (1, 2, 3):
            came = lax.rem(digit + 4 - j, 4)
            send(
                ring.at[l, came], ring.at[l, came], ring_s.at[l, j - 1], ring_r.at[l, j - 1], peer(4**l, j)
            ).wait_recv()
        sends += started
        high = compose(ring[l, 2], ring[l, 3])
        total = compose(compose(ring[l, 0], ring[l, 1]), high)
        suf[...] = high
    z_snd[...] = total

    q = lax.div(me, quarter)
    down, down2 = lax.rem(me + n - quarter, n), lax.rem(me + n - 2 * quarter, n)
    part = pl.ds(0, lean)
    near_full = send(z_snd, z_near, z_s.at[0], z_r.at[0], down)
    near_lean = send(z_snd.at[part], z_near.at[part], z_s.at[0], z_r.at[0], down)
    top_far = send(top_snd, top_rcv, z_s.at[1], z_r.at[1], down2)
    top_near = send(top_snd, top_rcv, z_s.at[2], z_r.at[1], down)

    @pl.when(q == 3)
    def _():
        near_lean.start()

    @pl.when(q == 1)
    def _():
        near_full.start()

    deferred(levels - 2)

    @pl.when(q == 3)
    def _():
        near_lean.wait_send()

    @pl.when(q == 2)
    def _():
        near_lean.wait_recv()
        top_snd[...] = compose(z_snd[...], z_near[part, :])
        top_far.start()
        top_near.start()
        absorb(z_near[part, :])
        top_far.wait_send()
        top_near.wait_send()

    @pl.when(q == 0)
    def _():
        near_full.wait_recv()
        absorb(z_near[...])

    @pl.when(q < 2)
    def _():
        top_near.wait_recv()
        absorb(top_rcv[...])

    @pl.when(q == 1)
    def _():
        near_full.wait_send()

    out_copies = []
    for t in range(steps):
        out_copies.append(pltpu.make_async_copy(own.at[t, pl.ds(0, width)], covs_out.at[t], out_s.at[t]))
    means = jnp.concatenate([own[t, width : width + 1] for t in range(steps)], axis=0)
    mean_rows[...] = means
    out_copies.append(pltpu.make_async_copy(mean_rows, means_out, out_s.at[steps]))
    sums = own[0, :width]
    for t in range(1, steps):
        sums = sums + own[t, :width]
    m_hi, m_lo = split(means)
    outer = lambda u, v: lax.dot_general(u, v, (((0,), (0,)), ((), ())), preferred_element_type=F32)
    sums = sums + (outer(m_hi, m_hi) + (outer(m_hi, m_lo) + outer(m_lo, m_hi)))
    mom[...] = sums * (1.0 / (steps * n))

    def group_rows(k):
        return pl.ds(pl.multiple_of(k * rows, rows), rows)

    for j in range(1, GROUP):
        to = lax.rem(place + j, GROUP)
        c = send(mom.at[group_rows(to)], rs_buf.at[j - 1], rs_s.at[j - 1], rs_r.at[j - 1], base + to)
        c.start()
        sends.append(c)
    for c in out_copies:
        c.start()
    acc = mom[group_rows(place), :]
    for c, j in zip(sends[1 - GROUP :], range(1, GROUP)):
        c.wait_recv()
        acc = acc + rs_buf[j - 1]
    k = 0
    while GROUP << k < n:
        bf_snd[k] = acc
        c = send(bf_snd.at[k], bf_rcv.at[k], bf_s.at[k], bf_r.at[k], flip(GROUP << k))
        c.start()
        c.wait()
        acc = acc + bf_rcv[k]
        k += 1
    red[...] = acc
    gather = []
    for j in range(1, GROUP):
        to = lax.rem(place + j, GROUP)
        c = send(red, mom_all.at[group_rows(place)], ag_s.at[j - 1], ag_r.at[j - 1], base + to)
        c.start()
        gather.append(c)
    mom_all[group_rows(place), :] = acc
    for c in sends + gather:
        c.wait_send()
    for c in out_copies:
        c.wait()
    for c in gather:
        c.wait_recv()
    last = pltpu.make_async_copy(mom_all, mom_out, out_s.at[steps + 1])
    last.start()
    last.wait()


def hand_over(a, b, c, a_out, b_out, c_out, sems):
    copies = [
        pltpu.make_async_copy(x, y, sems.at[i])
        for i, (x, y) in enumerate(((b, b_out), (c, c_out), (a, a_out)))
    ]
    for copy in copies:
        copy.start()
    for copy in copies:
        copy.wait()


def local(n, gains, offsets, cov_terms):
    steps, width = gains.shape[0], gains.shape[1]
    levels = (n.bit_length() - 1) // 2
    assert n == 4**levels and levels > 1
    slab, lean, rows = 2 * width + PAD, width + PAD, width // GROUP
    far = max(1, (n // GROUP).bit_length() - 1)
    dma = pltpu.SemaphoreType.DMA
    vmem = pl.BlockSpec(memory_space=pltpu.VMEM)
    any_space = pl.BlockSpec(memory_space=pl.ANY)
    shapes = (
        jax.ShapeDtypeStruct((steps, width), F32),
        jax.ShapeDtypeStruct((steps, width, width), F32),
        jax.ShapeDtypeStruct((width, width), F32),
    )
    results = pl.pallas_call(
        functools.partial(kernel, n),
        out_shape=shapes,
        in_specs=[vmem] * 3,
        out_specs=(any_space,) * 3,
        scratch_shapes=[
            pltpu.VMEM((steps, slab, width), F32),
            pltpu.VMEM((levels - 1, 4, slab, width), F32),
            pltpu.VMEM((slab, width), F32),
            pltpu.VMEM((slab, width), F32),
            pltpu.VMEM((slab, width), F32),
            pltpu.VMEM((lean, width), F32),
            pltpu.VMEM((lean, width), F32),
            pltpu.VMEM((width, width), F32),
            pltpu.VMEM((GROUP - 1, rows, width), F32),
            pltpu.VMEM((far, rows, width), F32),
            pltpu.VMEM((far, rows, width), F32),
            pltpu.VMEM((rows, width), F32),
            pltpu.VMEM((width, width), F32),
            pltpu.VMEM((steps, width), F32),
            dma((levels - 1, 3)), dma((levels - 1, 3)),
            dma((3,)), dma((2,)),
            dma((GROUP - 1,)), dma((GROUP - 1,)),
            dma((far,)), dma((far,)),
            dma((GROUP - 1,)), dma((GROUP - 1,)),
            dma((steps + 2,)),
        ],
        compiler_params=pltpu.CompilerParams(collective_id=0, has_side_effects=True),
    )(gains, offsets, cov_terms)
    return pl.pallas_call(
        hand_over,
        out_shape=shapes,
        in_specs=[vmem] * 3,
        out_specs=(any_space,) * 3,
        scratch_shapes=[dma((3,))],
    )(*results)


def kernel16(
    gains_in, offsets_in, covs_in, means_out, covs_out, mom_out,
    gains, offsets, covs, own, ring, lower, suf, z_snd, z_near, top_snd, top_rcv, mom, rs_buf, red,
    in_s, ring_s, ring_r, z_s, z_r, rs_s, rs_r, ag_s, ag_r,
):
    steps, width = gains.shape[0], gains.shape[1]
    lean = width + PAD
    n = 16
    me, core = lax.axis_index("tm"), lax.axis_index("seq")
    digit, q = lax.rem(me, 4), lax.div(me, 4)
    rows = width // 4
    hosts = [4 + i for i in range(4)]
    is_host = jnp.logical_and(q == 1, core == 1)
    is_last = me == n - 1
    part, psi = pl.ds(0, lean), pl.ds(lean, width)

    def at(tm, seq):
        return {"tm": tm, "seq": seq}

    def send(src, dst, s, r, to):
        return pltpu.make_async_remote_copy(
            src_ref=src, dst_ref=dst, send_sem=s, recv_sem=r,
            device_id=to, device_id_type=pl.DeviceIdType.MESH,
        )

    def landed(ref, sem):
        send(ref, ref, sem, sem, at(lax.rem(me + 1, n), core)).wait_recv()

    def sent(ref, sem):
        send(ref, ref, sem, sem, at(lax.rem(me + 1, n), core)).wait_send()

    barrier = pltpu.get_barrier_semaphore()

    def greet(tm, seq):
        pl.semaphore_signal(barrier, inc=1, device_id=at(tm, seq), device_id_type=pl.DeviceIdType.MESH)

    @pl.when(is_host)
    def _():
        for j in range(1, n):
            greet(lax.rem(me + j, n), core)
        for j in range(n):
            greet(j, 0)

    @pl.when(jnp.logical_not(is_host))
    def _():
        for j in (1, 2, 3):
            greet(me - digit + lax.rem(digit + j, 4), core)
        for host in hosts:
            greet(host, 1)

        @pl.when(q == 0)
        def _():
            greet(8 + digit, core)

        @pl.when(jnp.logical_or(q == 2, jnp.logical_and(q < 2, core == 0)))
        def _():
            greet(me + 4, core)

    fetch = [
        pltpu.make_async_copy(gains_in, gains, in_s.at[0]),
        pltpu.make_async_copy(covs_in, covs, in_s.at[1]),
        pltpu.make_async_copy(offsets_in, offsets, in_s.at[2]),
    ]
    for c in fetch:
        c.start()

    def compose(e, f):
        e_psi = e[lean:]
        x = mul(left(f), right(e_psi))
        p = e[:width] + mul(left(e_psi.T), right(x[:width]))
        out = [p, e[width:lean] + x[width:lean]]
        if f.shape[0] > lean:
            out.append(x[lean:])
        return jnp.concatenate(out, axis=0)

    def hop(j):
        return me - digit + lax.rem(digit + j, 4)

    def slot(d):
        return lax.rem(d + 4 - digit, 4)

    def total_of(d):
        return ring[slot(d)]

    def exchange(cut):
        for j in (2, 1, 3):
            send(ring.at[0, cut], ring.at[4 - j, cut], ring_s, ring_r.at[4 - j], at(hop(j), core)).start()

    fetch[0].wait()
    ready = jnp.where(q == 1, jnp.where(core == 1, 2 * n - 1, 8), jnp.where(q == 0, 7, jnp.where(q == 2, 9 - core, 8)))

    @pl.when(is_last)
    def _():
        own[steps - 1, psi] = jnp.zeros((width, width), F32)
        for t in range(steps - 1):
            own[t, psi] = jnp.zeros((width, width), F32)
        ring[0, psi] = jnp.zeros((width, width), F32)

    @pl.when(jnp.logical_not(is_last))
    def _():
        run = gains[steps - 1].T
        own[steps - 1, psi] = run
        for t in reversed(range(steps - 1)):
            run = mul(left(run), right(gains[t].T))
            own[t, psi] = run
        ring[0, psi] = run

        @pl.when(q == 3)
        def _():
            ring[slot(3), psi] = jnp.zeros((width, width), F32)

    pl.semaphore_wait(barrier, ready)

    @pl.when(jnp.logical_not(is_last))
    def _():
        exchange(psi)

    fetch[1].wait()
    fetch[2].wait()

    def element(t):
        offset = jnp.broadcast_to(offsets[t : t + 1, :], (PAD, width))
        return jnp.concatenate([covs[t], offset, gains[t].T], axis=0)

    run = element(steps - 1)[:lean]
    own[steps - 1, part] = run
    for t in reversed(range(steps - 1)):
        run = compose(element(t), run)
        own[t, part] = run
    ring[0, part] = run
    exchange(part)

    def absorb(f):
        for t in range(steps):
            own[t, : f.shape[0]] = compose(own[t], f)

    def arrive(d):
        @pl.when(digit != d)
        def _():
            if d == 3:
                @pl.when(q == 3)
                def _():
                    landed(ring.at[slot(d), part], ring_r.at[slot(d)])

                @pl.when(q != 3)
                def _():
                    landed(ring.at[slot(d)], ring_r.at[slot(d)])
            else:
                landed(ring.at[slot(d)], ring_r.at[slot(d)])

    for d in (0, 1, 2):
        arrive(d)
    lower[...] = compose(compose(total_of(0), total_of(1)), total_of(2))
    arrive(3)

    down, down2 = lax.rem(me + n - 4, n), lax.rem(me + n - 8, n)
    near_full = send(z_snd, z_near, z_s, z_r.at[0], at(down, core))
    near_lean = send(z_snd.at[part], z_near.at[part], z_s, z_r.at[0], at(down, core))
    top_far = send(top_snd, top_rcv, z_s, z_r.at[1], at(down2, core))
    top_near = send(top_snd, top_rcv, z_s, z_r.at[1], at(down, core))

    @pl.when(q == 3)
    def _():
        z_snd[part, :] = compose(lower[...], total_of(3)[:lean])
        near_lean.start()

    @pl.when(q < 3)
    def _():
        z_snd[...] = compose(lower[...], total_of(3))

        @pl.when(q == 1)
        def _():
            near_full.start()

    suf[...] = total_of(3)

    @pl.when(digit < 2)
    def _():
        suf[...] = compose(total_of(2), suf[...])

    @pl.when(digit == 0)
    def _():
        suf[...] = compose(total_of(1), suf[...])

    @pl.when(digit < 3)
    def _():
        @pl.when(q == 3)
        def _():
            absorb(suf[part, :])

        @pl.when(q < 3)
        def _():
            absorb(suf[...])

    @pl.when(q == 2)
    def _():
        near_lean.wait_recv()
        top_snd[...] = compose(z_snd[...], z_near[part, :])
        top_far.start()
        top_near.start()
        absorb(z_near[part, :])

    @pl.when(q == 0)
    def _():
        near_full.wait_recv()
        absorb(z_near[...])

    @pl.when(q < 2)
    def _():
        top_near.wait_recv()
        absorb(top_rcv[...])

    means = jnp.concatenate([own[t, width : width + 1] for t in range(steps)], axis=0)
    sums = own[0, :width]
    for t in range(1, steps):
        sums = sums + own[t, :width]
    m_hi, m_lo = split(means)
    outer = lambda u, v: lax.dot_general(u, v, (((0,), (0,)), ((), ())), preferred_element_type=F32)
    sums = sums + (outer(m_hi, m_hi) + (outer(m_hi, m_lo) + outer(m_lo, m_hi)))
    mom[...] = sums * (1.0 / (steps * n))

    for i, host in enumerate(hosts):
        block = mom.at[pl.ds(i * rows, rows)]
        scatter = send(block, rs_buf.at[core, lax.rem(me + n - host, n)], rs_s, rs_r.at[core], at(host, 1))

        @pl.when(jnp.logical_or(me != host, core == 0))
        def _():
            scatter.start()

    means_out[...] = means
    for t in range(steps):
        covs_out[t] = own[t, :width]

    @pl.when(is_host)
    def _():
        mine = pl.ds(pl.multiple_of(digit * rows, rows), rows)
        for p in (1, 0):
            landed(rs_buf.at[p, pl.ds(p, n - p)], rs_r.at[p])
            acc = rs_buf[p, 1] if p == 0 else rs_buf[p, 1] + mom[mine, :]
            for j in (0, *range(2, n)) if p == 0 else range(2, n):
                acc = acc + rs_buf[p, j]
            red[p] = acc
            for to in range(n):
                gather = send(red.at[p], mom_out.at[mine], ag_s, ag_r, at(to, p))
                if p == 0:
                    gather.start()
                else:
                    pl.when(me != to)(gather.start)
            if p == 1:
                mom_out[mine, :] = acc
        landed(mom_out.at[pl.ds(0, 3 * rows)], ag_r)
        sent(rs_buf.at[0], ag_s)
        sent(rs_buf.at[1, pl.ds(1, n - 1)], ag_s)
        sent(mom.at[pl.ds(0, 3 * rows)], rs_s)

    @pl.when(jnp.logical_not(is_host))
    def _():
        landed(mom_out, ag_r)
        sent(mom, rs_s)

    @pl.when(is_last)
    def _():
        sent(ring.at[pl.ds(1, 3), part], ring_s)

    @pl.when(jnp.logical_not(is_last))
    def _():
        sent(ring.at[pl.ds(1, 3)], ring_s)

    @pl.when(q == 3)
    def _():
        near_lean.wait_send()

    @pl.when(q == 1)
    def _():
        near_full.wait_send()

    @pl.when(q == 2)
    def _():
        top_far.wait_send()
        top_near.wait_send()


def write_out(a, b, c, a_out, b_out, c_out, sems):
    copies = [
        pltpu.make_async_copy(x, y, sems.at[i])
        for i, (x, y) in enumerate(((b, b_out), (c, c_out), (a, a_out)))
    ]
    for copy in copies:
        copy.start()
    for copy in copies:
        copy.wait()


def local16(gains, offsets, cov_terms):
    steps, width = gains.shape[0], gains.shape[1]
    slab, lean, rows = 2 * width + PAD, width + PAD, width // 4
    dma = pltpu.SemaphoreType.DMA
    vmem = pl.BlockSpec(memory_space=pltpu.VMEM)
    shapes = ((steps, width), (steps, width, width), (width, width))
    results = pl.pallas_call(
        kernel16,
        out_shape=tuple(pltpu.VMEM(s, F32) for s in shapes),
        in_specs=[pl.BlockSpec(memory_space=pltpu.HBM)] * 3,
        out_specs=(vmem,) * 3,
        scratch_shapes=[
            pltpu.VMEM((steps, width, width), F32),
            pltpu.VMEM((steps, width), F32),
            pltpu.VMEM((steps, width, width), F32),
            pltpu.VMEM((steps, slab, width), F32),
            pltpu.VMEM((4, slab, width), F32),
            pltpu.VMEM((slab, width), F32),
            pltpu.VMEM((slab, width), F32),
            pltpu.VMEM((slab, width), F32),
            pltpu.VMEM((slab, width), F32),
            pltpu.VMEM((lean, width), F32),
            pltpu.VMEM((lean, width), F32),
            pltpu.VMEM((width, width), F32),
            pltpu.VMEM((2, 16, rows, width), F32),
            pltpu.VMEM((2, rows, width), F32),
            dma((3,)), dma, dma((4,)), dma, dma((2,)), dma, dma((2,)), dma, dma,
        ],
        compiler_params=pltpu.CompilerParams(collective_id=0, has_side_effects=True),
    )(gains, offsets, cov_terms)
    results = [pltpu.with_memory_space_constraint(r, pltpu.VMEM) for r in results]
    return pl.pallas_call(
        write_out,
        out_shape=tuple(jax.ShapeDtypeStruct(s, F32) for s in shapes),
        in_specs=[vmem] * 3,
        out_specs=(pl.BlockSpec(memory_space=pl.ANY),) * 3,
        scratch_shapes=[dma((3,))],
    )(*results)


def solution(mesh):
    n = mesh.shape["tm"]
    in_specs = (P(("seq", "tm"), None, None), P(("seq", "tm"), None), P(("seq", "tm"), None, None))
    out_specs = (P(("seq", "tm"), None), P(("seq", "tm"), None, None), P("seq", None))
    return jax.shard_map(
        local16 if n == 16 and mesh.shape["seq"] == 2 else functools.partial(local, n), mesh=mesh, in_specs=in_specs, out_specs=out_specs, check_vma=False
    )
```

```python
import functools

import jax
import jax.numpy as jnp
from jax import lax
from jax.experimental import pallas as pl
from jax.experimental.pallas import tpu as pltpu
from jax.sharding import PartitionSpec as P

F32 = jnp.float32
BF16 = jnp.bfloat16
PAD = 8
GROUP = 16


def split(x):
    hi = x.astype(BF16)
    return hi, (x - hi.astype(F32)).astype(BF16)


def left(x):
    hi, lo = split(x)
    return hi, jnp.concatenate([hi, lo], axis=1)


def right(w):
    hi, lo = split(w)
    return jnp.concatenate([hi, hi], axis=0), lo


def mul(x, w):
    hi, both = x
    w_hi, w_lo = w
    return jnp.dot(both, w_hi, preferred_element_type=F32) + jnp.dot(
        hi, w_lo, preferred_element_type=F32
    )


def kernel(
    n, gains, offsets, covs, means_out, covs_out, mom_out,
    own, ring, suf, z_snd, z_near, top_snd, top_rcv,
    mom, rs_buf, bf_snd, bf_rcv, red, mom_all, mean_rows,
    ring_s, ring_r, z_s, z_r, rs_s, rs_r, bf_s, bf_r, ag_s, ag_r, out_s,
):
    steps, width = gains.shape[0], gains.shape[1]
    lean = width + PAD
    me = lax.axis_index("tm")
    levels = (n.bit_length() - 1) // 2
    quarter = n // 4
    rows = width // GROUP
    place = lax.rem(me, GROUP)
    base = me - place

    def flip(step):
        return me + step * (1 - 2 * lax.rem(lax.div(me, step), 2))

    def digit_of(stride):
        return lax.rem(lax.div(me, stride), 4)

    def peer(stride, j):
        digit = digit_of(stride)
        return me + stride * (lax.rem(digit + j, 4) - digit)

    peers = [base + lax.rem(place + j, GROUP) for j in range(1, GROUP)]
    peers += [peer(4**l, j) for l in range(2, levels) for j in (1, 2, 3)]
    barrier = pltpu.get_barrier_semaphore()
    for to in peers:
        pl.semaphore_signal(barrier, inc=1, device_id={"tm": to}, device_id_type=pl.DeviceIdType.MESH)

    def send(src, dst, s, r, to):
        return pltpu.make_async_remote_copy(
            src_ref=src, dst_ref=dst, send_sem=s, recv_sem=r,
            device_id={"tm": to}, device_id_type=pl.DeviceIdType.MESH,
        )

    def compose(e, f):
        e_psi = e[lean:]
        x = mul(left(f), right(e_psi))
        p = e[:width] + mul(left(e_psi.T), right(x[:width]))
        out = [p, e[width:lean] + x[width:lean]]
        if f.shape[0] > lean:
            out.append(x[lean:])
        return jnp.concatenate(out, axis=0)

    for t in reversed(range(steps)):
        gain = gains[t]
        if t == steps - 1:
            gain = jnp.where(me == n - 1, jnp.zeros_like(gain), gain)
        offset = jnp.broadcast_to(offsets[t : t + 1, :], (PAD, width))
        element = jnp.concatenate([covs[t], offset, gain.T], axis=0)
        own[t] = element if t == steps - 1 else compose(element, own[t + 1])

    def absorb(f):
        for t in range(steps):
            own[t, : f.shape[0]] = compose(own[t], f)

    pl.semaphore_wait(barrier, len(peers))

    def deferred(l):
        digit = digit_of(4**l)

        @pl.when(digit == 0)
        def _():
            suf[...] = compose(ring[l, 1], suf[...])

        @pl.when(digit == 2)
        def _():
            suf[...] = ring[l, 3]

        @pl.when(digit < 3)
        def _():
            absorb(suf[...])

    sends = []
    total = own[0]
    for l in range(levels - 1):
        digit = digit_of(4**l)
        ring[l, digit] = total
        started = []
        for j in (2, 1, 3):
            c = send(
                ring.at[l, digit], ring.at[l, digit], ring_s.at[l, j - 1], ring_r.at[l, j - 1], peer(4**l, j)
            )
            c.start()
            started.append(c)
        if l:
            deferred(l - 1)
        for j in (1, 2, 3):
            came = lax.rem(digit + 4 - j, 4)
            send(
                ring.at[l, came], ring.at[l, came], ring_s.at[l, j - 1], ring_r.at[l, j - 1], peer(4**l, j)
            ).wait_recv()
        sends += started
        high = compose(ring[l, 2], ring[l, 3])
        total = compose(compose(ring[l, 0], ring[l, 1]), high)
        suf[...] = high
    z_snd[...] = total

    q = lax.div(me, quarter)
    down, down2 = lax.rem(me + n - quarter, n), lax.rem(me + n - 2 * quarter, n)
    part = pl.ds(0, lean)
    near_full = send(z_snd, z_near, z_s.at[0], z_r.at[0], down)
    near_lean = send(z_snd.at[part], z_near.at[part], z_s.at[0], z_r.at[0], down)
    top_far = send(top_snd, top_rcv, z_s.at[1], z_r.at[1], down2)
    top_near = send(top_snd, top_rcv, z_s.at[2], z_r.at[1], down)

    @pl.when(q == 3)
    def _():
        near_lean.start()

    @pl.when(q == 1)
    def _():
        near_full.start()

    deferred(levels - 2)

    @pl.when(q == 3)
    def _():
        near_lean.wait_send()

    @pl.when(q == 2)
    def _():
        near_lean.wait_recv()
        top_snd[...] = compose(z_snd[...], z_near[part, :])
        top_far.start()
        top_near.start()
        absorb(z_near[part, :])
        top_far.wait_send()
        top_near.wait_send()

    @pl.when(q == 0)
    def _():
        near_full.wait_recv()
        absorb(z_near[...])

    @pl.when(q < 2)
    def _():
        top_near.wait_recv()
        absorb(top_rcv[...])

    @pl.when(q == 1)
    def _():
        near_full.wait_send()

    out_copies = []
    for t in range(steps):
        out_copies.append(pltpu.make_async_copy(own.at[t, pl.ds(0, width)], covs_out.at[t], out_s.at[t]))
    means = jnp.concatenate([own[t, width : width + 1] for t in range(steps)], axis=0)
    mean_rows[...] = means
    out_copies.append(pltpu.make_async_copy(mean_rows, means_out, out_s.at[steps]))
    sums = own[0, :width]
    for t in range(1, steps):
        sums = sums + own[t, :width]
    m_hi, m_lo = split(means)
    outer = lambda u, v: lax.dot_general(u, v, (((0,), (0,)), ((), ())), preferred_element_type=F32)
    sums = sums + (outer(m_hi, m_hi) + (outer(m_hi, m_lo) + outer(m_lo, m_hi)))
    mom[...] = sums * (1.0 / (steps * n))

    def group_rows(k):
        return pl.ds(pl.multiple_of(k * rows, rows), rows)

    for j in range(1, GROUP):
        to = lax.rem(place + j, GROUP)
        c = send(mom.at[group_rows(to)], rs_buf.at[j - 1], rs_s.at[j - 1], rs_r.at[j - 1], base + to)
        c.start()
        sends.append(c)
    for c in out_copies:
        c.start()
    acc = mom[group_rows(place), :]
    for c, j in zip(sends[1 - GROUP :], range(1, GROUP)):
        c.wait_recv()
        acc = acc + rs_buf[j - 1]
    k = 0
    while GROUP << k < n:
        bf_snd[k] = acc
        c = send(bf_snd.at[k], bf_rcv.at[k], bf_s.at[k], bf_r.at[k], flip(GROUP << k))
        c.start()
        c.wait()
        acc = acc + bf_rcv[k]
        k += 1
    red[...] = acc
    gather = []
    for j in range(1, GROUP):
        to = lax.rem(place + j, GROUP)
        c = send(red, mom_all.at[group_rows(place)], ag_s.at[j - 1], ag_r.at[j - 1], base + to)
        c.start()
        gather.append(c)
    mom_all[group_rows(place), :] = acc
    for c in sends + gather:
        c.wait_send()
    for c in out_copies:
        c.wait()
    for c in gather:
        c.wait_recv()
    last = pltpu.make_async_copy(mom_all, mom_out, out_s.at[steps + 1])
    last.start()
    last.wait()


def hand_over(a, b, c, a_out, b_out, c_out, sems):
    copies = [
        pltpu.make_async_copy(x, y, sems.at[i])
        for i, (x, y) in enumerate(((b, b_out), (c, c_out), (a, a_out)))
    ]
    for copy in copies:
        copy.start()
    for copy in copies:
        copy.wait()


def local(n, gains, offsets, cov_terms):
    steps, width = gains.shape[0], gains.shape[1]
    levels = (n.bit_length() - 1) // 2
    assert n == 4**levels and levels > 1
    slab, lean, rows = 2 * width + PAD, width + PAD, width // GROUP
    far = max(1, (n // GROUP).bit_length() - 1)
    dma = pltpu.SemaphoreType.DMA
    vmem = pl.BlockSpec(memory_space=pltpu.VMEM)
    any_space = pl.BlockSpec(memory_space=pl.ANY)
    shapes = (
        jax.ShapeDtypeStruct((steps, width), F32),
        jax.ShapeDtypeStruct((steps, width, width), F32),
        jax.ShapeDtypeStruct((width, width), F32),
    )
    results = pl.pallas_call(
        functools.partial(kernel, n),
        out_shape=shapes,
        in_specs=[vmem] * 3,
        out_specs=(any_space,) * 3,
        scratch_shapes=[
            pltpu.VMEM((steps, slab, width), F32),
            pltpu.VMEM((levels - 1, 4, slab, width), F32),
            pltpu.VMEM((slab, width), F32),
            pltpu.VMEM((slab, width), F32),
            pltpu.VMEM((slab, width), F32),
            pltpu.VMEM((lean, width), F32),
            pltpu.VMEM((lean, width), F32),
            pltpu.VMEM((width, width), F32),
            pltpu.VMEM((GROUP - 1, rows, width), F32),
            pltpu.VMEM((far, rows, width), F32),
            pltpu.VMEM((far, rows, width), F32),
            pltpu.VMEM((rows, width), F32),
            pltpu.VMEM((width, width), F32),
            pltpu.VMEM((steps, width), F32),
            dma((levels - 1, 3)), dma((levels - 1, 3)),
            dma((3,)), dma((2,)),
            dma((GROUP - 1,)), dma((GROUP - 1,)),
            dma((far,)), dma((far,)),
            dma((GROUP - 1,)), dma((GROUP - 1,)),
            dma((steps + 2,)),
        ],
        compiler_params=pltpu.CompilerParams(collective_id=0, has_side_effects=True),
    )(gains, offsets, cov_terms)
    return pl.pallas_call(
        hand_over,
        out_shape=shapes,
        in_specs=[vmem] * 3,
        out_specs=(any_space,) * 3,
        scratch_shapes=[dma((3,))],
    )(*results)


def pack(s):
    half = s.shape[1] // 2
    row = lax.broadcasted_iota(jnp.int32, (half, 2 * half), 0)
    col = lax.broadcasted_iota(jnp.int32, (half, 2 * half), 1)
    low = s[half : 2 * half]
    both = jnp.where(jnp.logical_or(col >= half, row >= col), s[:half], pltpu.roll(low, half, 1))
    diag = jnp.sum(jnp.where(col - half == row, low, 0.0), axis=0, keepdims=True)
    first = lax.broadcasted_iota(jnp.int32, (PAD, 2 * half), 0) == 0
    return jnp.concatenate([both, jnp.where(first, s[2 * half :], diag)], axis=0)


def unpack(p):
    half = p.shape[1] // 2
    row = lax.broadcasted_iota(jnp.int32, (half, 2 * half), 0)
    col = lax.broadcasted_iota(jnp.int32, (half, 2 * half), 1)
    m = p[:half]
    turned = jnp.concatenate([m, m], axis=0).T
    top = jnp.where(jnp.logical_or(col >= half, row >= col), m, turned[:half])
    k = col - half
    right_low = jnp.where(row < k, pltpu.roll(m, half, 1), jnp.where(row == k, p[half + 1 : half + 2], turned[:half]))
    low = jnp.where(col < half, turned[half:], right_low)
    mean = jnp.broadcast_to(p[half : half + 1], (PAD, 2 * half))
    return jnp.concatenate([top, low, mean], axis=0)


def kernel16(
    gains_in, offsets_in, covs_in, means_out, covs_out, mom_out,
    gains, offsets, covs, own, ring, lower, suf, z_snd, z_near, sym_snd, sym_rcv, z_sym, z_sym_rcv, top_snd, top_rcv, mom, rs_buf, red,
    in_s, ring_s, ring_r, z_s, z_r, rs_s, rs_r, ag_s, ag_r, pace,
):
    steps, width = gains.shape[0], gains.shape[1]
    lean = width + PAD
    n = 16
    me, core = lax.axis_index("tm"), lax.axis_index("seq")
    digit, q = lax.rem(me, 4), lax.div(me, 4)
    rows = width // 4
    hosts = [4 + i for i in range(4)]
    is_host = jnp.logical_and(q == 1, core == 1)
    is_last = me == n - 1
    part, psi = pl.ds(0, lean), pl.ds(lean, width)
    packed = width // 2 + PAD
    dx, dy = 1 - 2 * lax.rem(digit, 2), 2 - 4 * lax.div(digit, 2)

    def at(tm, seq):
        return {"tm": tm, "seq": seq}

    def send(src, dst, s, r, to):
        return pltpu.make_async_remote_copy(
            src_ref=src, dst_ref=dst, send_sem=s, recv_sem=r,
            device_id=to, device_id_type=pl.DeviceIdType.MESH,
        )

    def landed(ref, sem):
        send(ref, ref, sem, sem, at(lax.rem(me + 1, n), core)).wait_recv()

    def sent(ref, sem):
        send(ref, ref, sem, sem, at(lax.rem(me + 1, n), core)).wait_send()

    barrier = pltpu.get_barrier_semaphore()

    def greet(tm, seq):
        pl.semaphore_signal(barrier, inc=1, device_id=at(tm, seq), device_id_type=pl.DeviceIdType.MESH)

    @pl.when(is_host)
    def _():
        for j in range(1, n):
            greet(lax.rem(me + j, n), core)
        for j in range(n):
            greet(j, 0)

    @pl.when(jnp.logical_not(is_host))
    def _():
        for j in (1, 2, 3):
            greet(me - digit + lax.rem(digit + j, 4), core)
        for host in hosts:
            greet(host, 1)

        @pl.when(core == 1)
        def _():
            for j in range(4):
                greet(me - digit + j, 0)

        @pl.when(q == 0)
        def _():
            greet(8 + digit, core)

        @pl.when(jnp.logical_or(q == 2, jnp.logical_and(q < 2, core == 0)))
        def _():
            greet(me + 4, core)

    fetch = [
        pltpu.make_async_copy(gains_in, gains, in_s.at[0]),
        pltpu.make_async_copy(covs_in, covs, in_s.at[1]),
        pltpu.make_async_copy(offsets_in, offsets, in_s.at[2]),
    ]
    for c in fetch:
        c.start()

    def compose(e, f):
        e_psi = e[lean:]
        x = mul(left(f), right(e_psi))
        p = e[:width] + mul(left(e_psi.T), right(x[:width]))
        out = [p, e[width:lean] + x[width:lean]]
        if f.shape[0] > lean:
            out.append(x[lean:])
        return jnp.concatenate(out, axis=0)

    def slot(d):
        return lax.rem(d + 4 - digit, 4)

    def total_of(d):
        return ring[slot(d)]

    def exchange(src, dst):
        for step in (dx + dy, dx, dy):
            there = lax.rem(4 - step, 4)
            send(src, dst(there), ring_s, ring_r.at[there], at(me + step, core)).start()

    def exchange_psi():
        exchange(ring.at[0, psi], lambda there: ring.at[there, psi])

    fetch[0].wait()
    ready = jnp.where(q == 0, 7, jnp.where(q == 2, 9 - core, 8)) + jnp.where(q == 1, 0, 4 - 4 * core)
    ready = jnp.where(is_host, 2 * n - 1, ready)

    @pl.when(is_last)
    def _():
        own[steps - 1, psi] = jnp.zeros((width, width), F32)
        for t in range(steps - 1):
            own[t, psi] = jnp.zeros((width, width), F32)
        ring[0, psi] = jnp.zeros((width, width), F32)

    @pl.when(jnp.logical_not(is_last))
    def _():
        run = gains[steps - 1].T
        own[steps - 1, psi] = run
        for t in reversed(range(steps - 1)):
            run = mul(left(run), right(gains[t].T))
            own[t, psi] = run
        ring[0, psi] = run

        @pl.when(q == 3)
        def _():
            ring[slot(3), psi] = jnp.zeros((width, width), F32)

    pl.semaphore_wait(barrier, ready)

    @pl.when(jnp.logical_and(jnp.logical_not(is_last), core == 0))
    def _():
        exchange_psi()

    fetch[1].wait()
    fetch[2].wait()

    def element(t):
        offset = jnp.broadcast_to(offsets[t : t + 1, :], (PAD, width))
        return jnp.concatenate([covs[t], offset, gains[t].T], axis=0)

    run = element(steps - 1)[:lean]
    own[steps - 1, part] = run
    for t in reversed(range(steps - 1)):
        run = compose(element(t), run)
        own[t, part] = run
    ring[0, part] = run
    sym_snd[...] = pack(run)

    @pl.when(core == 1)
    def _():
        pl.semaphore_wait(pace, 4)

        @pl.when(jnp.logical_not(is_last))
        def _():
            exchange_psi()

    exchange(sym_snd, lambda there: sym_rcv.at[there])

    @pl.when(core == 0)
    def _():
        for j in range(4):
            pl.semaphore_signal(pace, inc=1, device_id=at(me - digit + j, 1), device_id_type=pl.DeviceIdType.MESH)

    def absorb(f):
        for t in range(steps):
            own[t, : f.shape[0]] = compose(own[t], f)

    def arrive(d):
        here = slot(d)

        @pl.when(digit != d)
        def _():
            if d == 3:
                @pl.when(q == 3)
                def _():
                    landed(sym_rcv.at[here], ring_r.at[here])

                @pl.when(q != 3)
                def _():
                    landed(ring.at[here, pl.ds(0, packed + width)], ring_r.at[here])
            else:
                landed(ring.at[here, pl.ds(0, packed + width)], ring_r.at[here])
            ring[here, part] = unpack(sym_rcv[here])

    for d in (0, 1, 2):
        arrive(d)
    lower[...] = compose(compose(total_of(0), total_of(1)), total_of(2))
    arrive(3)

    down, down2 = lax.rem(me + n - 4, n), lax.rem(me + n - 8, n)
    near_sym = send(z_sym, z_sym_rcv, z_s, z_r.at[0], at(down, core))
    near_psi = send(z_snd.at[psi], z_near.at[psi], z_s, z_r.at[0], at(down, core))
    top_far = send(top_snd, top_rcv, z_s, z_r.at[1], at(down2, core))
    top_near = send(top_snd, top_rcv, z_s, z_r.at[1], at(down, core))

    @pl.when(q == 3)
    def _():
        z_sym[...] = pack(compose(lower[...], total_of(3)[:lean]))
        near_sym.start()

    @pl.when(q < 3)
    def _():
        total = compose(lower[...], total_of(3))
        z_snd[...] = total

        @pl.when(q == 1)
        def _():
            z_sym[...] = pack(total[:lean])
            near_sym.start()
            near_psi.start()

    suf[...] = total_of(3)

    @pl.when(digit < 2)
    def _():
        suf[...] = compose(total_of(2), suf[...])

    @pl.when(digit == 0)
    def _():
        suf[...] = compose(total_of(1), suf[...])

    @pl.when(digit < 3)
    def _():
        @pl.when(q == 3)
        def _():
            absorb(suf[part, :])

        @pl.when(q < 3)
        def _():
            absorb(suf[...])

    @pl.when(q == 2)
    def _():
        near_sym.wait_recv()
        near = unpack(z_sym_rcv[...])
        top_snd[...] = pack(compose(z_snd[...], near))
        top_far.start()
        top_near.start()
        absorb(near)

    @pl.when(q == 0)
    def _():
        landed(z_near.at[pl.ds(0, packed + width)], z_r.at[0])
        z_near[part, :] = unpack(z_sym_rcv[...])
        absorb(z_near[...])

    @pl.when(q < 2)
    def _():
        top_near.wait_recv()
        absorb(unpack(top_rcv[...]))

    means = jnp.concatenate([own[t, width : width + 1] for t in range(steps)], axis=0)
    sums = own[0, :width]
    for t in range(1, steps):
        sums = sums + own[t, :width]
    m_hi, m_lo = split(means)
    outer = lambda u, v: lax.dot_general(u, v, (((0,), (0,)), ((), ())), preferred_element_type=F32)
    sums = sums + (outer(m_hi, m_hi) + (outer(m_hi, m_lo) + outer(m_lo, m_hi)))
    mom[...] = sums * (1.0 / (steps * n))

    for i, host in enumerate(hosts):
        block = mom.at[pl.ds(i * rows, rows)]
        scatter = send(block, rs_buf.at[core, lax.rem(me + n - host, n)], rs_s, rs_r.at[core], at(host, 1))

        @pl.when(jnp.logical_or(me != host, core == 0))
        def _():
            scatter.start()

    means_out[...] = means
    for t in range(steps):
        covs_out[t] = own[t, :width]

    @pl.when(is_host)
    def _():
        mine = pl.ds(pl.multiple_of(digit * rows, rows), rows)
        for p in (0, 1):
            landed(rs_buf.at[p, pl.ds(p, n - p)], rs_r.at[p])
            acc = rs_buf[p, 1] if p == 0 else rs_buf[p, 1] + mom[mine, :]
            for j in (0, *range(2, n)) if p == 0 else range(2, n):
                acc = acc + rs_buf[p, j]
            red[p] = acc
            for to in range(n):
                gather = send(red.at[p], mom_out.at[mine], ag_s, ag_r, at(to, p))
                if p == 0:
                    gather.start()
                else:
                    pl.when(me != to)(gather.start)
            if p == 1:
                mom_out[mine, :] = acc
        landed(mom_out.at[pl.ds(0, 3 * rows)], ag_r)
        sent(rs_buf.at[0], ag_s)
        sent(rs_buf.at[1, pl.ds(1, n - 1)], ag_s)
        sent(mom.at[pl.ds(0, 3 * rows)], rs_s)

    @pl.when(jnp.logical_not(is_host))
    def _():
        landed(mom_out, ag_r)
        sent(mom, rs_s)

    sent(sym_rcv.at[pl.ds(1, 3)], ring_s)

    @pl.when(jnp.logical_not(is_last))
    def _():
        sent(ring.at[pl.ds(1, 3), psi], ring_s)

    @pl.when(q == 3)
    def _():
        near_sym.wait_send()

    @pl.when(q == 1)
    def _():
        near_sym.wait_send()
        near_psi.wait_send()

    @pl.when(q == 2)
    def _():
        top_far.wait_send()
        top_near.wait_send()


def write_out(a, b, c, a_out, b_out, c_out, sems):
    copies = [
        pltpu.make_async_copy(x, y, sems.at[i])
        for i, (x, y) in enumerate(((b, b_out), (c, c_out), (a, a_out)))
    ]
    for copy in copies:
        copy.start()
    for copy in copies:
        copy.wait()


def local16(gains, offsets, cov_terms):
    steps, width = gains.shape[0], gains.shape[1]
    slab, rows, packed = 2 * width + PAD, width // 4, width // 2 + PAD
    dma = pltpu.SemaphoreType.DMA
    vmem = pl.BlockSpec(memory_space=pltpu.VMEM)
    shapes = ((steps, width), (steps, width, width), (width, width))
    results = pl.pallas_call(
        kernel16,
        out_shape=tuple(pltpu.VMEM(s, F32) for s in shapes),
        in_specs=[pl.BlockSpec(memory_space=pltpu.HBM)] * 3,
        out_specs=(vmem,) * 3,
        scratch_shapes=[
            pltpu.VMEM((steps, width, width), F32),
            pltpu.VMEM((steps, width), F32),
            pltpu.VMEM((steps, width, width), F32),
            pltpu.VMEM((steps, slab, width), F32),
            pltpu.VMEM((4, slab, width), F32),
            pltpu.VMEM((slab, width), F32),
            pltpu.VMEM((slab, width), F32),
            pltpu.VMEM((slab, width), F32),
            pltpu.VMEM((slab, width), F32),
            pltpu.VMEM((packed, width), F32),
            pltpu.VMEM((4, packed, width), F32),
            pltpu.VMEM((packed, width), F32),
            pltpu.VMEM((packed, width), F32),
            pltpu.VMEM((packed, width), F32),
            pltpu.VMEM((packed, width), F32),
            pltpu.VMEM((width, width), F32),
            pltpu.VMEM((2, 16, rows, width), F32),
            pltpu.VMEM((2, rows, width), F32),
            dma((3,)), dma, dma((4,)), dma, dma((2,)), dma, dma((2,)), dma, dma, pltpu.SemaphoreType.REGULAR,
        ],
        compiler_params=pltpu.CompilerParams(collective_id=0, has_side_effects=True),
    )(gains, offsets, cov_terms)
    results = [pltpu.with_memory_space_constraint(r, pltpu.VMEM) for r in results]
    return pl.pallas_call(
        write_out,
        out_shape=tuple(jax.ShapeDtypeStruct(s, F32) for s in shapes),
        in_specs=[vmem] * 3,
        out_specs=(pl.BlockSpec(memory_space=pl.ANY),) * 3,
        scratch_shapes=[dma((3,))],
    )(*results)


def solution(mesh):
    n = mesh.shape["tm"]
    in_specs = (P(("seq", "tm"), None, None), P(("seq", "tm"), None), P(("seq", "tm"), None, None))
    out_specs = (P(("seq", "tm"), None), P(("seq", "tm"), None, None), P("seq", None))
    return jax.shard_map(
        local16 if n == 16 and mesh.shape["seq"] == 2 else functools.partial(local, n), mesh=mesh, in_specs=in_specs, out_specs=out_specs, check_vma=False
    )
```

```python
import functools

import jax
import jax.numpy as jnp
from jax import lax
from jax.experimental import pallas as pl
from jax.experimental.pallas import tpu as pltpu
from jax.sharding import PartitionSpec as P

F32 = jnp.float32
BF16 = jnp.bfloat16
PAD = 8
GROUP = 16


def split(x):
    hi = x.astype(BF16)
    return hi, (x - hi.astype(F32)).astype(BF16)


def left(x):
    hi, lo = split(x)
    return hi, jnp.concatenate([hi, lo], axis=1)


def right(w):
    hi, lo = split(w)
    return jnp.concatenate([hi, hi], axis=0), lo


def mul(x, w):
    hi, both = x
    w_hi, w_lo = w
    return jnp.dot(both, w_hi, preferred_element_type=F32) + jnp.dot(
        hi, w_lo, preferred_element_type=F32
    )


def kernel(
    n, gains, offsets, covs, means_out, covs_out, mom_out,
    own, ring, suf, z_snd, z_near, top_snd, top_rcv,
    mom, rs_buf, bf_snd, bf_rcv, red, mom_all, mean_rows,
    ring_s, ring_r, z_s, z_r, rs_s, rs_r, bf_s, bf_r, ag_s, ag_r, out_s,
):
    steps, width = gains.shape[0], gains.shape[1]
    lean = width + PAD
    me = lax.axis_index("tm")
    levels = (n.bit_length() - 1) // 2
    quarter = n // 4
    rows = width // GROUP
    place = lax.rem(me, GROUP)
    base = me - place

    def flip(step):
        return me + step * (1 - 2 * lax.rem(lax.div(me, step), 2))

    def digit_of(stride):
        return lax.rem(lax.div(me, stride), 4)

    def peer(stride, j):
        digit = digit_of(stride)
        return me + stride * (lax.rem(digit + j, 4) - digit)

    peers = [base + lax.rem(place + j, GROUP) for j in range(1, GROUP)]
    peers += [peer(4**l, j) for l in range(2, levels) for j in (1, 2, 3)]
    barrier = pltpu.get_barrier_semaphore()
    for to in peers:
        pl.semaphore_signal(barrier, inc=1, device_id={"tm": to}, device_id_type=pl.DeviceIdType.MESH)

    def send(src, dst, s, r, to):
        return pltpu.make_async_remote_copy(
            src_ref=src, dst_ref=dst, send_sem=s, recv_sem=r,
            device_id={"tm": to}, device_id_type=pl.DeviceIdType.MESH,
        )

    def compose(e, f):
        e_psi = e[lean:]
        x = mul(left(f), right(e_psi))
        p = e[:width] + mul(left(e_psi.T), right(x[:width]))
        out = [p, e[width:lean] + x[width:lean]]
        if f.shape[0] > lean:
            out.append(x[lean:])
        return jnp.concatenate(out, axis=0)

    for t in reversed(range(steps)):
        gain = gains[t]
        if t == steps - 1:
            gain = jnp.where(me == n - 1, jnp.zeros_like(gain), gain)
        offset = jnp.broadcast_to(offsets[t : t + 1, :], (PAD, width))
        element = jnp.concatenate([covs[t], offset, gain.T], axis=0)
        own[t] = element if t == steps - 1 else compose(element, own[t + 1])

    def absorb(f):
        for t in range(steps):
            own[t, : f.shape[0]] = compose(own[t], f)

    pl.semaphore_wait(barrier, len(peers))

    def deferred(l):
        digit = digit_of(4**l)

        @pl.when(digit == 0)
        def _():
            suf[...] = compose(ring[l, 1], suf[...])

        @pl.when(digit == 2)
        def _():
            suf[...] = ring[l, 3]

        @pl.when(digit < 3)
        def _():
            absorb(suf[...])

    sends = []
    total = own[0]
    for l in range(levels - 1):
        digit = digit_of(4**l)
        ring[l, digit] = total
        started = []
        for j in (2, 1, 3):
            c = send(
                ring.at[l, digit], ring.at[l, digit], ring_s.at[l, j - 1], ring_r.at[l, j - 1], peer(4**l, j)
            )
            c.start()
            started.append(c)
        if l:
            deferred(l - 1)
        for j in (1, 2, 3):
            came = lax.rem(digit + 4 - j, 4)
            send(
                ring.at[l, came], ring.at[l, came], ring_s.at[l, j - 1], ring_r.at[l, j - 1], peer(4**l, j)
            ).wait_recv()
        sends += started
        high = compose(ring[l, 2], ring[l, 3])
        total = compose(compose(ring[l, 0], ring[l, 1]), high)
        suf[...] = high
    z_snd[...] = total

    q = lax.div(me, quarter)
    down, down2 = lax.rem(me + n - quarter, n), lax.rem(me + n - 2 * quarter, n)
    part = pl.ds(0, lean)
    near_full = send(z_snd, z_near, z_s.at[0], z_r.at[0], down)
    near_lean = send(z_snd.at[part], z_near.at[part], z_s.at[0], z_r.at[0], down)
    top_far = send(top_snd, top_rcv, z_s.at[1], z_r.at[1], down2)
    top_near = send(top_snd, top_rcv, z_s.at[2], z_r.at[1], down)

    @pl.when(q == 3)
    def _():
        near_lean.start()

    @pl.when(q == 1)
    def _():
        near_full.start()

    deferred(levels - 2)

    @pl.when(q == 3)
    def _():
        near_lean.wait_send()

    @pl.when(q == 2)
    def _():
        near_lean.wait_recv()
        top_snd[...] = compose(z_snd[...], z_near[part, :])
        top_far.start()
        top_near.start()
        absorb(z_near[part, :])
        top_far.wait_send()
        top_near.wait_send()

    @pl.when(q == 0)
    def _():
        near_full.wait_recv()
        absorb(z_near[...])

    @pl.when(q < 2)
    def _():
        top_near.wait_recv()
        absorb(top_rcv[...])

    @pl.when(q == 1)
    def _():
        near_full.wait_send()

    out_copies = []
    for t in range(steps):
        out_copies.append(pltpu.make_async_copy(own.at[t, pl.ds(0, width)], covs_out.at[t], out_s.at[t]))
    means = jnp.concatenate([own[t, width : width + 1] for t in range(steps)], axis=0)
    mean_rows[...] = means
    out_copies.append(pltpu.make_async_copy(mean_rows, means_out, out_s.at[steps]))
    sums = own[0, :width]
    for t in range(1, steps):
        sums = sums + own[t, :width]
    m_hi, m_lo = split(means)
    outer = lambda u, v: lax.dot_general(u, v, (((0,), (0,)), ((), ())), preferred_element_type=F32)
    sums = sums + (outer(m_hi, m_hi) + (outer(m_hi, m_lo) + outer(m_lo, m_hi)))
    mom[...] = sums * (1.0 / (steps * n))

    def group_rows(k):
        return pl.ds(pl.multiple_of(k * rows, rows), rows)

    for j in range(1, GROUP):
        to = lax.rem(place + j, GROUP)
        c = send(mom.at[group_rows(to)], rs_buf.at[j - 1], rs_s.at[j - 1], rs_r.at[j - 1], base + to)
        c.start()
        sends.append(c)
    for c in out_copies:
        c.start()
    acc = mom[group_rows(place), :]
    for c, j in zip(sends[1 - GROUP :], range(1, GROUP)):
        c.wait_recv()
        acc = acc + rs_buf[j - 1]
    k = 0
    while GROUP << k < n:
        bf_snd[k] = acc
        c = send(bf_snd.at[k], bf_rcv.at[k], bf_s.at[k], bf_r.at[k], flip(GROUP << k))
        c.start()
        c.wait()
        acc = acc + bf_rcv[k]
        k += 1
    red[...] = acc
    gather = []
    for j in range(1, GROUP):
        to = lax.rem(place + j, GROUP)
        c = send(red, mom_all.at[group_rows(place)], ag_s.at[j - 1], ag_r.at[j - 1], base + to)
        c.start()
        gather.append(c)
    mom_all[group_rows(place), :] = acc
    for c in sends + gather:
        c.wait_send()
    for c in out_copies:
        c.wait()
    for c in gather:
        c.wait_recv()
    last = pltpu.make_async_copy(mom_all, mom_out, out_s.at[steps + 1])
    last.start()
    last.wait()


def hand_over(a, b, c, a_out, b_out, c_out, sems):
    copies = [
        pltpu.make_async_copy(x, y, sems.at[i])
        for i, (x, y) in enumerate(((b, b_out), (c, c_out), (a, a_out)))
    ]
    for copy in copies:
        copy.start()
    for copy in copies:
        copy.wait()


def local(n, gains, offsets, cov_terms):
    steps, width = gains.shape[0], gains.shape[1]
    levels = (n.bit_length() - 1) // 2
    assert n == 4**levels and levels > 1
    slab, lean, rows = 2 * width + PAD, width + PAD, width // GROUP
    far = max(1, (n // GROUP).bit_length() - 1)
    dma = pltpu.SemaphoreType.DMA
    vmem = pl.BlockSpec(memory_space=pltpu.VMEM)
    any_space = pl.BlockSpec(memory_space=pl.ANY)
    shapes = (
        jax.ShapeDtypeStruct((steps, width), F32),
        jax.ShapeDtypeStruct((steps, width, width), F32),
        jax.ShapeDtypeStruct((width, width), F32),
    )
    results = pl.pallas_call(
        functools.partial(kernel, n),
        out_shape=shapes,
        in_specs=[vmem] * 3,
        out_specs=(any_space,) * 3,
        scratch_shapes=[
            pltpu.VMEM((steps, slab, width), F32),
            pltpu.VMEM((levels - 1, 4, slab, width), F32),
            pltpu.VMEM((slab, width), F32),
            pltpu.VMEM((slab, width), F32),
            pltpu.VMEM((slab, width), F32),
            pltpu.VMEM((lean, width), F32),
            pltpu.VMEM((lean, width), F32),
            pltpu.VMEM((width, width), F32),
            pltpu.VMEM((GROUP - 1, rows, width), F32),
            pltpu.VMEM((far, rows, width), F32),
            pltpu.VMEM((far, rows, width), F32),
            pltpu.VMEM((rows, width), F32),
            pltpu.VMEM((width, width), F32),
            pltpu.VMEM((steps, width), F32),
            dma((levels - 1, 3)), dma((levels - 1, 3)),
            dma((3,)), dma((2,)),
            dma((GROUP - 1,)), dma((GROUP - 1,)),
            dma((far,)), dma((far,)),
            dma((GROUP - 1,)), dma((GROUP - 1,)),
            dma((steps + 2,)),
        ],
        compiler_params=pltpu.CompilerParams(collective_id=0, has_side_effects=True),
    )(gains, offsets, cov_terms)
    return pl.pallas_call(
        hand_over,
        out_shape=shapes,
        in_specs=[vmem] * 3,
        out_specs=(any_space,) * 3,
        scratch_shapes=[dma((3,))],
    )(*results)


def pack(s):
    half = s.shape[1] // 2
    row = lax.broadcasted_iota(jnp.int32, (half, 2 * half), 0)
    col = lax.broadcasted_iota(jnp.int32, (half, 2 * half), 1)
    low = s[half : 2 * half]
    both = jnp.where(jnp.logical_or(col >= half, row >= col), s[:half], pltpu.roll(low, half, 1))
    diag = jnp.sum(jnp.where(col - half == row, low, 0.0), axis=0, keepdims=True)
    first = lax.broadcasted_iota(jnp.int32, (PAD, 2 * half), 0) == 0
    return jnp.concatenate([both, jnp.where(first, s[2 * half :], diag)], axis=0)


def unpack(p):
    half = p.shape[1] // 2
    row = lax.broadcasted_iota(jnp.int32, (half, 2 * half), 0)
    col = lax.broadcasted_iota(jnp.int32, (half, 2 * half), 1)
    m = p[:half]
    turned = jnp.concatenate([m, m], axis=0).T
    top = jnp.where(jnp.logical_or(col >= half, row >= col), m, turned[:half])
    k = col - half
    right_low = jnp.where(row < k, pltpu.roll(m, half, 1), jnp.where(row == k, p[half + 1 : half + 2], turned[:half]))
    low = jnp.where(col < half, turned[half:], right_low)
    mean = jnp.broadcast_to(p[half : half + 1], (PAD, 2 * half))
    return jnp.concatenate([top, low, mean], axis=0)


def kernel16(
    gains_in, offsets_in, covs_in, means_out, covs_out, mom_out,
    gains, offsets, covs, own, ring, acc, suf, z_near, sym_snd, sym_rcv, z_sym, z_sym_rcv, top_snd, top_rcv, mom, rs_buf, red,
    own_right, own_low, own_both, z_right, z_low, z_both,
    in_s, ring_s, ring_r, z_s, z_r, rs_s, rs_r, ag_s, ag_r, pace,
):
    steps, width = gains.shape[0], gains.shape[1]
    lean = width + PAD
    n = 16
    me, core = lax.axis_index("tm"), lax.axis_index("seq")
    digit, q = lax.rem(me, 4), lax.div(me, 4)
    rows = width // 4
    hosts = [4 + i for i in range(4)]
    is_host = jnp.logical_and(q == 1, core == 1)
    is_last = me == n - 1
    part, psi = pl.ds(0, lean), pl.ds(lean, width)
    packed = width // 2 + PAD
    dx, dy = 1 - 2 * lax.rem(digit, 2), 2 - 4 * lax.div(digit, 2)

    def at(tm, seq):
        return {"tm": tm, "seq": seq}

    def send(src, dst, s, r, to):
        return pltpu.make_async_remote_copy(
            src_ref=src, dst_ref=dst, send_sem=s, recv_sem=r,
            device_id=to, device_id_type=pl.DeviceIdType.MESH,
        )

    def landed(ref, sem):
        send(ref, ref, sem, sem, at(lax.rem(me + 1, n), core)).wait_recv()

    def sent(ref, sem):
        send(ref, ref, sem, sem, at(lax.rem(me + 1, n), core)).wait_send()

    barrier = pltpu.get_barrier_semaphore()

    def greet(tm, seq):
        pl.semaphore_signal(barrier, inc=1, device_id=at(tm, seq), device_id_type=pl.DeviceIdType.MESH)

    @pl.when(is_host)
    def _():
        for j in range(1, n):
            greet(lax.rem(me + j, n), core)
        for j in range(n):
            greet(j, 0)

    @pl.when(jnp.logical_not(is_host))
    def _():
        for j in (1, 2, 3):
            greet(me - digit + lax.rem(digit + j, 4), core)
        for host in hosts:
            greet(host, 1)

        @pl.when(core == 1)
        def _():
            for j in range(4):
                greet(me - digit + j, 0)

        @pl.when(q == 0)
        def _():
            greet(8 + digit, core)

        @pl.when(jnp.logical_or(q == 2, jnp.logical_and(q < 2, core == 0)))
        def _():
            greet(me + 4, core)

    fetch = [
        pltpu.make_async_copy(gains_in, gains, in_s.at[0]),
        pltpu.make_async_copy(covs_in, covs, in_s.at[1]),
        pltpu.make_async_copy(offsets_in, offsets, in_s.at[2]),
    ]
    for c in fetch:
        c.start()

    def compose(e, f):
        e_psi = e[lean:]
        x = mul(left(f), right(e_psi))
        p = e[:width] + mul(left(e_psi.T), right(x[:width]))
        out = [p, e[width:lean] + x[width:lean]]
        if f.shape[0] > lean:
            out.append(x[lean:])
        return jnp.concatenate(out, axis=0)

    def slot(d):
        return lax.rem(d + 4 - digit, 4)

    def total_of(d):
        return ring[slot(d)]

    def exchange(src, dst):
        for step in (dx + dy, dx, dy):
            there = lax.rem(4 - step, 4)
            send(src, dst(there), ring_s, ring_r.at[there], at(me + step, core)).start()

    def exchange_psi():
        exchange(ring.at[0, psi], lambda there: ring.at[there, psi])

    fetch[0].wait()
    ready = jnp.where(q == 0, 7, jnp.where(q == 2, 9 - core, 8)) + jnp.where(q == 1, 0, 4 - 4 * core)
    ready = jnp.where(is_host, 2 * n - 1, ready)

    @pl.when(is_last)
    def _():
        own[steps - 1, psi] = jnp.zeros((width, width), F32)
        for t in range(steps - 1):
            own[t, psi] = jnp.zeros((width, width), F32)
        ring[0, psi] = jnp.zeros((width, width), F32)

    @pl.when(jnp.logical_not(is_last))
    def _():
        run = gains[steps - 1].T
        own[steps - 1, psi] = run
        for t in reversed(range(steps - 1)):
            run = mul(left(run), right(gains[t].T))
            own[t, psi] = run
        ring[0, psi] = run

        @pl.when(q == 3)
        def _():
            ring[slot(3), psi] = jnp.zeros((width, width), F32)

    pl.semaphore_wait(barrier, ready)

    @pl.when(jnp.logical_and(jnp.logical_not(is_last), core == 0))
    def _():
        exchange_psi()

    fetch[1].wait()
    fetch[2].wait()

    def element(t):
        offset = jnp.broadcast_to(offsets[t : t + 1, :], (PAD, width))
        return jnp.concatenate([covs[t], offset, gains[t].T], axis=0)

    run = element(steps - 1)[:lean]
    own[steps - 1, part] = run
    for t in reversed(range(steps - 1)):
        run = compose(element(t), run)
        own[t, part] = run
    ring[0, part] = run
    sym_snd[...] = pack(run)

    @pl.when(core == 1)
    def _():
        pl.semaphore_wait(pace, 4)

        @pl.when(jnp.logical_not(is_last))
        def _():
            exchange_psi()

    exchange(sym_snd, lambda there: sym_rcv.at[there])

    @pl.when(core == 0)
    def _():
        for j in range(4):
            pl.semaphore_signal(pace, inc=1, device_id=at(me - digit + j, 1), device_id_type=pl.DeviceIdType.MESH)

    def prepare():
        for t in range(steps):
            e, cols = own[t, psi], pl.ds(t * width, width)
            own_right[:, cols], own_low[:, cols] = right(e)
            own_both[t] = left(e.T)[1]

    def absorb(f):
        x = mul(left(f), (own_right[...], own_low[...]))
        for t in range(steps):
            both, xt = own_both[t], x[:, t * width : (t + 1) * width]
            own[t, :width] = own[t, :width] + mul((both[:, :width], both), right(xt[:width]))
            own[t, width:lean] = own[t, width:lean] + xt[width:lean]
            if f.shape[0] > lean:
                own[t, psi] = xt[lean:]

    def arrive(d):
        here = slot(d)

        @pl.when(digit != d)
        def _():
            if d == 3:
                @pl.when(q == 3)
                def _():
                    landed(sym_rcv.at[here], ring_r.at[here])

                @pl.when(q != 3)
                def _():
                    landed(ring.at[here, pl.ds(0, packed + width)], ring_r.at[here])
            else:
                landed(ring.at[here, pl.ds(0, packed + width)], ring_r.at[here])
            ring[here, part] = unpack(sym_rcv[here])

    down, down2 = lax.rem(me + n - 4, n), lax.rem(me + n - 8, n)
    near_sym = send(z_sym, z_sym_rcv, z_s, z_r.at[0], at(down, core))
    near_psi = send(acc.at[psi], z_near.at[psi], z_s, z_r.at[0], at(down, core))
    top_far = send(top_snd, top_rcv, z_s, z_r.at[1], at(down2, core))
    top_near = send(top_snd, top_rcv, z_s, z_r.at[1], at(down, core))

    arrive(3)
    acc[...] = total_of(3)
    for d in (2, 1, 0):
        @pl.when(digit == d)
        def _():
            suf[...] = acc[...]

        arrive(d)

        @pl.when(q == 3)
        def _():
            state = compose(total_of(d), acc[part, :])
            if d:
                acc[part, :] = state
            else:
                z_sym[...] = pack(state)
                near_sym.start()

        @pl.when(q < 3)
        def _():
            acc[...] = compose(total_of(d), acc[...])

    @pl.when(q == 1)
    def _():
        z_sym[...] = pack(acc[part, :])
        near_sym.start()
        near_psi.start()

    @pl.when(q == 2)
    def _():
        z_right[...], z_low[...] = right(acc[psi, :])
        z_both[...] = left(acc[psi, :].T)[1]

    prepare()

    @pl.when(digit < 3)
    def _():
        @pl.when(q == 3)
        def _():
            absorb(suf[part, :])

        @pl.when(q < 3)
        def _():
            absorb(suf[...])
            prepare()

    @pl.when(q == 2)
    def _():
        near_sym.wait_recv()
        near = unpack(z_sym_rcv[...])
        x = mul(left(near), (z_right[...], z_low[...]))
        both = z_both[...]
        cov = acc[:width, :] + mul((both[:, :width], both), right(x[:width]))
        top_snd[...] = pack(jnp.concatenate([cov, acc[width:lean, :] + x[width:]], axis=0))
        top_far.start()
        top_near.start()
        absorb(near)

    @pl.when(q == 0)
    def _():
        landed(z_near.at[pl.ds(0, packed + width)], z_r.at[0])
        z_near[part, :] = unpack(z_sym_rcv[...])
        absorb(z_near[...])
        prepare()

    @pl.when(q < 2)
    def _():
        top_near.wait_recv()
        absorb(unpack(top_rcv[...]))

    means = jnp.concatenate([own[t, width : width + 1] for t in range(steps)], axis=0)
    sums = own[0, :width]
    for t in range(1, steps):
        sums = sums + own[t, :width]
    m_hi, m_lo = split(means)
    outer = lambda u, v: lax.dot_general(u, v, (((0,), (0,)), ((), ())), preferred_element_type=F32)
    sums = sums + (outer(m_hi, m_hi) + (outer(m_hi, m_lo) + outer(m_lo, m_hi)))
    mom[...] = sums * (1.0 / (steps * n))

    for i, host in enumerate(hosts):
        block = mom.at[pl.ds(i * rows, rows)]
        scatter = send(block, rs_buf.at[core, lax.rem(me + n - host, n)], rs_s, rs_r.at[core], at(host, 1))

        @pl.when(jnp.logical_or(me != host, core == 0))
        def _():
            scatter.start()

    means_out[...] = means
    for t in range(steps):
        covs_out[t] = own[t, :width]

    @pl.when(is_host)
    def _():
        mine = pl.ds(pl.multiple_of(digit * rows, rows), rows)
        for p in (0, 1):
            landed(rs_buf.at[p, pl.ds(p, n - p)], rs_r.at[p])
            acc = rs_buf[p, 1] if p == 0 else rs_buf[p, 1] + mom[mine, :]
            for j in (0, *range(2, n)) if p == 0 else range(2, n):
                acc = acc + rs_buf[p, j]
            red[p] = acc
            for to in range(n):
                gather = send(red.at[p], mom_out.at[mine], ag_s, ag_r, at(to, p))
                if p == 0:
                    gather.start()
                else:
                    pl.when(me != to)(gather.start)
            if p == 1:
                mom_out[mine, :] = acc
        landed(mom_out.at[pl.ds(0, 3 * rows)], ag_r)
        sent(rs_buf.at[0], ag_s)
        sent(rs_buf.at[1, pl.ds(1, n - 1)], ag_s)
        sent(mom.at[pl.ds(0, 3 * rows)], rs_s)

    @pl.when(jnp.logical_not(is_host))
    def _():
        landed(mom_out, ag_r)
        sent(mom, rs_s)

    sent(sym_rcv.at[pl.ds(1, 3)], ring_s)

    @pl.when(jnp.logical_not(is_last))
    def _():
        sent(ring.at[pl.ds(1, 3), psi], ring_s)

    @pl.when(q == 3)
    def _():
        near_sym.wait_send()

    @pl.when(q == 1)
    def _():
        near_sym.wait_send()
        near_psi.wait_send()

    @pl.when(q == 2)
    def _():
        top_far.wait_send()
        top_near.wait_send()


def write_out(a, b, c, a_out, b_out, c_out, sems):
    copies = [
        pltpu.make_async_copy(x, y, sems.at[i])
        for i, (x, y) in enumerate(((b, b_out), (c, c_out), (a, a_out)))
    ]
    for copy in copies:
        copy.start()
    for copy in copies:
        copy.wait()


def local16(gains, offsets, cov_terms):
    steps, width = gains.shape[0], gains.shape[1]
    slab, rows, packed = 2 * width + PAD, width // 4, width // 2 + PAD
    dma = pltpu.SemaphoreType.DMA
    vmem = pl.BlockSpec(memory_space=pltpu.VMEM)
    shapes = ((steps, width), (steps, width, width), (width, width))
    results = pl.pallas_call(
        kernel16,
        out_shape=tuple(pltpu.VMEM(s, F32) for s in shapes),
        in_specs=[pl.BlockSpec(memory_space=pltpu.HBM)] * 3,
        out_specs=(vmem,) * 3,
        scratch_shapes=[
            pltpu.VMEM((steps, width, width), F32),
            pltpu.VMEM((steps, width), F32),
            pltpu.VMEM((steps, width, width), F32),
            pltpu.VMEM((steps, slab, width), F32),
            pltpu.VMEM((4, slab, width), F32),
            pltpu.VMEM((slab, width), F32),
            pltpu.VMEM((slab, width), F32),
            pltpu.VMEM((slab, width), F32),
            pltpu.VMEM((packed, width), F32),
            pltpu.VMEM((4, packed, width), F32),
            pltpu.VMEM((packed, width), F32),
            pltpu.VMEM((packed, width), F32),
            pltpu.VMEM((packed, width), F32),
            pltpu.VMEM((packed, width), F32),
            pltpu.VMEM((width, width), F32),
            pltpu.VMEM((2, 16, rows, width), F32),
            pltpu.VMEM((2, rows, width), F32),
            pltpu.VMEM((2 * width, steps * width), BF16),
            pltpu.VMEM((width, steps * width), BF16),
            pltpu.VMEM((steps, width, 2 * width), BF16),
            pltpu.VMEM((2 * width, width), BF16),
            pltpu.VMEM((width, width), BF16),
            pltpu.VMEM((width, 2 * width), BF16),
            dma((3,)), dma, dma((4,)), dma, dma((2,)), dma, dma((2,)), dma, dma, pltpu.SemaphoreType.REGULAR,
        ],
        compiler_params=pltpu.CompilerParams(collective_id=0, has_side_effects=True),
    )(gains, offsets, cov_terms)
    results = [pltpu.with_memory_space_constraint(r, pltpu.VMEM) for r in results]
    return pl.pallas_call(
        write_out,
        out_shape=tuple(jax.ShapeDtypeStruct(s, F32) for s in shapes),
        in_specs=[vmem] * 3,
        out_specs=(pl.BlockSpec(memory_space=pl.ANY),) * 3,
        scratch_shapes=[dma((3,))],
    )(*results)


def solution(mesh):
    n = mesh.shape["tm"]
    in_specs = (P(("seq", "tm"), None, None), P(("seq", "tm"), None), P(("seq", "tm"), None, None))
    out_specs = (P(("seq", "tm"), None), P(("seq", "tm"), None, None), P("seq", None))
    return jax.shard_map(
        local16 if n == 16 and mesh.shape["seq"] == 2 else functools.partial(local, n), mesh=mesh, in_specs=in_specs, out_specs=out_specs, check_vma=False
    )
```

```python
import functools

import jax
import jax.numpy as jnp
from jax import lax
from jax.experimental import pallas as pl
from jax.experimental.pallas import tpu as pltpu
from jax.sharding import PartitionSpec as P

F32 = jnp.float32
BF16 = jnp.bfloat16
PAD = 8
GROUP = 16


def split(x):
    hi = x.astype(BF16)
    return hi, (x - hi.astype(F32)).astype(BF16)


def left(x):
    hi, lo = split(x)
    return hi, jnp.concatenate([hi, lo], axis=1)


def right(w):
    hi, lo = split(w)
    return jnp.concatenate([hi, hi], axis=0), lo


def mul(x, w):
    hi, both = x
    w_hi, w_lo = w
    return jnp.dot(both, w_hi, preferred_element_type=F32) + jnp.dot(
        hi, w_lo, preferred_element_type=F32
    )


def kernel(
    n, gains, offsets, covs, means_out, covs_out, mom_out,
    own, ring, suf, z_snd, z_near, top_snd, top_rcv,
    mom, rs_buf, bf_snd, bf_rcv, red, mom_all, mean_rows,
    ring_s, ring_r, z_s, z_r, rs_s, rs_r, bf_s, bf_r, ag_s, ag_r, out_s,
):
    steps, width = gains.shape[0], gains.shape[1]
    lean = width + PAD
    me = lax.axis_index("tm")
    levels = (n.bit_length() - 1) // 2
    quarter = n // 4
    rows = width // GROUP
    place = lax.rem(me, GROUP)
    base = me - place

    def flip(step):
        return me + step * (1 - 2 * lax.rem(lax.div(me, step), 2))

    def digit_of(stride):
        return lax.rem(lax.div(me, stride), 4)

    def peer(stride, j):
        digit = digit_of(stride)
        return me + stride * (lax.rem(digit + j, 4) - digit)

    peers = [base + lax.rem(place + j, GROUP) for j in range(1, GROUP)]
    peers += [peer(4**l, j) for l in range(2, levels) for j in (1, 2, 3)]
    barrier = pltpu.get_barrier_semaphore()
    for to in peers:
        pl.semaphore_signal(barrier, inc=1, device_id={"tm": to}, device_id_type=pl.DeviceIdType.MESH)

    def send(src, dst, s, r, to):
        return pltpu.make_async_remote_copy(
            src_ref=src, dst_ref=dst, send_sem=s, recv_sem=r,
            device_id={"tm": to}, device_id_type=pl.DeviceIdType.MESH,
        )

    def compose(e, f):
        e_psi = e[lean:]
        x = mul(left(f), right(e_psi))
        p = e[:width] + mul(left(e_psi.T), right(x[:width]))
        out = [p, e[width:lean] + x[width:lean]]
        if f.shape[0] > lean:
            out.append(x[lean:])
        return jnp.concatenate(out, axis=0)

    for t in reversed(range(steps)):
        gain = gains[t]
        if t == steps - 1:
            gain = jnp.where(me == n - 1, jnp.zeros_like(gain), gain)
        offset = jnp.broadcast_to(offsets[t : t + 1, :], (PAD, width))
        element = jnp.concatenate([covs[t], offset, gain.T], axis=0)
        own[t] = element if t == steps - 1 else compose(element, own[t + 1])

    def absorb(f):
        for t in range(steps):
            own[t, : f.shape[0]] = compose(own[t], f)

    pl.semaphore_wait(barrier, len(peers))

    def deferred(l):
        digit = digit_of(4**l)

        @pl.when(digit == 0)
        def _():
            suf[...] = compose(ring[l, 1], suf[...])

        @pl.when(digit == 2)
        def _():
            suf[...] = ring[l, 3]

        @pl.when(digit < 3)
        def _():
            absorb(suf[...])

    sends = []
    total = own[0]
    for l in range(levels - 1):
        digit = digit_of(4**l)
        ring[l, digit] = total
        started = []
        for j in (2, 1, 3):
            c = send(
                ring.at[l, digit], ring.at[l, digit], ring_s.at[l, j - 1], ring_r.at[l, j - 1], peer(4**l, j)
            )
            c.start()
            started.append(c)
        if l:
            deferred(l - 1)
        for j in (1, 2, 3):
            came = lax.rem(digit + 4 - j, 4)
            send(
                ring.at[l, came], ring.at[l, came], ring_s.at[l, j - 1], ring_r.at[l, j - 1], peer(4**l, j)
            ).wait_recv()
        sends += started
        high = compose(ring[l, 2], ring[l, 3])
        total = compose(compose(ring[l, 0], ring[l, 1]), high)
        suf[...] = high
    z_snd[...] = total

    q = lax.div(me, quarter)
    down, down2 = lax.rem(me + n - quarter, n), lax.rem(me + n - 2 * quarter, n)
    part = pl.ds(0, lean)
    near_full = send(z_snd, z_near, z_s.at[0], z_r.at[0], down)
    near_lean = send(z_snd.at[part], z_near.at[part], z_s.at[0], z_r.at[0], down)
    top_far = send(top_snd, top_rcv, z_s.at[1], z_r.at[1], down2)
    top_near = send(top_snd, top_rcv, z_s.at[2], z_r.at[1], down)

    @pl.when(q == 3)
    def _():
        near_lean.start()

    @pl.when(q == 1)
    def _():
        near_full.start()

    deferred(levels - 2)

    @pl.when(q == 3)
    def _():
        near_lean.wait_send()

    @pl.when(q == 2)
    def _():
        near_lean.wait_recv()
        top_snd[...] = compose(z_snd[...], z_near[part, :])
        top_far.start()
        top_near.start()
        absorb(z_near[part, :])
        top_far.wait_send()
        top_near.wait_send()

    @pl.when(q == 0)
    def _():
        near_full.wait_recv()
        absorb(z_near[...])

    @pl.when(q < 2)
    def _():
        top_near.wait_recv()
        absorb(top_rcv[...])

    @pl.when(q == 1)
    def _():
        near_full.wait_send()

    out_copies = []
    for t in range(steps):
        out_copies.append(pltpu.make_async_copy(own.at[t, pl.ds(0, width)], covs_out.at[t], out_s.at[t]))
    means = jnp.concatenate([own[t, width : width + 1] for t in range(steps)], axis=0)
    mean_rows[...] = means
    out_copies.append(pltpu.make_async_copy(mean_rows, means_out, out_s.at[steps]))
    sums = own[0, :width]
    for t in range(1, steps):
        sums = sums + own[t, :width]
    m_hi, m_lo = split(means)
    outer = lambda u, v: lax.dot_general(u, v, (((0,), (0,)), ((), ())), preferred_element_type=F32)
    sums = sums + (outer(m_hi, m_hi) + (outer(m_hi, m_lo) + outer(m_lo, m_hi)))
    mom[...] = sums * (1.0 / (steps * n))

    def group_rows(k):
        return pl.ds(pl.multiple_of(k * rows, rows), rows)

    for j in range(1, GROUP):
        to = lax.rem(place + j, GROUP)
        c = send(mom.at[group_rows(to)], rs_buf.at[j - 1], rs_s.at[j - 1], rs_r.at[j - 1], base + to)
        c.start()
        sends.append(c)
    for c in out_copies:
        c.start()
    acc = mom[group_rows(place), :]
    for c, j in zip(sends[1 - GROUP :], range(1, GROUP)):
        c.wait_recv()
        acc = acc + rs_buf[j - 1]
    k = 0
    while GROUP << k < n:
        bf_snd[k] = acc
        c = send(bf_snd.at[k], bf_rcv.at[k], bf_s.at[k], bf_r.at[k], flip(GROUP << k))
        c.start()
        c.wait()
        acc = acc + bf_rcv[k]
        k += 1
    red[...] = acc
    gather = []
    for j in range(1, GROUP):
        to = lax.rem(place + j, GROUP)
        c = send(red, mom_all.at[group_rows(place)], ag_s.at[j - 1], ag_r.at[j - 1], base + to)
        c.start()
        gather.append(c)
    mom_all[group_rows(place), :] = acc
    for c in sends + gather:
        c.wait_send()
    for c in out_copies:
        c.wait()
    for c in gather:
        c.wait_recv()
    last = pltpu.make_async_copy(mom_all, mom_out, out_s.at[steps + 1])
    last.start()
    last.wait()


def hand_over(a, b, c, a_out, b_out, c_out, sems):
    copies = [
        pltpu.make_async_copy(x, y, sems.at[i])
        for i, (x, y) in enumerate(((b, b_out), (c, c_out), (a, a_out)))
    ]
    for copy in copies:
        copy.start()
    for copy in copies:
        copy.wait()


def local(n, gains, offsets, cov_terms):
    steps, width = gains.shape[0], gains.shape[1]
    levels = (n.bit_length() - 1) // 2
    assert n == 4**levels and levels > 1
    slab, lean, rows = 2 * width + PAD, width + PAD, width // GROUP
    far = max(1, (n // GROUP).bit_length() - 1)
    dma = pltpu.SemaphoreType.DMA
    vmem = pl.BlockSpec(memory_space=pltpu.VMEM)
    any_space = pl.BlockSpec(memory_space=pl.ANY)
    shapes = (
        jax.ShapeDtypeStruct((steps, width), F32),
        jax.ShapeDtypeStruct((steps, width, width), F32),
        jax.ShapeDtypeStruct((width, width), F32),
    )
    results = pl.pallas_call(
        functools.partial(kernel, n),
        out_shape=shapes,
        in_specs=[vmem] * 3,
        out_specs=(any_space,) * 3,
        scratch_shapes=[
            pltpu.VMEM((steps, slab, width), F32),
            pltpu.VMEM((levels - 1, 4, slab, width), F32),
            pltpu.VMEM((slab, width), F32),
            pltpu.VMEM((slab, width), F32),
            pltpu.VMEM((slab, width), F32),
            pltpu.VMEM((lean, width), F32),
            pltpu.VMEM((lean, width), F32),
            pltpu.VMEM((width, width), F32),
            pltpu.VMEM((GROUP - 1, rows, width), F32),
            pltpu.VMEM((far, rows, width), F32),
            pltpu.VMEM((far, rows, width), F32),
            pltpu.VMEM((rows, width), F32),
            pltpu.VMEM((width, width), F32),
            pltpu.VMEM((steps, width), F32),
            dma((levels - 1, 3)), dma((levels - 1, 3)),
            dma((3,)), dma((2,)),
            dma((GROUP - 1,)), dma((GROUP - 1,)),
            dma((far,)), dma((far,)),
            dma((GROUP - 1,)), dma((GROUP - 1,)),
            dma((steps + 2,)),
        ],
        compiler_params=pltpu.CompilerParams(collective_id=0, has_side_effects=True),
    )(gains, offsets, cov_terms)
    return pl.pallas_call(
        hand_over,
        out_shape=shapes,
        in_specs=[vmem] * 3,
        out_specs=(any_space,) * 3,
        scratch_shapes=[dma((3,))],
    )(*results)


def pack(s):
    half = s.shape[1] // 2
    row = lax.broadcasted_iota(jnp.int32, (half, 2 * half), 0)
    col = lax.broadcasted_iota(jnp.int32, (half, 2 * half), 1)
    low = s[half : 2 * half]
    both = jnp.where(jnp.logical_or(col >= half, row >= col), s[:half], pltpu.roll(low, half, 1))
    diag = jnp.sum(jnp.where(col - half == row, low, 0.0), axis=0, keepdims=True)
    first = lax.broadcasted_iota(jnp.int32, (PAD, 2 * half), 0) == 0
    return jnp.concatenate([both, jnp.where(first, s[2 * half :], diag)], axis=0)


def unpack(p):
    half = p.shape[1] // 2
    row = lax.broadcasted_iota(jnp.int32, (half, 2 * half), 0)
    col = lax.broadcasted_iota(jnp.int32, (half, 2 * half), 1)
    m = p[:half]
    turned = jnp.concatenate([m, m], axis=0).T
    top = jnp.where(jnp.logical_or(col >= half, row >= col), m, turned[:half])
    k = col - half
    right_low = jnp.where(row < k, pltpu.roll(m, half, 1), jnp.where(row == k, p[half + 1 : half + 2], turned[:half]))
    low = jnp.where(col < half, turned[half:], right_low)
    mean = jnp.broadcast_to(p[half : half + 1], (PAD, 2 * half))
    return jnp.concatenate([top, low, mean], axis=0)


def kernel16(
    gains_in, offsets_in, covs_in, means_out, covs_out, mom_out,
    gains, offsets, covs, own, ring, acc, suf, z_near, sym_snd, sym_rcv, z_sym, z_sym_rcv, top_snd, top_rcv, mom, rs_buf, pre_buf, red,
    own_right, own_low, own_both, z_right, z_low, z_both,
    in_s, ring_s, ring_r, z_s, z_r, rs_s, rs_r, pre_r, ag_s, ag_r, pace,
):
    steps, width = gains.shape[0], gains.shape[1]
    lean = width + PAD
    n = 16
    me, core = lax.axis_index("tm"), lax.axis_index("seq")
    digit, q = lax.rem(me, 4), lax.div(me, 4)
    rows = width // 4
    hosts = [4 + i for i in range(4)]
    is_host = jnp.logical_and(q == 1, core == 1)
    is_last = me == n - 1
    part, psi = pl.ds(0, lean), pl.ds(lean, width)
    packed = width // 2 + PAD
    dx, dy = 1 - 2 * lax.rem(digit, 2), 2 - 4 * lax.div(digit, 2)

    def at(tm, seq):
        return {"tm": tm, "seq": seq}

    def send(src, dst, s, r, to):
        return pltpu.make_async_remote_copy(
            src_ref=src, dst_ref=dst, send_sem=s, recv_sem=r,
            device_id=to, device_id_type=pl.DeviceIdType.MESH,
        )

    def landed(ref, sem):
        send(ref, ref, sem, sem, at(lax.rem(me + 1, n), core)).wait_recv()

    def sent(ref, sem):
        send(ref, ref, sem, sem, at(lax.rem(me + 1, n), core)).wait_send()

    barrier = pltpu.get_barrier_semaphore()

    def greet(tm, seq):
        pl.semaphore_signal(barrier, inc=1, device_id=at(tm, seq), device_id_type=pl.DeviceIdType.MESH)

    @pl.when(is_host)
    def _():
        for j in range(1, n):
            greet(lax.rem(me + j, n), core)
        for j in range(n):
            greet(j, 0)

    @pl.when(jnp.logical_not(is_host))
    def _():
        for j in (1, 2, 3):
            greet(me - digit + lax.rem(digit + j, 4), core)
        for host in hosts:
            greet(host, 1)

        @pl.when(core == 1)
        def _():
            for j in range(4):
                greet(me - digit + j, 0)

        @pl.when(q == 0)
        def _():
            greet(8 + digit, core)

        @pl.when(jnp.logical_or(q == 2, jnp.logical_and(q < 2, core == 0)))
        def _():
            greet(me + 4, core)

    fetch = [
        pltpu.make_async_copy(gains_in, gains, in_s.at[0]),
        pltpu.make_async_copy(covs_in, covs, in_s.at[1]),
        pltpu.make_async_copy(offsets_in, offsets, in_s.at[2]),
    ]
    for c in fetch:
        c.start()

    def compose(e, f):
        e_psi = e[lean:]
        x = mul(left(f), right(e_psi))
        p = e[:width] + mul(left(e_psi.T), right(x[:width]))
        out = [p, e[width:lean] + x[width:lean]]
        if f.shape[0] > lean:
            out.append(x[lean:])
        return jnp.concatenate(out, axis=0)

    def slot(d):
        return lax.rem(d + 4 - digit, 4)

    def total_of(d):
        return ring[slot(d)]

    def exchange(src, dst):
        for step in (dx + dy, dx, dy):
            there = lax.rem(4 - step, 4)
            send(src, dst(there), ring_s, ring_r.at[there], at(me + step, core)).start()

    def exchange_psi():
        exchange(ring.at[0, psi], lambda there: ring.at[there, psi])

    fetch[0].wait()
    ready = jnp.where(q == 0, 7, jnp.where(q == 2, 9 - core, 8)) + jnp.where(q == 1, 0, 4 - 4 * core)
    ready = jnp.where(is_host, 2 * n - 1, ready)

    @pl.when(is_last)
    def _():
        own[steps - 1, psi] = jnp.zeros((width, width), F32)
        for t in range(steps - 1):
            own[t, psi] = jnp.zeros((width, width), F32)
        ring[0, psi] = jnp.zeros((width, width), F32)

    @pl.when(jnp.logical_not(is_last))
    def _():
        run = gains[steps - 1].T
        own[steps - 1, psi] = run
        for t in reversed(range(steps - 1)):
            run = mul(left(run), right(gains[t].T))
            own[t, psi] = run
        ring[0, psi] = run

        @pl.when(q == 3)
        def _():
            ring[slot(3), psi] = jnp.zeros((width, width), F32)

    pl.semaphore_wait(barrier, ready)

    @pl.when(jnp.logical_and(jnp.logical_not(is_last), core == 0))
    def _():
        exchange_psi()

    fetch[1].wait()
    fetch[2].wait()

    def element(t):
        offset = jnp.broadcast_to(offsets[t : t + 1, :], (PAD, width))
        return jnp.concatenate([covs[t], offset, gains[t].T], axis=0)

    run = element(steps - 1)[:lean]
    own[steps - 1, part] = run
    for t in reversed(range(steps - 1)):
        run = compose(element(t), run)
        own[t, part] = run
    ring[0, part] = run
    sym_snd[...] = pack(run)

    @pl.when(core == 1)
    def _():
        pl.semaphore_wait(pace, 4)

        @pl.when(jnp.logical_not(is_last))
        def _():
            exchange_psi()

    exchange(sym_snd, lambda there: sym_rcv.at[there])

    @pl.when(core == 0)
    def _():
        for j in range(4):
            pl.semaphore_signal(pace, inc=1, device_id=at(me - digit + j, 1), device_id_type=pl.DeviceIdType.MESH)

    def prepare():
        for t in range(steps):
            e, cols = own[t, psi], pl.ds(t * width, width)
            own_right[:, cols], own_low[:, cols] = right(e)
            own_both[t] = left(e.T)[1]

    def apply(f):
        x = mul(left(f), (own_right[...], own_low[...]))
        out = []
        for t in range(steps):
            both, xt = own_both[t], x[:, t * width : (t + 1) * width]
            cov = own[t, :width] + mul((both[:, :width], both), right(xt[:width]))
            out.append((cov, own[t, width:lean] + xt[width:lean], xt[lean:]))
        return out

    def absorb(f):
        for t, (cov, mean, rest) in enumerate(apply(f)):
            own[t, :width] = cov
            own[t, width:lean] = mean
            if f.shape[0] > lean:
                own[t, psi] = rest

    def finish(found):
        means = jnp.concatenate([mean[:1] for _, mean in found], axis=0)
        sums = found[0][0]
        for cov, _ in found[1:]:
            sums = sums + cov
        m_hi, m_lo = split(means)
        outer = lambda u, v: lax.dot_general(u, v, (((0,), (0,)), ((), ())), preferred_element_type=F32)
        sums = sums + (outer(m_hi, m_hi) + (outer(m_hi, m_lo) + outer(m_lo, m_hi)))
        mom[...] = sums * (1.0 / (steps * n))
        means_out[...] = means
        for t, (cov, _) in enumerate(found):
            covs_out[t] = cov

    def block(i):
        return pl.ds(i * rows, rows)

    mine = pl.ds(pl.multiple_of(digit * rows, rows), rows)

    def arrive(d):
        here = slot(d)

        @pl.when(digit != d)
        def _():
            if d == 3:
                @pl.when(q == 3)
                def _():
                    landed(sym_rcv.at[here], ring_r.at[here])

                @pl.when(q != 3)
                def _():
                    landed(ring.at[here, pl.ds(0, packed + width)], ring_r.at[here])
            else:
                landed(ring.at[here, pl.ds(0, packed + width)], ring_r.at[here])
            ring[here, part] = unpack(sym_rcv[here])

    down, down2 = lax.rem(me + n - 4, n), lax.rem(me + n - 8, n)
    near_sym = send(z_sym, z_sym_rcv, z_s, z_r.at[0], at(down, core))
    near_psi = send(acc.at[psi], z_near.at[psi], z_s, z_r.at[0], at(down, core))
    top_far = send(top_snd, top_rcv, z_s, z_r.at[1], at(down2, core))
    top_near = send(top_snd, top_rcv, z_s, z_r.at[1], at(down, core))

    arrive(3)
    acc[...] = total_of(3)
    for d in (2, 1, 0):
        @pl.when(digit == d)
        def _():
            suf[...] = acc[...]

        arrive(d)

        @pl.when(q == 3)
        def _():
            state = compose(total_of(d), acc[part, :])
            if d:
                acc[part, :] = state
            else:
                z_sym[...] = pack(state)
                near_sym.start()

        @pl.when(q < 3)
        def _():
            acc[...] = compose(total_of(d), acc[...])

    @pl.when(q == 1)
    def _():
        z_sym[...] = pack(acc[part, :])
        near_sym.start()
        near_psi.start()

    @pl.when(q == 2)
    def _():
        z_right[...], z_low[...] = right(acc[psi, :])
        z_both[...] = left(acc[psi, :].T)[1]

    prepare()

    @pl.when(digit < 3)
    def _():
        @pl.when(q == 3)
        def _():
            absorb(suf[part, :])

        @pl.when(q < 3)
        def _():
            absorb(suf[...])
            prepare()

    @pl.when(q == 2)
    def _():
        near_sym.wait_recv()
        near = unpack(z_sym_rcv[...])
        x = mul(left(near), (z_right[...], z_low[...]))
        both = z_both[...]
        cov = acc[:width, :] + mul((both[:, :width], both), right(x[:width]))
        top_snd[...] = pack(jnp.concatenate([cov, acc[width:lean, :] + x[width:]], axis=0))
        top_far.start()
        top_near.start()
        absorb(near)

    @pl.when(q == 0)
    def _():
        landed(z_near.at[pl.ds(0, packed + width)], z_r.at[0])
        z_near[part, :] = unpack(z_sym_rcv[...])
        absorb(z_near[...])
        prepare()

    @pl.when(q < 2)
    def _():
        top_near.wait_recv()
        finish([found[:2] for found in apply(unpack(top_rcv[...]))])

        for i, host in enumerate(hosts):
            scatter = send(mom.at[block(i)], rs_buf.at[core, me], rs_s, rs_r.at[core], at(host, 1))

            @pl.when(jnp.logical_or(me != host, core == 0))
            def _():
                scatter.start()

    @pl.when(q >= 2)
    def _():
        finish([(own[t, :width], own[t, width:lean]) for t in range(steps)])

        @pl.when(q == 3)
        def _():
            near_sym.wait_send()

        for step in (dx + dy, dx, dy):
            to = digit + step
            theirs = pl.ds(pl.multiple_of(to * rows, rows), rows)
            send(mom.at[theirs], pre_buf.at[lax.rem(4 - step, 4)], rs_s, pre_r, at(me + step, core)).start()
        landed(pre_buf.at[pl.ds(1, 3)], pre_r)
        pre_buf[0] = (mom[mine, :] + pre_buf[1]) + (pre_buf[2] + pre_buf[3])
        send(pre_buf.at[0], rs_buf.at[core, 6 + q], rs_s, rs_r.at[core], at(4 + digit, 1)).start()

    @pl.when(is_host)
    def _():
        rs_buf[1, me] = mom[mine, :]
        for p in (0, 1):
            landed(rs_buf.at[p, pl.ds(0, 10 - p)], rs_r.at[p])
            parts = [rs_buf[p, j] for j in range(10)]
            while len(parts) > 1:
                parts = [u + v for u, v in zip(parts[::2], parts[1::2])] + parts[len(parts) & ~1 :]
            red[p] = parts[0]
            for to in range(n):
                gather = send(red.at[p], mom_out.at[mine], ag_s, ag_r, at(to, p))
                if p == 0:
                    gather.start()
                else:
                    pl.when(me != to)(gather.start)
            if p == 1:
                mom_out[mine, :] = parts[0]
        landed(mom_out.at[pl.ds(0, 3 * rows)], ag_r)
        for p in (0, 1):
            sent(own.at[0, pl.ds(0, 2 * width)], ag_s)
            sent(own.at[0, pl.ds(0, 2 * width - p * rows)], ag_s)
        sent(mom.at[pl.ds(0, 3 * rows)], rs_s)

    @pl.when(jnp.logical_not(is_host))
    def _():
        landed(mom_out, ag_r)
        sent(mom, rs_s)

    sent(sym_rcv.at[pl.ds(1, 3)], ring_s)

    @pl.when(jnp.logical_not(is_last))
    def _():
        sent(ring.at[pl.ds(1, 3), psi], ring_s)

    @pl.when(q == 1)
    def _():
        near_sym.wait_send()
        near_psi.wait_send()

    @pl.when(q == 2)
    def _():
        top_far.wait_send()
        top_near.wait_send()


def write_out(a, b, c, a_out, b_out, c_out, sems):
    copies = [
        pltpu.make_async_copy(x, y, sems.at[i])
        for i, (x, y) in enumerate(((b, b_out), (c, c_out), (a, a_out)))
    ]
    for copy in copies:
        copy.start()
    for copy in copies:
        copy.wait()


def local16(gains, offsets, cov_terms):
    steps, width = gains.shape[0], gains.shape[1]
    slab, rows, packed = 2 * width + PAD, width // 4, width // 2 + PAD
    dma = pltpu.SemaphoreType.DMA
    vmem = pl.BlockSpec(memory_space=pltpu.VMEM)
    shapes = ((steps, width), (steps, width, width), (width, width))
    results = pl.pallas_call(
        kernel16,
        out_shape=tuple(pltpu.VMEM(s, F32) for s in shapes),
        in_specs=[pl.BlockSpec(memory_space=pltpu.HBM)] * 3,
        out_specs=(vmem,) * 3,
        scratch_shapes=[
            pltpu.VMEM((steps, width, width), F32),
            pltpu.VMEM((steps, width), F32),
            pltpu.VMEM((steps, width, width), F32),
            pltpu.VMEM((steps, slab, width), F32),
            pltpu.VMEM((4, slab, width), F32),
            pltpu.VMEM((slab, width), F32),
            pltpu.VMEM((slab, width), F32),
            pltpu.VMEM((slab, width), F32),
            pltpu.VMEM((packed, width), F32),
            pltpu.VMEM((4, packed, width), F32),
            pltpu.VMEM((packed, width), F32),
            pltpu.VMEM((packed, width), F32),
            pltpu.VMEM((packed, width), F32),
            pltpu.VMEM((packed, width), F32),
            pltpu.VMEM((width, width), F32),
            pltpu.VMEM((2, 10, rows, width), F32),
            pltpu.VMEM((4, rows, width), F32),
            pltpu.VMEM((2, rows, width), F32),
            pltpu.VMEM((2 * width, steps * width), BF16),
            pltpu.VMEM((width, steps * width), BF16),
            pltpu.VMEM((steps, width, 2 * width), BF16),
            pltpu.VMEM((2 * width, width), BF16),
            pltpu.VMEM((width, width), BF16),
            pltpu.VMEM((width, 2 * width), BF16),
            dma((3,)), dma, dma((4,)), dma, dma((2,)), dma, dma((2,)), dma, dma, dma, pltpu.SemaphoreType.REGULAR,
        ],
        compiler_params=pltpu.CompilerParams(collective_id=0, has_side_effects=True),
    )(gains, offsets, cov_terms)
    results = [pltpu.with_memory_space_constraint(r, pltpu.VMEM) for r in results]
    return pl.pallas_call(
        write_out,
        out_shape=tuple(jax.ShapeDtypeStruct(s, F32) for s in shapes),
        in_specs=[vmem] * 3,
        out_specs=(pl.BlockSpec(memory_space=pl.ANY),) * 3,
        scratch_shapes=[dma((3,))],
    )(*results)


def solution(mesh):
    n = mesh.shape["tm"]
    in_specs = (P(("seq", "tm"), None, None), P(("seq", "tm"), None), P(("seq", "tm"), None, None))
    out_specs = (P(("seq", "tm"), None), P(("seq", "tm"), None, None), P("seq", None))
    return jax.shard_map(
        local16 if n == 16 and mesh.shape["seq"] == 2 else functools.partial(local, n), mesh=mesh, in_specs=in_specs, out_specs=out_specs, check_vma=False
    )
```

```python
import functools

import jax
import jax.numpy as jnp
from jax import lax
from jax.experimental import pallas as pl
from jax.experimental.pallas import tpu as pltpu
from jax.sharding import PartitionSpec as P

F32 = jnp.float32
BF16 = jnp.bfloat16
PAD = 8
GROUP = 16


def split(x):
    hi = x.astype(BF16)
    return hi, (x - hi.astype(F32)).astype(BF16)


def left(x):
    hi, lo = split(x)
    return hi, jnp.concatenate([hi, lo], axis=1)


def right(w):
    hi, lo = split(w)
    return jnp.concatenate([hi, hi], axis=0), lo


def mul(x, w):
    hi, both = x
    w_hi, w_lo = w
    return jnp.dot(both, w_hi, preferred_element_type=F32) + jnp.dot(
        hi, w_lo, preferred_element_type=F32
    )


def kernel(
    n, gains, offsets, covs, means_out, covs_out, mom_out,
    own, ring, suf, z_snd, z_near, top_snd, top_rcv,
    mom, rs_buf, bf_snd, bf_rcv, red, mom_all, mean_rows,
    ring_s, ring_r, z_s, z_r, rs_s, rs_r, bf_s, bf_r, ag_s, ag_r, out_s,
):
    steps, width = gains.shape[0], gains.shape[1]
    lean = width + PAD
    me = lax.axis_index("tm")
    levels = (n.bit_length() - 1) // 2
    quarter = n // 4
    rows = width // GROUP
    place = lax.rem(me, GROUP)
    base = me - place

    def flip(step):
        return me + step * (1 - 2 * lax.rem(lax.div(me, step), 2))

    def digit_of(stride):
        return lax.rem(lax.div(me, stride), 4)

    def peer(stride, j):
        digit = digit_of(stride)
        return me + stride * (lax.rem(digit + j, 4) - digit)

    peers = [base + lax.rem(place + j, GROUP) for j in range(1, GROUP)]
    peers += [peer(4**l, j) for l in range(2, levels) for j in (1, 2, 3)]
    barrier = pltpu.get_barrier_semaphore()
    for to in peers:
        pl.semaphore_signal(barrier, inc=1, device_id={"tm": to}, device_id_type=pl.DeviceIdType.MESH)

    def send(src, dst, s, r, to):
        return pltpu.make_async_remote_copy(
            src_ref=src, dst_ref=dst, send_sem=s, recv_sem=r,
            device_id={"tm": to}, device_id_type=pl.DeviceIdType.MESH,
        )

    def compose(e, f):
        e_psi = e[lean:]
        x = mul(left(f), right(e_psi))
        p = e[:width] + mul(left(e_psi.T), right(x[:width]))
        out = [p, e[width:lean] + x[width:lean]]
        if f.shape[0] > lean:
            out.append(x[lean:])
        return jnp.concatenate(out, axis=0)

    for t in reversed(range(steps)):
        gain = gains[t]
        if t == steps - 1:
            gain = jnp.where(me == n - 1, jnp.zeros_like(gain), gain)
        offset = jnp.broadcast_to(offsets[t : t + 1, :], (PAD, width))
        element = jnp.concatenate([covs[t], offset, gain.T], axis=0)
        own[t] = element if t == steps - 1 else compose(element, own[t + 1])

    def absorb(f):
        for t in range(steps):
            own[t, : f.shape[0]] = compose(own[t], f)

    pl.semaphore_wait(barrier, len(peers))

    def deferred(l):
        digit = digit_of(4**l)

        @pl.when(digit == 0)
        def _():
            suf[...] = compose(ring[l, 1], suf[...])

        @pl.when(digit == 2)
        def _():
            suf[...] = ring[l, 3]

        @pl.when(digit < 3)
        def _():
            absorb(suf[...])

    sends = []
    total = own[0]
    for l in range(levels - 1):
        digit = digit_of(4**l)
        ring[l, digit] = total
        started = []
        for j in (2, 1, 3):
            c = send(
                ring.at[l, digit], ring.at[l, digit], ring_s.at[l, j - 1], ring_r.at[l, j - 1], peer(4**l, j)
            )
            c.start()
            started.append(c)
        if l:
            deferred(l - 1)
        for j in (1, 2, 3):
            came = lax.rem(digit + 4 - j, 4)
            send(
                ring.at[l, came], ring.at[l, came], ring_s.at[l, j - 1], ring_r.at[l, j - 1], peer(4**l, j)
            ).wait_recv()
        sends += started
        high = compose(ring[l, 2], ring[l, 3])
        total = compose(compose(ring[l, 0], ring[l, 1]), high)
        suf[...] = high
    z_snd[...] = total

    q = lax.div(me, quarter)
    down, down2 = lax.rem(me + n - quarter, n), lax.rem(me + n - 2 * quarter, n)
    part = pl.ds(0, lean)
    near_full = send(z_snd, z_near, z_s.at[0], z_r.at[0], down)
    near_lean = send(z_snd.at[part], z_near.at[part], z_s.at[0], z_r.at[0], down)
    top_far = send(top_snd, top_rcv, z_s.at[1], z_r.at[1], down2)
    top_near = send(top_snd, top_rcv, z_s.at[2], z_r.at[1], down)

    @pl.when(q == 3)
    def _():
        near_lean.start()

    @pl.when(q == 1)
    def _():
        near_full.start()

    deferred(levels - 2)

    @pl.when(q == 3)
    def _():
        near_lean.wait_send()

    @pl.when(q == 2)
    def _():
        near_lean.wait_recv()
        top_snd[...] = compose(z_snd[...], z_near[part, :])
        top_far.start()
        top_near.start()
        absorb(z_near[part, :])
        top_far.wait_send()
        top_near.wait_send()

    @pl.when(q == 0)
    def _():
        near_full.wait_recv()
        absorb(z_near[...])

    @pl.when(q < 2)
    def _():
        top_near.wait_recv()
        absorb(top_rcv[...])

    @pl.when(q == 1)
    def _():
        near_full.wait_send()

    out_copies = []
    for t in range(steps):
        out_copies.append(pltpu.make_async_copy(own.at[t, pl.ds(0, width)], covs_out.at[t], out_s.at[t]))
    means = jnp.concatenate([own[t, width : width + 1] for t in range(steps)], axis=0)
    mean_rows[...] = means
    out_copies.append(pltpu.make_async_copy(mean_rows, means_out, out_s.at[steps]))
    sums = own[0, :width]
    for t in range(1, steps):
        sums = sums + own[t, :width]
    m_hi, m_lo = split(means)
    outer = lambda u, v: lax.dot_general(u, v, (((0,), (0,)), ((), ())), preferred_element_type=F32)
    sums = sums + (outer(m_hi, m_hi) + (outer(m_hi, m_lo) + outer(m_lo, m_hi)))
    mom[...] = sums * (1.0 / (steps * n))

    def group_rows(k):
        return pl.ds(pl.multiple_of(k * rows, rows), rows)

    for j in range(1, GROUP):
        to = lax.rem(place + j, GROUP)
        c = send(mom.at[group_rows(to)], rs_buf.at[j - 1], rs_s.at[j - 1], rs_r.at[j - 1], base + to)
        c.start()
        sends.append(c)
    for c in out_copies:
        c.start()
    acc = mom[group_rows(place), :]
    for c, j in zip(sends[1 - GROUP :], range(1, GROUP)):
        c.wait_recv()
        acc = acc + rs_buf[j - 1]
    k = 0
    while GROUP << k < n:
        bf_snd[k] = acc
        c = send(bf_snd.at[k], bf_rcv.at[k], bf_s.at[k], bf_r.at[k], flip(GROUP << k))
        c.start()
        c.wait()
        acc = acc + bf_rcv[k]
        k += 1
    red[...] = acc
    gather = []
    for j in range(1, GROUP):
        to = lax.rem(place + j, GROUP)
        c = send(red, mom_all.at[group_rows(place)], ag_s.at[j - 1], ag_r.at[j - 1], base + to)
        c.start()
        gather.append(c)
    mom_all[group_rows(place), :] = acc
    for c in sends + gather:
        c.wait_send()
    for c in out_copies:
        c.wait()
    for c in gather:
        c.wait_recv()
    last = pltpu.make_async_copy(mom_all, mom_out, out_s.at[steps + 1])
    last.start()
    last.wait()


def hand_over(a, b, c, a_out, b_out, c_out, sems):
    copies = [
        pltpu.make_async_copy(x, y, sems.at[i])
        for i, (x, y) in enumerate(((b, b_out), (c, c_out), (a, a_out)))
    ]
    for copy in copies:
        copy.start()
    for copy in copies:
        copy.wait()


def local(n, gains, offsets, cov_terms):
    steps, width = gains.shape[0], gains.shape[1]
    levels = (n.bit_length() - 1) // 2
    assert n == 4**levels and levels > 1
    slab, lean, rows = 2 * width + PAD, width + PAD, width // GROUP
    far = max(1, (n // GROUP).bit_length() - 1)
    dma = pltpu.SemaphoreType.DMA
    vmem = pl.BlockSpec(memory_space=pltpu.VMEM)
    any_space = pl.BlockSpec(memory_space=pl.ANY)
    shapes = (
        jax.ShapeDtypeStruct((steps, width), F32),
        jax.ShapeDtypeStruct((steps, width, width), F32),
        jax.ShapeDtypeStruct((width, width), F32),
    )
    results = pl.pallas_call(
        functools.partial(kernel, n),
        out_shape=shapes,
        in_specs=[vmem] * 3,
        out_specs=(any_space,) * 3,
        scratch_shapes=[
            pltpu.VMEM((steps, slab, width), F32),
            pltpu.VMEM((levels - 1, 4, slab, width), F32),
            pltpu.VMEM((slab, width), F32),
            pltpu.VMEM((slab, width), F32),
            pltpu.VMEM((slab, width), F32),
            pltpu.VMEM((lean, width), F32),
            pltpu.VMEM((lean, width), F32),
            pltpu.VMEM((width, width), F32),
            pltpu.VMEM((GROUP - 1, rows, width), F32),
            pltpu.VMEM((far, rows, width), F32),
            pltpu.VMEM((far, rows, width), F32),
            pltpu.VMEM((rows, width), F32),
            pltpu.VMEM((width, width), F32),
            pltpu.VMEM((steps, width), F32),
            dma((levels - 1, 3)), dma((levels - 1, 3)),
            dma((3,)), dma((2,)),
            dma((GROUP - 1,)), dma((GROUP - 1,)),
            dma((far,)), dma((far,)),
            dma((GROUP - 1,)), dma((GROUP - 1,)),
            dma((steps + 2,)),
        ],
        compiler_params=pltpu.CompilerParams(collective_id=0, has_side_effects=True),
    )(gains, offsets, cov_terms)
    return pl.pallas_call(
        hand_over,
        out_shape=shapes,
        in_specs=[vmem] * 3,
        out_specs=(any_space,) * 3,
        scratch_shapes=[dma((3,))],
    )(*results)


def pack(s):
    half = s.shape[1] // 2
    row = lax.broadcasted_iota(jnp.int32, (half, 2 * half), 0)
    col = lax.broadcasted_iota(jnp.int32, (half, 2 * half), 1)
    low = s[half : 2 * half]
    both = jnp.where(jnp.logical_or(col >= half, row >= col), s[:half], pltpu.roll(low, half, 1))
    diag = jnp.sum(jnp.where(col - half == row, low, 0.0), axis=0, keepdims=True)
    first = lax.broadcasted_iota(jnp.int32, (PAD, 2 * half), 0) == 0
    return jnp.concatenate([both, jnp.where(first, s[2 * half :], diag)], axis=0)


def unpack(p):
    half = p.shape[1] // 2
    row = lax.broadcasted_iota(jnp.int32, (half, 2 * half), 0)
    col = lax.broadcasted_iota(jnp.int32, (half, 2 * half), 1)
    m = p[:half]
    turned = jnp.concatenate([m, m], axis=0).T
    top = jnp.where(jnp.logical_or(col >= half, row >= col), m, turned[:half])
    k = col - half
    right_low = jnp.where(row < k, pltpu.roll(m, half, 1), jnp.where(row == k, p[half + 1 : half + 2], turned[:half]))
    low = jnp.where(col < half, turned[half:], right_low)
    mean = jnp.broadcast_to(p[half : half + 1], (PAD, 2 * half))
    return jnp.concatenate([top, low, mean], axis=0)


def kernel16(
    gains_in, offsets_in, covs_in, means_out, covs_out, mom_out,
    gains, offsets, covs, own, ring, acc, suf, z_near, sym_snd, sym_rcv, z_sym, z_sym_rcv, top_snd, top_rcv, mom, mom_rcv, rs_buf, pre_buf, red,
    own_right, own_low, own_both, z_right, z_low, z_both,
    in_s, ring_s, ring_r, z_s, z_r, rs_s, rs_r, pre_r, ag_s, ag_r, pace,
):
    steps, width = gains.shape[0], gains.shape[1]
    lean = width + PAD
    n = 16
    me, core = lax.axis_index("tm"), lax.axis_index("seq")
    digit, q = lax.rem(me, 4), lax.div(me, 4)
    rows = (width // 2 + PAD) // 3
    central = [4 + i for i in range(4)]
    hosts = central[:3]
    is_central = jnp.logical_and(q == 1, core == 1)
    is_host = jnp.logical_and(is_central, digit < 3)
    is_last = me == n - 1
    part, psi = pl.ds(0, lean), pl.ds(lean, width)
    packed = width // 2 + PAD
    dx, dy = 1 - 2 * lax.rem(digit, 2), 2 - 4 * lax.div(digit, 2)

    def at(tm, seq):
        return {"tm": tm, "seq": seq}

    def send(src, dst, s, r, to):
        return pltpu.make_async_remote_copy(
            src_ref=src, dst_ref=dst, send_sem=s, recv_sem=r,
            device_id=to, device_id_type=pl.DeviceIdType.MESH,
        )

    def landed(ref, sem):
        send(ref, ref, sem, sem, at(lax.rem(me + 1, n), core)).wait_recv()

    def sent(ref, sem):
        send(ref, ref, sem, sem, at(lax.rem(me + 1, n), core)).wait_send()

    barrier = pltpu.get_barrier_semaphore()

    def greet(tm, seq):
        pl.semaphore_signal(barrier, inc=1, device_id=at(tm, seq), device_id_type=pl.DeviceIdType.MESH)

    @pl.when(is_central)
    def _():
        for j in range(1, n):
            greet(lax.rem(me + j, n), core)
        for j in range(n):
            greet(j, 0)

    @pl.when(jnp.logical_not(is_central))
    def _():
        @pl.when(jnp.logical_or(q < 3, digit < 2))
        def _():
            for step in (dx, dy, dx + dy):
                greet(me + step, core)

        @pl.when(jnp.logical_and(q == 3, digit == 2))
        def _():
            greet(me + 1, core)

        for host in central:
            greet(host, 1)

        @pl.when(core == 1)
        def _():
            greet(me - digit, 0)

        @pl.when(q == 0)
        def _():
            greet(8 + digit, core)

        @pl.when(q == 2)
        def _():
            greet(12 + lax.rem(digit, 2), core)

        @pl.when(jnp.logical_and(q < 2, core == 0))
        def _():
            greet(me + 4, core)

    fetch = [
        pltpu.make_async_copy(gains_in, gains, in_s.at[0]),
        pltpu.make_async_copy(covs_in, covs, in_s.at[1]),
        pltpu.make_async_copy(offsets_in, offsets, in_s.at[2]),
    ]
    for c in fetch:
        c.start()

    def compose(e, f):
        e_psi = e[lean:]
        x = mul(left(f), right(e_psi))
        p = e[:width] + mul(left(e_psi.T), right(x[:width]))
        out = [p, e[width:lean] + x[width:lean]]
        if f.shape[0] > lean:
            out.append(x[lean:])
        return jnp.concatenate(out, axis=0)

    def slot(d):
        return lax.rem(d + 4 - digit, 4)

    def total_of(d):
        return ring[slot(d)]

    def exchange(src, dst):
        upper, lower = jnp.logical_or(q < 3, digit >= 2), jnp.logical_or(q < 3, digit != 2)
        for step, needed in ((dx + dy, upper), (dy, upper), (dx, lower)):
            there = lax.rem(4 - step, 4)
            pl.when(needed)(send(src, dst(there), ring_s, ring_r.at[there], at(me + step, core)).start)

    def exchange_psi():
        exchange(ring.at[0, psi], lambda there: ring.at[there, psi])

    fetch[0].wait()
    ready = jnp.where(q == 0, 7, jnp.where(q == 1, 8, jnp.where(q == 2, 9 - core, jnp.where(digit < 2, 7, 4 + digit))))
    leads = jnp.logical_and(core == 0, digit == 3)
    ready = ready + jnp.where(jnp.logical_and(core == 0, jnp.logical_and(digit == 0, q != 1)), 4, 0)
    ready = jnp.where(is_central, 2 * n - 1, ready)

    @pl.when(is_last)
    def _():
        own[steps - 1, psi] = jnp.zeros((width, width), F32)
        for t in range(steps - 1):
            own[t, psi] = jnp.zeros((width, width), F32)
        ring[0, psi] = jnp.zeros((width, width), F32)

    @pl.when(jnp.logical_not(is_last))
    def _():
        run = gains[steps - 1].T
        own[steps - 1, psi] = run
        for t in reversed(range(steps - 1)):
            run = mul(left(run), right(gains[t].T))
            own[t, psi] = run
        ring[0, psi] = run

    pl.semaphore_wait(barrier, ready)

    @pl.when(jnp.logical_and(jnp.logical_not(is_last), core == 0))
    def _():
        exchange_psi()

    fetch[1].wait()
    fetch[2].wait()

    def element(t):
        offset = jnp.broadcast_to(offsets[t : t + 1, :], (PAD, width))
        return jnp.concatenate([covs[t], offset, gains[t].T], axis=0)

    run = element(steps - 1)[:lean]
    own[steps - 1, part] = run
    for t in reversed(range(steps - 1)):
        run = compose(element(t), run)
        own[t, part] = run
    ring[0, part] = run
    sym_snd[...] = pack(run)

    @pl.when(core == 1)
    def _():
        pl.semaphore_wait(pace, 1)

        @pl.when(jnp.logical_not(is_last))
        def _():
            exchange_psi()

    exchange(sym_snd, lambda there: sym_rcv.at[there])

    @pl.when(leads)
    def _():
        pl.semaphore_signal(pace, inc=1, device_id=at(me - 3, 0), device_id_type=pl.DeviceIdType.MESH)

    @pl.when(jnp.logical_and(core == 0, digit == 0))
    def _():
        pl.semaphore_wait(pace, 1)
        for j in range(4):
            pl.semaphore_signal(pace, inc=1, device_id=at(me + j, 1), device_id_type=pl.DeviceIdType.MESH)

    def prepare():
        for t in range(steps):
            e, cols = own[t, psi], pl.ds(t * width, width)
            own_right[:, cols], own_low[:, cols] = right(e)
            own_both[t] = left(e.T)[1]

    def apply(f):
        x = mul(left(f), (own_right[...], own_low[...]))
        out = []
        for t in range(steps):
            both, xt = own_both[t], x[:, t * width : (t + 1) * width]
            cov = own[t, :width] + mul((both[:, :width], both), right(xt[:width]))
            out.append((cov, own[t, width:lean] + xt[width:lean], xt[lean:]))
        return out

    def absorb(f):
        for t, (cov, mean, rest) in enumerate(apply(f)):
            own[t, :width] = cov
            own[t, width:lean] = mean
            if f.shape[0] > lean:
                own[t, psi] = rest

    def finish(found):
        means = jnp.concatenate([mean[:1] for _, mean in found], axis=0)
        sums = found[0][0]
        for cov, _ in found[1:]:
            sums = sums + cov
        m_hi, m_lo = split(means)
        outer = lambda u, v: lax.dot_general(u, v, (((0,), (0,)), ((), ())), preferred_element_type=F32)
        sums = sums + (outer(m_hi, m_hi) + (outer(m_hi, m_lo) + outer(m_lo, m_hi)))
        mom[...] = pack(jnp.concatenate([sums * (1.0 / (steps * n)), jnp.zeros((PAD, width), F32)], axis=0))
        means_out[...] = means
        for t, (cov, _) in enumerate(found):
            covs_out[t] = cov

    def block(i):
        return pl.ds(i * rows, rows)

    mine = pl.ds(pl.multiple_of(lax.rem(digit, 3) * rows, PAD), rows)

    def arrive(d):
        here = slot(d)

        @pl.when(digit != d)
        def _():
            landed(ring.at[here, pl.ds(0, packed + width)], ring_r.at[here])
            ring[here, part] = unpack(sym_rcv[here])

    def state_of(base, f, right_ref, low_ref, both):
        x = mul(left(f), (right_ref, low_ref))
        cov = base[:width] + mul((both[:, :width], both), right(x[:width]))
        return jnp.concatenate([cov, base[width:lean] + x[width:]], axis=0)

    def hold(e):
        z_right[...], z_low[...] = right(e)
        z_both[...] = left(e.T)[1]

    down, down2 = lax.rem(me + n - 4, n), lax.rem(me + n - 8, n)
    near_sym = send(z_sym, z_sym_rcv, z_s, z_r.at[0], at(down, core))
    near_psi = send(acc.at[psi], z_near.at[psi], z_s, z_r.at[0], at(down, core))
    top_far = send(top_snd, top_rcv, z_s, z_r.at[1], at(down2, core))
    top_near = send(top_snd, top_rcv, z_s, z_r.at[1], at(down, core))
    far_sym = send(z_sym, z_sym_rcv, z_s, z_r.at[0], at(lax.rem(me + n - 2, n), core))

    @pl.when(jnp.logical_and(q == 3, digit < 2))
    def _():
        arrive(0)
        arrive(1)
        acc[...] = compose(total_of(0), total_of(1))
        hold(acc[psi, :])
        arrive(2)
        e = total_of(2)[lean:]
        cols = pl.ds(0, width)
        own_right[:, cols], own_low[:, cols] = right(e)
        own_both[0] = left(e.T)[1]
        landed(sym_rcv.at[slot(3)], ring_r.at[slot(3)])
        newest = unpack(sym_rcv[slot(3)])
        state = state_of(total_of(2)[:lean], newest, own_right[:, cols], own_low[:, cols], own_both[0])
        suf[part, :] = state
        z_sym[...] = pack(state_of(acc[part, :], state, z_right[...], z_low[...], z_both[...]))
        far_sym.start()
        near_sym.start()

        @pl.when(digit == 0)
        def _():
            suf[part, :] = compose(total_of(1), suf[part, :])

    @pl.when(jnp.logical_and(q == 3, digit == 2))
    def _():
        landed(sym_rcv.at[slot(3)], ring_r.at[slot(3)])
        suf[part, :] = unpack(sym_rcv[slot(3)])

    @pl.when(q < 3)
    def _():
        arrive(3)
        acc[...] = total_of(3)
        for d in (2, 1, 0):
            @pl.when(digit == d)
            def _():
                suf[...] = acc[...]

            arrive(d)
            acc[...] = compose(total_of(d), acc[...])

    @pl.when(q == 1)
    def _():
        z_sym[...] = pack(acc[part, :])
        near_sym.start()
        near_psi.start()

    @pl.when(q == 2)
    def _():
        hold(acc[psi, :])

    prepare()

    @pl.when(digit < 3)
    def _():
        @pl.when(q == 3)
        def _():
            absorb(suf[part, :])

        @pl.when(q < 3)
        def _():
            absorb(suf[...])
            prepare()

    @pl.when(q == 2)
    def _():
        near_sym.wait_recv()
        near = unpack(z_sym_rcv[...])
        top_snd[...] = pack(state_of(acc[part, :], near, z_right[...], z_low[...], z_both[...]))
        top_far.start()
        top_near.start()
        absorb(near)

    @pl.when(q == 0)
    def _():
        landed(z_near.at[pl.ds(0, packed + width)], z_r.at[0])
        z_near[part, :] = unpack(z_sym_rcv[...])
        absorb(z_near[...])
        prepare()

    @pl.when(q < 2)
    def _():
        top_near.wait_recv()
        finish([found[:2] for found in apply(unpack(top_rcv[...]))])

        for i, host in enumerate(hosts):
            scatter = send(mom.at[block(i)], rs_buf.at[core, me], rs_s, rs_r.at[core], at(host, 1))

            @pl.when(jnp.logical_or(me != host, core == 0))
            def _():
                scatter.start()

    @pl.when(q >= 2)
    def _():
        finish([(own[t, :width], own[t, width:lean]) for t in range(steps)])

        @pl.when(jnp.logical_and(q == 3, digit < 2))
        def _():
            near_sym.wait_send()
            far_sym.wait_send()

        for step in (dx + dy, dx, dy):
            to = digit + step
            theirs = pl.ds(pl.multiple_of(lax.rem(to, 3) * rows, PAD), rows)
            part_sum = send(mom.at[theirs], pre_buf.at[lax.rem(4 - step, 4)], rs_s, pre_r, at(me + step, core))
            pl.when(to < 3)(part_sum.start)

        @pl.when(digit < 3)
        def _():
            landed(pre_buf.at[pl.ds(1, 3)], pre_r)
            pre_buf[0] = (mom[mine, :] + pre_buf[1]) + (pre_buf[2] + pre_buf[3])
            send(pre_buf.at[0], rs_buf.at[core, 6 + q], rs_s, rs_r.at[core], at(4 + digit, 1)).start()

    @pl.when(is_host)
    def _():
        rs_buf[1, me] = mom[mine, :]
        for p in (1, 0):
            landed(rs_buf.at[p, pl.ds(0, 10 - p)], rs_r.at[p])
            parts = [rs_buf[p, j] for j in range(10)]
            while len(parts) > 1:
                parts = [u + v for u, v in zip(parts[::2], parts[1::2])] + parts[len(parts) & ~1 :]
            red[p] = parts[0]
            if p == 1:
                mom_rcv[mine, :] = parts[0]
        for some in (range(8), range(8, n)):
            for p in (0, 1):
                for to in some:
                    gather = send(red.at[p], mom_rcv.at[mine], ag_s, ag_r, at(to, p))
                    if p == 0:
                        gather.start()
                    else:
                        pl.when(me != to)(gather.start)
        landed(mom_rcv.at[pl.ds(0, 2 * rows)], ag_r)

    @pl.when(jnp.logical_not(is_host))
    def _():
        landed(mom_rcv, ag_r)

    mom_out[...] = unpack(mom_rcv[...])[:width]

    @pl.when(is_host)
    def _():
        for p in (0, 1):
            sent(rs_buf.at[p], ag_s)
            sent(rs_buf.at[p, pl.ds(0, 6 - p)], ag_s)
        sent(mom.at[pl.ds(0, 2 * rows)], rs_s)

    @pl.when(jnp.logical_not(is_host))
    def _():
        sent(mom, rs_s)

    @pl.when(q < 3)
    def _():
        sent(sym_rcv.at[pl.ds(1, 3)], ring_s)
        sent(ring.at[pl.ds(1, 3), psi], ring_s)

    @pl.when(q == 3)
    def _():
        @pl.when(digit < 3)
        def _():
            sent(ring.at[1, pl.ds(0, packed + width)], ring_s)

        @pl.when(digit == 2)
        def _():
            sent(ring.at[1, pl.ds(0, packed + width)], ring_s)

        @pl.when(digit == 3)
        def _():
            sent(sym_rcv.at[pl.ds(1, 3)], ring_s)

    @pl.when(q == 1)
    def _():
        near_sym.wait_send()
        near_psi.wait_send()

    @pl.when(q == 2)
    def _():
        top_far.wait_send()
        top_near.wait_send()


def write_out(a, b, c, a_out, b_out, c_out, sems):
    copies = [
        pltpu.make_async_copy(x, y, sems.at[i])
        for i, (x, y) in enumerate(((b, b_out), (c, c_out), (a, a_out)))
    ]
    for copy in copies:
        copy.start()
    for copy in copies:
        copy.wait()


def local16(gains, offsets, cov_terms):
    steps, width = gains.shape[0], gains.shape[1]
    slab, packed = 2 * width + PAD, width // 2 + PAD
    rows = packed // 3
    assert packed == 3 * rows and rows % PAD == 0
    dma = pltpu.SemaphoreType.DMA
    vmem = pl.BlockSpec(memory_space=pltpu.VMEM)
    shapes = ((steps, width), (steps, width, width), (width, width))
    results = pl.pallas_call(
        kernel16,
        out_shape=tuple(pltpu.VMEM(s, F32) for s in shapes),
        in_specs=[pl.BlockSpec(memory_space=pltpu.HBM)] * 3,
        out_specs=(vmem,) * 3,
        scratch_shapes=[
            pltpu.VMEM((steps, width, width), F32),
            pltpu.VMEM((steps, width), F32),
            pltpu.VMEM((steps, width, width), F32),
            pltpu.VMEM((steps, slab, width), F32),
            pltpu.VMEM((4, slab, width), F32),
            pltpu.VMEM((slab, width), F32),
            pltpu.VMEM((slab, width), F32),
            pltpu.VMEM((slab, width), F32),
            pltpu.VMEM((packed, width), F32),
            pltpu.VMEM((4, packed, width), F32),
            pltpu.VMEM((packed, width), F32),
            pltpu.VMEM((packed, width), F32),
            pltpu.VMEM((packed, width), F32),
            pltpu.VMEM((packed, width), F32),
            pltpu.VMEM((packed, width), F32),
            pltpu.VMEM((packed, width), F32),
            pltpu.VMEM((2, 10, rows, width), F32),
            pltpu.VMEM((4, rows, width), F32),
            pltpu.VMEM((2, rows, width), F32),
            pltpu.VMEM((2 * width, steps * width), BF16),
            pltpu.VMEM((width, steps * width), BF16),
            pltpu.VMEM((steps, width, 2 * width), BF16),
            pltpu.VMEM((2 * width, width), BF16),
            pltpu.VMEM((width, width), BF16),
            pltpu.VMEM((width, 2 * width), BF16),
            dma((3,)), dma, dma((4,)), dma, dma((2,)), dma, dma((2,)), dma, dma, dma, pltpu.SemaphoreType.REGULAR,
        ],
        compiler_params=pltpu.CompilerParams(collective_id=0, has_side_effects=True),
    )(gains, offsets, cov_terms)
    results = [pltpu.with_memory_space_constraint(r, pltpu.VMEM) for r in results]
    return pl.pallas_call(
        write_out,
        out_shape=tuple(jax.ShapeDtypeStruct(s, F32) for s in shapes),
        in_specs=[vmem] * 3,
        out_specs=(pl.BlockSpec(memory_space=pl.ANY),) * 3,
        scratch_shapes=[dma((3,))],
    )(*results)


def solution(mesh):
    n = mesh.shape["tm"]
    in_specs = (P(("seq", "tm"), None, None), P(("seq", "tm"), None), P(("seq", "tm"), None, None))
    out_specs = (P(("seq", "tm"), None), P(("seq", "tm"), None, None), P("seq", None))
    return jax.shard_map(
        local16 if n == 16 and mesh.shape["seq"] == 2 else functools.partial(local, n), mesh=mesh, in_specs=in_specs, out_specs=out_specs, check_vma=False
    )
```

```python
import functools

import jax
import jax.numpy as jnp
from jax import lax
from jax.experimental import pallas as pl
from jax.experimental.pallas import tpu as pltpu
from jax.sharding import PartitionSpec as P

F32 = jnp.float32
BF16 = jnp.bfloat16
PAD = 8
GROUP = 16


def split(x):
    hi = x.astype(BF16)
    return hi, (x - hi.astype(F32)).astype(BF16)


def left(x):
    hi, lo = split(x)
    return hi, jnp.concatenate([hi, lo], axis=1)


def right(w):
    hi, lo = split(w)
    return jnp.concatenate([hi, hi], axis=0), lo


def mul(x, w):
    hi, both = x
    w_hi, w_lo = w
    return jnp.dot(both, w_hi, preferred_element_type=F32) + jnp.dot(
        hi, w_lo, preferred_element_type=F32
    )


def kernel(
    n, gains, offsets, covs, means_out, covs_out, mom_out,
    own, ring, suf, z_snd, z_near, top_snd, top_rcv,
    mom, rs_buf, bf_snd, bf_rcv, red, mom_all, mean_rows,
    ring_s, ring_r, z_s, z_r, rs_s, rs_r, bf_s, bf_r, ag_s, ag_r, out_s,
):
    steps, width = gains.shape[0], gains.shape[1]
    lean = width + PAD
    me = lax.axis_index("tm")
    levels = (n.bit_length() - 1) // 2
    quarter = n // 4
    rows = width // GROUP
    place = lax.rem(me, GROUP)
    base = me - place

    def flip(step):
        return me + step * (1 - 2 * lax.rem(lax.div(me, step), 2))

    def digit_of(stride):
        return lax.rem(lax.div(me, stride), 4)

    def peer(stride, j):
        digit = digit_of(stride)
        return me + stride * (lax.rem(digit + j, 4) - digit)

    peers = [base + lax.rem(place + j, GROUP) for j in range(1, GROUP)]
    peers += [peer(4**l, j) for l in range(2, levels) for j in (1, 2, 3)]
    barrier = pltpu.get_barrier_semaphore()
    for to in peers:
        pl.semaphore_signal(barrier, inc=1, device_id={"tm": to}, device_id_type=pl.DeviceIdType.MESH)

    def send(src, dst, s, r, to):
        return pltpu.make_async_remote_copy(
            src_ref=src, dst_ref=dst, send_sem=s, recv_sem=r,
            device_id={"tm": to}, device_id_type=pl.DeviceIdType.MESH,
        )

    def compose(e, f):
        e_psi = e[lean:]
        x = mul(left(f), right(e_psi))
        p = e[:width] + mul(left(e_psi.T), right(x[:width]))
        out = [p, e[width:lean] + x[width:lean]]
        if f.shape[0] > lean:
            out.append(x[lean:])
        return jnp.concatenate(out, axis=0)

    for t in reversed(range(steps)):
        gain = gains[t]
        if t == steps - 1:
            gain = jnp.where(me == n - 1, jnp.zeros_like(gain), gain)
        offset = jnp.broadcast_to(offsets[t : t + 1, :], (PAD, width))
        element = jnp.concatenate([covs[t], offset, gain.T], axis=0)
        own[t] = element if t == steps - 1 else compose(element, own[t + 1])

    def absorb(f):
        for t in range(steps):
            own[t, : f.shape[0]] = compose(own[t], f)

    pl.semaphore_wait(barrier, len(peers))

    def deferred(l):
        digit = digit_of(4**l)

        @pl.when(digit == 0)
        def _():
            suf[...] = compose(ring[l, 1], suf[...])

        @pl.when(digit == 2)
        def _():
            suf[...] = ring[l, 3]

        @pl.when(digit < 3)
        def _():
            absorb(suf[...])

    sends = []
    total = own[0]
    for l in range(levels - 1):
        digit = digit_of(4**l)
        ring[l, digit] = total
        started = []
        for j in (2, 1, 3):
            c = send(
                ring.at[l, digit], ring.at[l, digit], ring_s.at[l, j - 1], ring_r.at[l, j - 1], peer(4**l, j)
            )
            c.start()
            started.append(c)
        if l:
            deferred(l - 1)
        for j in (1, 2, 3):
            came = lax.rem(digit + 4 - j, 4)
            send(
                ring.at[l, came], ring.at[l, came], ring_s.at[l, j - 1], ring_r.at[l, j - 1], peer(4**l, j)
            ).wait_recv()
        sends += started
        high = compose(ring[l, 2], ring[l, 3])
        total = compose(compose(ring[l, 0], ring[l, 1]), high)
        suf[...] = high
    z_snd[...] = total

    q = lax.div(me, quarter)
    down, down2 = lax.rem(me + n - quarter, n), lax.rem(me + n - 2 * quarter, n)
    part = pl.ds(0, lean)
    near_full = send(z_snd, z_near, z_s.at[0], z_r.at[0], down)
    near_lean = send(z_snd.at[part], z_near.at[part], z_s.at[0], z_r.at[0], down)
    top_far = send(top_snd, top_rcv, z_s.at[1], z_r.at[1], down2)
    top_near = send(top_snd, top_rcv, z_s.at[2], z_r.at[1], down)

    @pl.when(q == 3)
    def _():
        near_lean.start()

    @pl.when(q == 1)
    def _():
        near_full.start()

    deferred(levels - 2)

    @pl.when(q == 3)
    def _():
        near_lean.wait_send()

    @pl.when(q == 2)
    def _():
        near_lean.wait_recv()
        top_snd[...] = compose(z_snd[...], z_near[part, :])
        top_far.start()
        top_near.start()
        absorb(z_near[part, :])
        top_far.wait_send()
        top_near.wait_send()

    @pl.when(q == 0)
    def _():
        near_full.wait_recv()
        absorb(z_near[...])

    @pl.when(q < 2)
    def _():
        top_near.wait_recv()
        absorb(top_rcv[...])

    @pl.when(q == 1)
    def _():
        near_full.wait_send()

    out_copies = []
    for t in range(steps):
        out_copies.append(pltpu.make_async_copy(own.at[t, pl.ds(0, width)], covs_out.at[t], out_s.at[t]))
    means = jnp.concatenate([own[t, width : width + 1] for t in range(steps)], axis=0)
    mean_rows[...] = means
    out_copies.append(pltpu.make_async_copy(mean_rows, means_out, out_s.at[steps]))
    sums = own[0, :width]
    for t in range(1, steps):
        sums = sums + own[t, :width]
    m_hi, m_lo = split(means)
    outer = lambda u, v: lax.dot_general(u, v, (((0,), (0,)), ((), ())), preferred_element_type=F32)
    sums = sums + (outer(m_hi, m_hi) + (outer(m_hi, m_lo) + outer(m_lo, m_hi)))
    mom[...] = sums * (1.0 / (steps * n))

    def group_rows(k):
        return pl.ds(pl.multiple_of(k * rows, rows), rows)

    for j in range(1, GROUP):
        to = lax.rem(place + j, GROUP)
        c = send(mom.at[group_rows(to)], rs_buf.at[j - 1], rs_s.at[j - 1], rs_r.at[j - 1], base + to)
        c.start()
        sends.append(c)
    for c in out_copies:
        c.start()
    acc = mom[group_rows(place), :]
    for c, j in zip(sends[1 - GROUP :], range(1, GROUP)):
        c.wait_recv()
        acc = acc + rs_buf[j - 1]
    k = 0
    while GROUP << k < n:
        bf_snd[k] = acc
        c = send(bf_snd.at[k], bf_rcv.at[k], bf_s.at[k], bf_r.at[k], flip(GROUP << k))
        c.start()
        c.wait()
        acc = acc + bf_rcv[k]
        k += 1
    red[...] = acc
    gather = []
    for j in range(1, GROUP):
        to = lax.rem(place + j, GROUP)
        c = send(red, mom_all.at[group_rows(place)], ag_s.at[j - 1], ag_r.at[j - 1], base + to)
        c.start()
        gather.append(c)
    mom_all[group_rows(place), :] = acc
    for c in sends + gather:
        c.wait_send()
    for c in out_copies:
        c.wait()
    for c in gather:
        c.wait_recv()
    last = pltpu.make_async_copy(mom_all, mom_out, out_s.at[steps + 1])
    last.start()
    last.wait()


def hand_over(a, b, c, a_out, b_out, c_out, sems):
    copies = [
        pltpu.make_async_copy(x, y, sems.at[i])
        for i, (x, y) in enumerate(((b, b_out), (c, c_out), (a, a_out)))
    ]
    for copy in copies:
        copy.start()
    for copy in copies:
        copy.wait()


def local(n, gains, offsets, cov_terms):
    steps, width = gains.shape[0], gains.shape[1]
    levels = (n.bit_length() - 1) // 2
    assert n == 4**levels and levels > 1
    slab, lean, rows = 2 * width + PAD, width + PAD, width // GROUP
    far = max(1, (n // GROUP).bit_length() - 1)
    dma = pltpu.SemaphoreType.DMA
    vmem = pl.BlockSpec(memory_space=pltpu.VMEM)
    any_space = pl.BlockSpec(memory_space=pl.ANY)
    shapes = (
        jax.ShapeDtypeStruct((steps, width), F32),
        jax.ShapeDtypeStruct((steps, width, width), F32),
        jax.ShapeDtypeStruct((width, width), F32),
    )
    results = pl.pallas_call(
        functools.partial(kernel, n),
        out_shape=shapes,
        in_specs=[vmem] * 3,
        out_specs=(any_space,) * 3,
        scratch_shapes=[
            pltpu.VMEM((steps, slab, width), F32),
            pltpu.VMEM((levels - 1, 4, slab, width), F32),
            pltpu.VMEM((slab, width), F32),
            pltpu.VMEM((slab, width), F32),
            pltpu.VMEM((slab, width), F32),
            pltpu.VMEM((lean, width), F32),
            pltpu.VMEM((lean, width), F32),
            pltpu.VMEM((width, width), F32),
            pltpu.VMEM((GROUP - 1, rows, width), F32),
            pltpu.VMEM((far, rows, width), F32),
            pltpu.VMEM((far, rows, width), F32),
            pltpu.VMEM((rows, width), F32),
            pltpu.VMEM((width, width), F32),
            pltpu.VMEM((steps, width), F32),
            dma((levels - 1, 3)), dma((levels - 1, 3)),
            dma((3,)), dma((2,)),
            dma((GROUP - 1,)), dma((GROUP - 1,)),
            dma((far,)), dma((far,)),
            dma((GROUP - 1,)), dma((GROUP - 1,)),
            dma((steps + 2,)),
        ],
        compiler_params=pltpu.CompilerParams(collective_id=0, has_side_effects=True),
    )(gains, offsets, cov_terms)
    return pl.pallas_call(
        hand_over,
        out_shape=shapes,
        in_specs=[vmem] * 3,
        out_specs=(any_space,) * 3,
        scratch_shapes=[dma((3,))],
    )(*results)


def pack(s):
    half = s.shape[1] // 2
    row = lax.broadcasted_iota(jnp.int32, (half, 2 * half), 0)
    col = lax.broadcasted_iota(jnp.int32, (half, 2 * half), 1)
    low = s[half : 2 * half]
    both = jnp.where(jnp.logical_or(col >= half, row >= col), s[:half], pltpu.roll(low, half, 1))
    diag = jnp.sum(jnp.where(col - half == row, low, 0.0), axis=0, keepdims=True)
    first = lax.broadcasted_iota(jnp.int32, (PAD, 2 * half), 0) == 0
    return jnp.concatenate([both, jnp.where(first, s[2 * half :], diag)], axis=0)


def unpack(p):
    half = p.shape[1] // 2
    row = lax.broadcasted_iota(jnp.int32, (half, 2 * half), 0)
    col = lax.broadcasted_iota(jnp.int32, (half, 2 * half), 1)
    m = p[:half]
    turned = jnp.concatenate([m, m], axis=0).T
    top = jnp.where(jnp.logical_or(col >= half, row >= col), m, turned[:half])
    k = col - half
    right_low = jnp.where(row < k, pltpu.roll(m, half, 1), jnp.where(row == k, p[half + 1 : half + 2], turned[:half]))
    low = jnp.where(col < half, turned[half:], right_low)
    mean = jnp.broadcast_to(p[half : half + 1], (PAD, 2 * half))
    return jnp.concatenate([top, low, mean], axis=0)


def kernel16(
    gains_in, offsets_in, covs_in, means_out, covs_out, mom_out,
    gains, offsets, covs, own, reach, ring, acc, suf, z_near, sym_snd, sym_rcv, z_sym, z_sym_rcv, top_snd, top_rcv, mom, mom_rcv, rs_buf, pre_buf, red,
    own_right, own_low, own_both, z_right, z_low, z_both,
    in_s, ring_s, ring_r, z_s, z_r, rs_s, rs_r, pre_r, ag_s, ag_r, pace,
):
    steps, width = gains.shape[0], gains.shape[1]
    lean = width + PAD
    n = 16
    me, core = lax.axis_index("tm"), lax.axis_index("seq")
    digit, q = lax.rem(me, 4), lax.div(me, 4)
    rows = (width // 2 + PAD) // 3
    central = [4 + i for i in range(4)]
    hosts = central[:3]
    is_central = jnp.logical_and(q == 1, core == 1)
    is_host = jnp.logical_and(is_central, digit < 3)
    is_last = me == n - 1
    part, psi = pl.ds(0, lean), pl.ds(lean, width)
    packed = width // 2 + PAD
    dx, dy = 1 - 2 * lax.rem(digit, 2), 2 - 4 * lax.div(digit, 2)

    def at(tm, seq):
        return {"tm": tm, "seq": seq}

    def send(src, dst, s, r, to):
        return pltpu.make_async_remote_copy(
            src_ref=src, dst_ref=dst, send_sem=s, recv_sem=r,
            device_id=to, device_id_type=pl.DeviceIdType.MESH,
        )

    def landed(ref, sem):
        send(ref, ref, sem, sem, at(lax.rem(me + 1, n), core)).wait_recv()

    def sent(ref, sem):
        send(ref, ref, sem, sem, at(lax.rem(me + 1, n), core)).wait_send()

    barrier = pltpu.get_barrier_semaphore()

    def greet(tm, seq):
        pl.semaphore_signal(barrier, inc=1, device_id=at(tm, seq), device_id_type=pl.DeviceIdType.MESH)

    @pl.when(is_central)
    def _():
        for j in range(1, n):
            greet(lax.rem(me + j, n), core)
        for j in range(n):
            greet(j, 0)

    @pl.when(jnp.logical_not(is_central))
    def _():
        @pl.when(jnp.logical_or(q < 3, digit < 2))
        def _():
            for step in (dx, dy, dx + dy):
                greet(me + step, core)

        @pl.when(jnp.logical_and(q == 3, digit == 2))
        def _():
            greet(me + 1, core)

        for host in central:
            greet(host, 1)

        @pl.when(core == 1)
        def _():
            greet(me - digit + 2, 0)

        @pl.when(q == 0)
        def _():
            greet(8 + digit, core)

        @pl.when(q == 2)
        def _():
            greet(12 + lax.rem(digit, 2), core)

        @pl.when(jnp.logical_and(q < 2, core == 0))
        def _():
            greet(me + 4, core)

    early, late = pl.ds(0, 2), pl.ds(2, steps - 2)
    fetch = [
        pltpu.make_async_copy(gains_in.at[early], gains.at[early], in_s.at[0]),
        pltpu.make_async_copy(gains_in.at[late], gains.at[late], in_s.at[1]),
        pltpu.make_async_copy(covs_in, covs, in_s.at[2]),
        pltpu.make_async_copy(offsets_in, offsets, in_s.at[3]),
    ]
    for c in fetch:
        c.start()

    def compose(e, f):
        e_psi = e[lean:]
        x = mul(left(f), right(e_psi))
        p = e[:width] + mul(left(e_psi.T), right(x[:width]))
        out = [p, e[width:lean] + x[width:lean]]
        if f.shape[0] > lean:
            out.append(x[lean:])
        return jnp.concatenate(out, axis=0)

    def slot(d):
        return lax.rem(d + 4 - digit, 4)

    def total_of(d):
        return ring[slot(d)]

    def exchange(src, dst):
        upper, lower = jnp.logical_or(q < 3, digit >= 2), jnp.logical_or(q < 3, digit != 2)
        for step, needed in ((dx + dy, upper), (dy, upper), (dx, lower)):
            there = lax.rem(4 - step, 4)
            pl.when(needed)(send(src, dst(there), ring_s, ring_r.at[there], at(me + step, core)).start)

    def exchange_psi():
        exchange(ring.at[0, psi], lambda there: ring.at[there, psi])

    fetch[0].wait()
    ready = jnp.where(q == 0, 7, jnp.where(q == 1, 8, jnp.where(q == 2, 9 - core, jnp.where(digit < 2, 7, 4 + digit))))
    ready = ready + jnp.where(jnp.logical_and(core == 0, jnp.logical_and(digit == 2, q != 1)), 4, 0)
    ready = jnp.where(is_central, 2 * n - 1, ready)

    reach[0] = gains[0]
    run = mul(left(gains[0]), right(gains[1]))
    reach[1] = run
    fetch[1].wait()
    for t in range(2, steps - 1):
        run = mul(left(run), right(gains[t]))
        reach[t] = run

    @pl.when(is_last)
    def _():
        ring[0, psi] = jnp.zeros((width, width), F32)

    @pl.when(jnp.logical_not(is_last))
    def _():
        ring[0, psi] = mul(left(reach[steps - 2]), right(gains[steps - 1])).T

    pl.semaphore_wait(barrier, ready)

    @pl.when(jnp.logical_and(jnp.logical_not(is_last), core == 0))
    def _():
        exchange_psi()

    fetch[2].wait()
    fetch[3].wait()
    offset = [jnp.broadcast_to(offsets[t : t + 1, :], (PAD, width)) for t in range(steps)]
    cov, mean = covs[0], offset[0]
    for t in range(1, steps):
        e = reach[t - 1]
        x = mul(left(jnp.concatenate([covs[t], offset[t]], axis=0)), right(e.T))
        cov = cov + mul(left(e), right(x[:width]))
        mean = mean + x[width:]
    ring[0, part] = jnp.concatenate([cov, mean], axis=0)
    sym_snd[...] = pack(jnp.concatenate([cov, mean], axis=0))

    @pl.when(core == 0)
    def _():
        exchange(sym_snd, lambda there: sym_rcv.at[there])

        @pl.when(digit == 3)
        def _():
            pl.semaphore_signal(pace, inc=1, device_id=at(me - 1, 0), device_id_type=pl.DeviceIdType.MESH)

    own[0] = ring[0]
    run = jnp.where(is_last, jnp.zeros_like(gains[0]), gains[steps - 1])
    run = jnp.concatenate([covs[steps - 1], offset[steps - 1], run.T], axis=0)
    own[steps - 1] = run
    for t in reversed(range(1, steps - 1)):
        run = compose(jnp.concatenate([covs[t], offset[t], gains[t].T], axis=0), run)
        own[t] = run

    @pl.when(jnp.logical_and(core == 0, digit == 2))
    def _():
        pl.semaphore_wait(pace, 1)
        for j in range(4):
            pl.semaphore_signal(pace, inc=1, device_id=at(me - 2 + j, 1), device_id_type=pl.DeviceIdType.MESH)

    @pl.when(core == 1)
    def _():
        pl.semaphore_wait(pace, 1)

        @pl.when(jnp.logical_not(is_last))
        def _():
            exchange_psi()

        exchange(sym_snd, lambda there: sym_rcv.at[there])

    def prepare():
        for t in range(steps):
            e, cols = own[t, psi], pl.ds(t * width, width)
            own_right[:, cols], own_low[:, cols] = right(e)
            own_both[t] = left(e.T)[1]

    def apply(f):
        x = mul(left(f), (own_right[...], own_low[...]))
        out = []
        for t in range(steps):
            both, xt = own_both[t], x[:, t * width : (t + 1) * width]
            cov = own[t, :width] + mul((both[:, :width], both), right(xt[:width]))
            out.append((cov, own[t, width:lean] + xt[width:lean], xt[lean:]))
        return out

    def absorb(f):
        for t, (cov, mean, rest) in enumerate(apply(f)):
            own[t, :width] = cov
            own[t, width:lean] = mean
            if f.shape[0] > lean:
                own[t, psi] = rest

    def finish(found):
        means = jnp.concatenate([mean[:1] for _, mean in found], axis=0)
        sums = found[0][0]
        for cov, _ in found[1:]:
            sums = sums + cov
        m_hi, m_lo = split(means)
        outer = lambda u, v: lax.dot_general(u, v, (((0,), (0,)), ((), ())), preferred_element_type=F32)
        sums = sums + (outer(m_hi, m_hi) + (outer(m_hi, m_lo) + outer(m_lo, m_hi)))
        mom[...] = pack(jnp.concatenate([sums * (1.0 / (steps * n)), jnp.zeros((PAD, width), F32)], axis=0))
        means_out[...] = means
        for t, (cov, _) in enumerate(found):
            covs_out[t] = cov

    def block(i):
        return pl.ds(i * rows, rows)

    mine = pl.ds(pl.multiple_of(lax.rem(digit, 3) * rows, PAD), rows)

    def arrive(d):
        here = slot(d)

        @pl.when(digit != d)
        def _():
            landed(ring.at[here, pl.ds(0, packed + width)], ring_r.at[here])
            ring[here, part] = unpack(sym_rcv[here])

    def state_of(base, f, right_ref, low_ref, both):
        x = mul(left(f), (right_ref, low_ref))
        cov = base[:width] + mul((both[:, :width], both), right(x[:width]))
        return jnp.concatenate([cov, base[width:lean] + x[width:]], axis=0)

    def hold(e):
        z_right[...], z_low[...] = right(e)
        z_both[...] = left(e.T)[1]

    down, down2 = lax.rem(me + n - 4, n), lax.rem(me + n - 8, n)
    near_sym = send(z_sym, z_sym_rcv, z_s, z_r.at[0], at(down, core))
    near_psi = send(acc.at[psi], z_near.at[psi], z_s, z_r.at[0], at(down, core))
    top_far = send(top_snd, top_rcv, z_s, z_r.at[1], at(down2, core))
    top_near = send(top_snd, top_rcv, z_s, z_r.at[1], at(down, core))
    far_sym = send(z_sym, z_sym_rcv, z_s, z_r.at[0], at(lax.rem(me + n - 2, n), core))

    @pl.when(jnp.logical_and(q == 3, digit < 2))
    def _():
        arrive(0)
        arrive(1)
        acc[...] = compose(total_of(0), total_of(1))
        hold(acc[psi, :])
        arrive(2)
        e = total_of(2)[lean:]
        cols = pl.ds(0, width)
        own_right[:, cols], own_low[:, cols] = right(e)
        own_both[0] = left(e.T)[1]
        landed(sym_rcv.at[slot(3)], ring_r.at[slot(3)])
        newest = unpack(sym_rcv[slot(3)])
        state = state_of(total_of(2)[:lean], newest, own_right[:, cols], own_low[:, cols], own_both[0])
        suf[part, :] = state
        z_sym[...] = pack(state_of(acc[part, :], state, z_right[...], z_low[...], z_both[...]))
        far_sym.start()
        near_sym.start()

        @pl.when(digit == 0)
        def _():
            suf[part, :] = compose(total_of(1), suf[part, :])

    @pl.when(jnp.logical_and(q == 3, digit == 2))
    def _():
        landed(sym_rcv.at[slot(3)], ring_r.at[slot(3)])
        suf[part, :] = unpack(sym_rcv[slot(3)])

    @pl.when(q < 3)
    def _():
        arrive(3)
        acc[...] = total_of(3)
        for d in (2, 1, 0):
            @pl.when(digit == d)
            def _():
                suf[...] = acc[...]

            arrive(d)
            acc[...] = compose(total_of(d), acc[...])

    @pl.when(q == 1)
    def _():
        z_sym[...] = pack(acc[part, :])
        near_sym.start()
        near_psi.start()

    @pl.when(q == 2)
    def _():
        hold(acc[psi, :])

    prepare()

    @pl.when(digit < 3)
    def _():
        @pl.when(q == 3)
        def _():
            absorb(suf[part, :])

        @pl.when(q < 3)
        def _():
            absorb(suf[...])
            prepare()

    @pl.when(q == 2)
    def _():
        near_sym.wait_recv()
        near = unpack(z_sym_rcv[...])
        top_snd[...] = pack(state_of(acc[part, :], near, z_right[...], z_low[...], z_both[...]))
        top_far.start()
        top_near.start()
        absorb(near)

    @pl.when(q == 0)
    def _():
        landed(z_near.at[pl.ds(0, packed + width)], z_r.at[0])
        z_near[part, :] = unpack(z_sym_rcv[...])
        absorb(z_near[...])
        prepare()

    @pl.when(q < 2)
    def _():
        top_near.wait_recv()
        finish([found[:2] for found in apply(unpack(top_rcv[...]))])

        for i, host in enumerate(hosts):
            scatter = send(mom.at[block(i)], rs_buf.at[core, me], rs_s, rs_r.at[core], at(host, 1))

            @pl.when(jnp.logical_or(me != host, core == 0))
            def _():
                scatter.start()

    @pl.when(q >= 2)
    def _():
        finish([(own[t, :width], own[t, width:lean]) for t in range(steps)])

        @pl.when(jnp.logical_and(q == 3, digit < 2))
        def _():
            near_sym.wait_send()
            far_sym.wait_send()

        for step in (dx + dy, dx, dy):
            to = digit + step
            theirs = pl.ds(pl.multiple_of(lax.rem(to, 3) * rows, PAD), rows)
            part_sum = send(mom.at[theirs], pre_buf.at[lax.rem(4 - step, 4)], rs_s, pre_r, at(me + step, core))
            pl.when(to < 3)(part_sum.start)

        @pl.when(digit < 3)
        def _():
            landed(pre_buf.at[pl.ds(1, 3)], pre_r)
            pre_buf[0] = (mom[mine, :] + pre_buf[1]) + (pre_buf[2] + pre_buf[3])
            send(pre_buf.at[0], rs_buf.at[core, 6 + q], rs_s, rs_r.at[core], at(4 + digit, 1)).start()

    @pl.when(is_host)
    def _():
        rs_buf[1, me] = mom[mine, :]
        def gather(to, p):
            copy = send(red.at[p], mom_rcv.at[mine], ag_s, ag_r, at(to, p))
            if p == 0 or to not in hosts:
                copy.start()
            else:
                pl.when(me != to)(copy.start)

        for p in (0, 1):
            landed(rs_buf.at[p, pl.ds(0, 10 - p)], rs_r.at[p])
            parts = [rs_buf[p, j] for j in range(10)]
            while len(parts) > 1:
                parts = [u + v for u, v in zip(parts[::2], parts[1::2])] + parts[len(parts) & ~1 :]
            red[p] = parts[0]
            gather(0, p)
            if p == 1:
                mom_rcv[mine, :] = parts[0]
        for some in (range(1, 8), range(8, n)):
            for p in (0, 1):
                for to in some:
                    gather(to, p)
        landed(mom_rcv.at[pl.ds(0, 2 * rows)], ag_r)

    @pl.when(jnp.logical_not(is_host))
    def _():
        landed(mom_rcv, ag_r)

    mom_out[...] = unpack(mom_rcv[...])[:width]

    @pl.when(is_host)
    def _():
        for p in (0, 1):
            sent(rs_buf.at[p], ag_s)
            sent(rs_buf.at[p, pl.ds(0, 6 - p)], ag_s)
        sent(mom.at[pl.ds(0, 2 * rows)], rs_s)

    @pl.when(jnp.logical_not(is_host))
    def _():
        sent(mom, rs_s)

    @pl.when(q < 3)
    def _():
        sent(sym_rcv.at[pl.ds(1, 3)], ring_s)
        sent(ring.at[pl.ds(1, 3), psi], ring_s)

    @pl.when(q == 3)
    def _():
        @pl.when(digit < 3)
        def _():
            sent(ring.at[1, pl.ds(0, packed + width)], ring_s)

        @pl.when(digit == 2)
        def _():
            sent(ring.at[1, pl.ds(0, packed + width)], ring_s)

        @pl.when(digit == 3)
        def _():
            sent(sym_rcv.at[pl.ds(1, 3)], ring_s)

    @pl.when(q == 1)
    def _():
        near_sym.wait_send()
        near_psi.wait_send()

    @pl.when(q == 2)
    def _():
        top_far.wait_send()
        top_near.wait_send()


def write_out(a, b, c, a_out, b_out, c_out, sems):
    copies = [
        pltpu.make_async_copy(x, y, sems.at[i])
        for i, (x, y) in enumerate(((b, b_out), (c, c_out), (a, a_out)))
    ]
    for copy in copies:
        copy.start()
    for copy in copies:
        copy.wait()


def local16(gains, offsets, cov_terms):
    steps, width = gains.shape[0], gains.shape[1]
    slab, packed = 2 * width + PAD, width // 2 + PAD
    rows = packed // 3
    assert packed == 3 * rows and rows % PAD == 0
    dma = pltpu.SemaphoreType.DMA
    vmem = pl.BlockSpec(memory_space=pltpu.VMEM)
    shapes = ((steps, width), (steps, width, width), (width, width))
    results = pl.pallas_call(
        kernel16,
        out_shape=tuple(pltpu.VMEM(s, F32) for s in shapes),
        in_specs=[pl.BlockSpec(memory_space=pltpu.HBM)] * 3,
        out_specs=(vmem,) * 3,
        scratch_shapes=[
            pltpu.VMEM((steps, width, width), F32),
            pltpu.VMEM((steps, width), F32),
            pltpu.VMEM((steps, width, width), F32),
            pltpu.VMEM((steps, slab, width), F32),
            pltpu.VMEM((steps - 1, width, width), F32),
            pltpu.VMEM((4, slab, width), F32),
            pltpu.VMEM((slab, width), F32),
            pltpu.VMEM((slab, width), F32),
            pltpu.VMEM((slab, width), F32),
            pltpu.VMEM((packed, width), F32),
            pltpu.VMEM((4, packed, width), F32),
            pltpu.VMEM((packed, width), F32),
            pltpu.VMEM((packed, width), F32),
            pltpu.VMEM((packed, width), F32),
            pltpu.VMEM((packed, width), F32),
            pltpu.VMEM((packed, width), F32),
            pltpu.VMEM((packed, width), F32),
            pltpu.VMEM((2, 10, rows, width), F32),
            pltpu.VMEM((4, rows, width), F32),
            pltpu.VMEM((2, rows, width), F32),
            pltpu.VMEM((2 * width, steps * width), BF16),
            pltpu.VMEM((width, steps * width), BF16),
            pltpu.VMEM((steps, width, 2 * width), BF16),
            pltpu.VMEM((2 * width, width), BF16),
            pltpu.VMEM((width, width), BF16),
            pltpu.VMEM((width, 2 * width), BF16),
            dma((4,)), dma, dma((4,)), dma, dma((2,)), dma, dma((2,)), dma, dma, dma, pltpu.SemaphoreType.REGULAR,
        ],
        compiler_params=pltpu.CompilerParams(collective_id=0, has_side_effects=True),
    )(gains, offsets, cov_terms)
    results = [pltpu.with_memory_space_constraint(r, pltpu.VMEM) for r in results]
    return pl.pallas_call(
        write_out,
        out_shape=tuple(jax.ShapeDtypeStruct(s, F32) for s in shapes),
        in_specs=[vmem] * 3,
        out_specs=(pl.BlockSpec(memory_space=pl.ANY),) * 3,
        scratch_shapes=[dma((3,))],
    )(*results)


def solution(mesh):
    n = mesh.shape["tm"]
    in_specs = (P(("seq", "tm"), None, None), P(("seq", "tm"), None), P(("seq", "tm"), None, None))
    out_specs = (P(("seq", "tm"), None), P(("seq", "tm"), None, None), P("seq", None))
    return jax.shard_map(
        local16 if n == 16 and mesh.shape["seq"] == 2 else functools.partial(local, n), mesh=mesh, in_specs=in_specs, out_specs=out_specs, check_vma=False
    )
```

```python
import functools

import jax
import jax.numpy as jnp
from jax import lax
from jax.experimental import pallas as pl
from jax.experimental.pallas import tpu as pltpu
from jax.sharding import PartitionSpec as P

F32 = jnp.float32
BF16 = jnp.bfloat16
PAD = 8
GROUP = 16


def split(x):
    hi = x.astype(BF16)
    return hi, (x - hi.astype(F32)).astype(BF16)


def left(x):
    return jnp.concatenate(split(x), axis=1)


def right(w):
    both = jnp.concatenate(split(w), axis=1)
    return jnp.concatenate([both, both], axis=0)


def fold(x):
    half = x.shape[1] // 2
    return x[:, :half] + x[:, half:]


def mul(x, w):
    return fold(jnp.dot(x, w, preferred_element_type=F32))


def kernel(
    n, gains, offsets, covs, means_out, covs_out, mom_out,
    own, ring, suf, z_snd, z_near, top_snd, top_rcv,
    mom, rs_buf, bf_snd, bf_rcv, red, mom_all, mean_rows,
    ring_s, ring_r, z_s, z_r, rs_s, rs_r, bf_s, bf_r, ag_s, ag_r, out_s,
):
    steps, width = gains.shape[0], gains.shape[1]
    lean = width + PAD
    me = lax.axis_index("tm")
    levels = (n.bit_length() - 1) // 2
    quarter = n // 4
    rows = width // GROUP
    place = lax.rem(me, GROUP)
    base = me - place

    def flip(step):
        return me + step * (1 - 2 * lax.rem(lax.div(me, step), 2))

    def digit_of(stride):
        return lax.rem(lax.div(me, stride), 4)

    def peer(stride, j):
        digit = digit_of(stride)
        return me + stride * (lax.rem(digit + j, 4) - digit)

    peers = [base + lax.rem(place + j, GROUP) for j in range(1, GROUP)]
    peers += [peer(4**l, j) for l in range(2, levels) for j in (1, 2, 3)]
    barrier = pltpu.get_barrier_semaphore()
    for to in peers:
        pl.semaphore_signal(barrier, inc=1, device_id={"tm": to}, device_id_type=pl.DeviceIdType.MESH)

    def send(src, dst, s, r, to):
        return pltpu.make_async_remote_copy(
            src_ref=src, dst_ref=dst, send_sem=s, recv_sem=r,
            device_id={"tm": to}, device_id_type=pl.DeviceIdType.MESH,
        )

    def compose(e, f):
        e_psi = e[lean:]
        x = mul(left(f), right(e_psi))
        p = e[:width] + mul(left(e_psi.T), right(x[:width]))
        out = [p, e[width:lean] + x[width:lean]]
        if f.shape[0] > lean:
            out.append(x[lean:])
        return jnp.concatenate(out, axis=0)

    for t in reversed(range(steps)):
        gain = gains[t]
        if t == steps - 1:
            gain = jnp.where(me == n - 1, jnp.zeros_like(gain), gain)
        offset = jnp.broadcast_to(offsets[t : t + 1, :], (PAD, width))
        element = jnp.concatenate([covs[t], offset, gain.T], axis=0)
        own[t] = element if t == steps - 1 else compose(element, own[t + 1])

    def absorb(f):
        for t in range(steps):
            own[t, : f.shape[0]] = compose(own[t], f)

    pl.semaphore_wait(barrier, len(peers))

    def deferred(l):
        digit = digit_of(4**l)

        @pl.when(digit == 0)
        def _():
            suf[...] = compose(ring[l, 1], suf[...])

        @pl.when(digit == 2)
        def _():
            suf[...] = ring[l, 3]

        @pl.when(digit < 3)
        def _():
            absorb(suf[...])

    sends = []
    total = own[0]
    for l in range(levels - 1):
        digit = digit_of(4**l)
        ring[l, digit] = total
        started = []
        for j in (2, 1, 3):
            c = send(
                ring.at[l, digit], ring.at[l, digit], ring_s.at[l, j - 1], ring_r.at[l, j - 1], peer(4**l, j)
            )
            c.start()
            started.append(c)
        if l:
            deferred(l - 1)
        for j in (1, 2, 3):
            came = lax.rem(digit + 4 - j, 4)
            send(
                ring.at[l, came], ring.at[l, came], ring_s.at[l, j - 1], ring_r.at[l, j - 1], peer(4**l, j)
            ).wait_recv()
        sends += started
        high = compose(ring[l, 2], ring[l, 3])
        total = compose(compose(ring[l, 0], ring[l, 1]), high)
        suf[...] = high
    z_snd[...] = total

    q = lax.div(me, quarter)
    down, down2 = lax.rem(me + n - quarter, n), lax.rem(me + n - 2 * quarter, n)
    part = pl.ds(0, lean)
    near_full = send(z_snd, z_near, z_s.at[0], z_r.at[0], down)
    near_lean = send(z_snd.at[part], z_near.at[part], z_s.at[0], z_r.at[0], down)
    top_far = send(top_snd, top_rcv, z_s.at[1], z_r.at[1], down2)
    top_near = send(top_snd, top_rcv, z_s.at[2], z_r.at[1], down)

    @pl.when(q == 3)
    def _():
        near_lean.start()

    @pl.when(q == 1)
    def _():
        near_full.start()

    deferred(levels - 2)

    @pl.when(q == 3)
    def _():
        near_lean.wait_send()

    @pl.when(q == 2)
    def _():
        near_lean.wait_recv()
        top_snd[...] = compose(z_snd[...], z_near[part, :])
        top_far.start()
        top_near.start()
        absorb(z_near[part, :])
        top_far.wait_send()
        top_near.wait_send()

    @pl.when(q == 0)
    def _():
        near_full.wait_recv()
        absorb(z_near[...])

    @pl.when(q < 2)
    def _():
        top_near.wait_recv()
        absorb(top_rcv[...])

    @pl.when(q == 1)
    def _():
        near_full.wait_send()

    out_copies = []
    for t in range(steps):
        out_copies.append(pltpu.make_async_copy(own.at[t, pl.ds(0, width)], covs_out.at[t], out_s.at[t]))
    means = jnp.concatenate([own[t, width : width + 1] for t in range(steps)], axis=0)
    mean_rows[...] = means
    out_copies.append(pltpu.make_async_copy(mean_rows, means_out, out_s.at[steps]))
    sums = own[0, :width]
    for t in range(1, steps):
        sums = sums + own[t, :width]
    m_hi, m_lo = split(means)
    outer = lambda u, v: lax.dot_general(u, v, (((0,), (0,)), ((), ())), preferred_element_type=F32)
    sums = sums + (outer(m_hi, m_hi) + (outer(m_hi, m_lo) + outer(m_lo, m_hi)))
    mom[...] = sums * (1.0 / (steps * n))

    def group_rows(k):
        return pl.ds(pl.multiple_of(k * rows, rows), rows)

    for j in range(1, GROUP):
        to = lax.rem(place + j, GROUP)
        c = send(mom.at[group_rows(to)], rs_buf.at[j - 1], rs_s.at[j - 1], rs_r.at[j - 1], base + to)
        c.start()
        sends.append(c)
    for c in out_copies:
        c.start()
    acc = mom[group_rows(place), :]
    for c, j in zip(sends[1 - GROUP :], range(1, GROUP)):
        c.wait_recv()
        acc = acc + rs_buf[j - 1]
    k = 0
    while GROUP << k < n:
        bf_snd[k] = acc
        c = send(bf_snd.at[k], bf_rcv.at[k], bf_s.at[k], bf_r.at[k], flip(GROUP << k))
        c.start()
        c.wait()
        acc = acc + bf_rcv[k]
        k += 1
    red[...] = acc
    gather = []
    for j in range(1, GROUP):
        to = lax.rem(place + j, GROUP)
        c = send(red, mom_all.at[group_rows(place)], ag_s.at[j - 1], ag_r.at[j - 1], base + to)
        c.start()
        gather.append(c)
    mom_all[group_rows(place), :] = acc
    for c in sends + gather:
        c.wait_send()
    for c in out_copies:
        c.wait()
    for c in gather:
        c.wait_recv()
    last = pltpu.make_async_copy(mom_all, mom_out, out_s.at[steps + 1])
    last.start()
    last.wait()


def hand_over(a, b, c, a_out, b_out, c_out, sems):
    copies = [
        pltpu.make_async_copy(x, y, sems.at[i])
        for i, (x, y) in enumerate(((b, b_out), (c, c_out), (a, a_out)))
    ]
    for copy in copies:
        copy.start()
    for copy in copies:
        copy.wait()


def local(n, gains, offsets, cov_terms):
    steps, width = gains.shape[0], gains.shape[1]
    levels = (n.bit_length() - 1) // 2
    assert n == 4**levels and levels > 1
    slab, lean, rows = 2 * width + PAD, width + PAD, width // GROUP
    far = max(1, (n // GROUP).bit_length() - 1)
    dma = pltpu.SemaphoreType.DMA
    vmem = pl.BlockSpec(memory_space=pltpu.VMEM)
    any_space = pl.BlockSpec(memory_space=pl.ANY)
    shapes = (
        jax.ShapeDtypeStruct((steps, width), F32),
        jax.ShapeDtypeStruct((steps, width, width), F32),
        jax.ShapeDtypeStruct((width, width), F32),
    )
    results = pl.pallas_call(
        functools.partial(kernel, n),
        out_shape=shapes,
        in_specs=[vmem] * 3,
        out_specs=(any_space,) * 3,
        scratch_shapes=[
            pltpu.VMEM((steps, slab, width), F32),
            pltpu.VMEM((levels - 1, 4, slab, width), F32),
            pltpu.VMEM((slab, width), F32),
            pltpu.VMEM((slab, width), F32),
            pltpu.VMEM((slab, width), F32),
            pltpu.VMEM((lean, width), F32),
            pltpu.VMEM((lean, width), F32),
            pltpu.VMEM((width, width), F32),
            pltpu.VMEM((GROUP - 1, rows, width), F32),
            pltpu.VMEM((far, rows, width), F32),
            pltpu.VMEM((far, rows, width), F32),
            pltpu.VMEM((rows, width), F32),
            pltpu.VMEM((width, width), F32),
            pltpu.VMEM((steps, width), F32),
            dma((levels - 1, 3)), dma((levels - 1, 3)),
            dma((3,)), dma((2,)),
            dma((GROUP - 1,)), dma((GROUP - 1,)),
            dma((far,)), dma((far,)),
            dma((GROUP - 1,)), dma((GROUP - 1,)),
            dma((steps + 2,)),
        ],
        compiler_params=pltpu.CompilerParams(collective_id=0, has_side_effects=True),
    )(gains, offsets, cov_terms)
    return pl.pallas_call(
        hand_over,
        out_shape=shapes,
        in_specs=[vmem] * 3,
        out_specs=(any_space,) * 3,
        scratch_shapes=[dma((3,))],
    )(*results)


def pack(s):
    half = s.shape[1] // 2
    row = lax.broadcasted_iota(jnp.int32, (half, 2 * half), 0)
    col = lax.broadcasted_iota(jnp.int32, (half, 2 * half), 1)
    low = s[half : 2 * half]
    both = jnp.where(jnp.logical_or(col >= half, row >= col), s[:half], pltpu.roll(low, half, 1))
    diag = jnp.sum(jnp.where(col - half == row, low, 0.0), axis=0, keepdims=True)
    first = lax.broadcasted_iota(jnp.int32, (PAD, 2 * half), 0) == 0
    return jnp.concatenate([both, jnp.where(first, s[2 * half :], diag)], axis=0)


def unpack(p):
    half = p.shape[1] // 2
    row = lax.broadcasted_iota(jnp.int32, (half, 2 * half), 0)
    col = lax.broadcasted_iota(jnp.int32, (half, 2 * half), 1)
    m = p[:half]
    turned = jnp.concatenate([m, m], axis=0).T
    top = jnp.where(jnp.logical_or(col >= half, row >= col), m, turned[:half])
    k = col - half
    right_low = jnp.where(row < k, pltpu.roll(m, half, 1), jnp.where(row == k, p[half + 1 : half + 2], turned[:half]))
    low = jnp.where(col < half, turned[half:], right_low)
    mean = jnp.broadcast_to(p[half : half + 1], (PAD, 2 * half))
    return jnp.concatenate([top, low, mean], axis=0)


def kernel16(
    gains_in, offsets_in, covs_in, means_out, covs_out, mom_out,
    gains, offsets, covs, own, reach, ring, acc, suf, z_near, sym_snd, sym_rcv, z_sym, z_sym_rcv, top_snd, top_rcv, mom, mom_rcv, rs_buf, pre_buf, red,
    own_right, own_both, z_right, z_both,
    in_s, ring_s, ring_r, z_s, z_r, rs_s, rs_r, pre_r, ag_s, ag_r, pace,
):
    steps, width = gains.shape[0], gains.shape[1]
    lean = width + PAD
    n = 16
    me, core = lax.axis_index("tm"), lax.axis_index("seq")
    digit, q = lax.rem(me, 4), lax.div(me, 4)
    rows = (width // 2 + PAD) // 3
    central = [4 + i for i in range(4)]
    hosts = [(4, 0), (5, 1), (6, 2), (1, 1), (2, 2)]
    is_central = jnp.logical_and(q == 1, core == 1)
    is_wide = jnp.logical_and(is_central, digit < 3)
    is_near = jnp.logical_and(core == 1, jnp.logical_or(me == 1, me == 2))
    is_host = jnp.logical_or(is_wide, is_near)
    is_last = me == n - 1
    part, psi = pl.ds(0, lean), pl.ds(lean, width)
    packed = width // 2 + PAD
    dx, dy = 1 - 2 * lax.rem(digit, 2), 2 - 4 * lax.div(digit, 2)

    def at(tm, seq):
        return {"tm": tm, "seq": seq}

    def send(src, dst, s, r, to):
        return pltpu.make_async_remote_copy(
            src_ref=src, dst_ref=dst, send_sem=s, recv_sem=r,
            device_id=to, device_id_type=pl.DeviceIdType.MESH,
        )

    def landed(ref, sem):
        send(ref, ref, sem, sem, at(lax.rem(me + 1, n), core)).wait_recv()

    def sent(ref, sem):
        send(ref, ref, sem, sem, at(lax.rem(me + 1, n), core)).wait_send()

    barrier = pltpu.get_barrier_semaphore()

    def greet(tm, seq):
        pl.semaphore_signal(barrier, inc=1, device_id=at(tm, seq), device_id_type=pl.DeviceIdType.MESH)

    @pl.when(is_central)
    def _():
        for j in range(1, n):
            greet(lax.rem(me + j, n), core)
        for j in range(n):
            greet(j, 0)

    @pl.when(jnp.logical_not(is_central))
    def _():
        @pl.when(jnp.logical_or(q < 3, digit < 2))
        def _():
            for step in (dx, dy, dx + dy):
                greet(me + step, core)

        @pl.when(jnp.logical_and(q == 3, digit == 2))
        def _():
            greet(me + 1, core)

        for host in central:
            greet(host, 1)

        @pl.when(core == 1)
        def _():
            greet(me - digit + 2, 0)

        @pl.when(q == 0)
        def _():
            greet(8 + digit, core)

        @pl.when(is_near)
        def _():
            for j in range(8):
                greet(j, 0)
            for j in range(1, 4):
                greet(lax.rem(me + j, 4), 1)
            for seq in (0, 1):
                greet(8 + me, seq)
                greet(12 + me, seq)

        @pl.when(q == 2)
        def _():
            greet(12 + lax.rem(digit, 2), core)

        @pl.when(jnp.logical_and(q < 2, core == 0))
        def _():
            greet(me + 4, core)

    early, late = pl.ds(0, 2), pl.ds(2, steps - 2)
    fetch = [
        pltpu.make_async_copy(gains_in.at[early], gains.at[early], in_s.at[0]),
        pltpu.make_async_copy(gains_in.at[late], gains.at[late], in_s.at[1]),
        pltpu.make_async_copy(covs_in, covs, in_s.at[2]),
        pltpu.make_async_copy(offsets_in, offsets, in_s.at[3]),
    ]
    for c in fetch:
        c.start()

    def compose(e, f):
        e_psi = e[lean:]
        x = mul(left(f), right(e_psi))
        p = e[:width] + mul(left(e_psi.T), right(x[:width]))
        out = [p, e[width:lean] + x[width:lean]]
        if f.shape[0] > lean:
            out.append(x[lean:])
        return jnp.concatenate(out, axis=0)

    def slot(d):
        return lax.rem(d + 4 - digit, 4)

    def total_of(d):
        return ring[slot(d)]

    def exchange(src, dst):
        upper, lower = jnp.logical_or(q < 3, digit >= 2), jnp.logical_or(q < 3, digit != 2)
        for step, needed in ((dx + dy, upper), (dy, upper), (dx, lower)):
            there = lax.rem(4 - step, 4)
            pl.when(needed)(send(src, dst(there), ring_s, ring_r.at[there], at(me + step, core)).start)

    def exchange_psi():
        exchange(ring.at[0, psi], lambda there: ring.at[there, psi])

    fetch[0].wait()
    ready = jnp.where(q == 0, 7, jnp.where(q == 1, 8, jnp.where(q == 2, 9 - core, jnp.where(digit < 2, 7, 4 + digit))))
    ready = ready + jnp.where(jnp.logical_and(core == 0, jnp.logical_and(digit == 2, q != 1)), 4, 0)
    ready = ready + jnp.where(q < 2, 2, jnp.where(lax.rem(digit, 3) == 0, 0, 1)) - jnp.where(is_near, 1, 0)
    ready = jnp.where(is_central, 2 * n - 1, ready)

    reach[0] = gains[0]
    run = mul(left(gains[0]), right(gains[1]))
    reach[1] = run
    fetch[1].wait()
    for t in range(2, steps - 1):
        run = mul(left(run), right(gains[t]))
        reach[t] = run

    @pl.when(is_last)
    def _():
        ring[0, psi] = jnp.zeros((width, width), F32)

    @pl.when(jnp.logical_not(is_last))
    def _():
        ring[0, psi] = mul(left(reach[steps - 2]), right(gains[steps - 1])).T

    pl.semaphore_wait(barrier, ready)

    @pl.when(jnp.logical_and(jnp.logical_not(is_last), core == 0))
    def _():
        exchange_psi()

    fetch[2].wait()
    fetch[3].wait()
    offset = [jnp.broadcast_to(offsets[t : t + 1, :], (PAD, width)) for t in range(steps)]
    cov, mean = covs[0], offset[0]
    for t in range(1, steps):
        e = reach[t - 1]
        x = mul(left(jnp.concatenate([covs[t], offset[t]], axis=0)), right(e.T))
        cov = cov + mul(left(e), right(x[:width]))
        mean = mean + x[width:]
    ring[0, part] = jnp.concatenate([cov, mean], axis=0)
    sym_snd[...] = pack(jnp.concatenate([cov, mean], axis=0))

    @pl.when(jnp.logical_or(core == 0, is_last))
    def _():
        exchange(sym_snd, lambda there: sym_rcv.at[there])

        @pl.when(jnp.logical_and(core == 0, digit == 3))
        def _():
            pl.semaphore_signal(pace, inc=1, device_id=at(me - 1, 0), device_id_type=pl.DeviceIdType.MESH)

    own[0] = ring[0]
    run = jnp.where(is_last, jnp.zeros_like(gains[0]), gains[steps - 1])
    run = jnp.concatenate([covs[steps - 1], offset[steps - 1], run.T], axis=0)
    own[steps - 1] = run
    for t in reversed(range(1, steps - 1)):
        run = compose(jnp.concatenate([covs[t], offset[t], gains[t].T], axis=0), run)
        own[t] = run

    @pl.when(jnp.logical_and(core == 0, digit == 2))
    def _():
        pl.semaphore_wait(pace, 1)
        for j in range(4):
            pl.semaphore_signal(pace, inc=1, device_id=at(me - 2 + j, 1), device_id_type=pl.DeviceIdType.MESH)

    @pl.when(core == 1)
    def _():
        pl.semaphore_wait(pace, 1)

        @pl.when(jnp.logical_not(is_last))
        def _():
            exchange_psi()
            exchange(sym_snd, lambda there: sym_rcv.at[there])

    def prepare():
        for t in range(steps):
            e = own[t, psi]
            own_right[:, pl.ds(2 * t * width, 2 * width)] = right(e)
            own_both[t] = left(e.T)

    def apply(f):
        x = jnp.dot(left(f), own_right[...], preferred_element_type=F32)
        out = []
        for t in range(steps):
            xt = fold(x[:, 2 * t * width : 2 * (t + 1) * width])
            cov = own[t, :width] + mul(own_both[t], right(xt[:width]))
            out.append((cov, own[t, width:lean] + xt[width:lean], xt[lean:]))
        return out

    def absorb(f):
        for t, (cov, mean, rest) in enumerate(apply(f)):
            own[t, :width] = cov
            own[t, width:lean] = mean
            if f.shape[0] > lean:
                own[t, psi] = rest

    def finish(found):
        means = jnp.concatenate([mean[:1] for _, mean in found], axis=0)
        sums = found[0][0]
        for cov, _ in found[1:]:
            sums = sums + cov
        m_hi, m_lo = split(means)
        outer = lambda u, v: lax.dot_general(u, v, (((0,), (0,)), ((), ())), preferred_element_type=F32)
        sums = sums + (outer(m_hi, m_hi) + (outer(m_hi, m_lo) + outer(m_lo, m_hi)))
        mom[...] = pack(jnp.concatenate([sums * (1.0 / (steps * n)), jnp.zeros((PAD, width), F32)], axis=0))
        means_out[...] = means
        for t, (cov, _) in enumerate(found):
            covs_out[t] = cov

    def block(i):
        return pl.ds(i * rows, rows)

    mine = pl.ds(pl.multiple_of(lax.rem(digit, 3) * rows, PAD), rows)

    def arrive(d):
        here = slot(d)

        @pl.when(digit != d)
        def _():
            landed(ring.at[here, pl.ds(0, packed + width)], ring_r.at[here])
            ring[here, part] = unpack(sym_rcv[here])

    def state_of(base, f, after, before):
        x = mul(left(f), after)
        cov = base[:width] + mul(before, right(x[:width]))
        return jnp.concatenate([cov, base[width:lean] + x[width:]], axis=0)

    def hold(e):
        z_right[...] = right(e)
        z_both[...] = left(e.T)

    down, down2 = lax.rem(me + n - 4, n), lax.rem(me + n - 8, n)
    near_sym = send(z_sym, z_sym_rcv, z_s, z_r.at[0], at(down, core))
    near_psi = send(acc.at[psi], z_near.at[psi], z_s, z_r.at[0], at(down, core))
    top_far = send(top_snd, top_rcv, z_s, z_r.at[1], at(down2, core))
    top_near = send(top_snd, top_rcv, z_s, z_r.at[1], at(down, core))
    far_sym = send(z_sym, z_sym_rcv, z_s, z_r.at[0], at(lax.rem(me + n - 2, n), core))

    @pl.when(jnp.logical_and(q == 3, digit < 2))
    def _():
        arrive(0)
        arrive(1)
        acc[...] = compose(total_of(0), total_of(1))
        hold(acc[psi, :])
        arrive(2)
        e = total_of(2)[lean:]
        own_right[:, pl.ds(0, 2 * width)] = right(e)
        own_both[0] = left(e.T)
        landed(sym_rcv.at[slot(3)], ring_r.at[slot(3)])
        newest = unpack(sym_rcv[slot(3)])
        state = state_of(total_of(2)[:lean], newest, own_right[:, pl.ds(0, 2 * width)], own_both[0])
        suf[part, :] = state
        z_sym[...] = pack(state_of(acc[part, :], state, z_right[...], z_both[...]))
        far_sym.start()
        near_sym.start()

        @pl.when(digit == 0)
        def _():
            suf[part, :] = compose(total_of(1), suf[part, :])

    @pl.when(jnp.logical_and(q == 3, digit == 2))
    def _():
        landed(sym_rcv.at[slot(3)], ring_r.at[slot(3)])
        suf[part, :] = unpack(sym_rcv[slot(3)])

    @pl.when(q < 3)
    def _():
        arrive(3)
        acc[...] = total_of(3)
        for d in (2, 1, 0):
            @pl.when(digit == d)
            def _():
                suf[...] = acc[...]

            arrive(d)
            acc[...] = compose(total_of(d), acc[...])

    @pl.when(q == 1)
    def _():
        z_sym[...] = pack(acc[part, :])
        near_sym.start()
        near_psi.start()

    @pl.when(q == 2)
    def _():
        hold(acc[psi, :])

    prepare()

    @pl.when(digit < 3)
    def _():
        @pl.when(q == 3)
        def _():
            absorb(suf[part, :])

        @pl.when(q < 3)
        def _():
            absorb(suf[...])
            prepare()

    @pl.when(q == 2)
    def _():
        near_sym.wait_recv()
        near = unpack(z_sym_rcv[...])
        top_snd[...] = pack(state_of(acc[part, :], near, z_right[...], z_both[...]))
        top_far.start()
        top_near.start()
        absorb(near)

    @pl.when(q == 0)
    def _():
        landed(z_near.at[pl.ds(0, packed + width)], z_r.at[0])
        z_near[part, :] = unpack(z_sym_rcv[...])
        absorb(z_near[...])
        prepare()

    @pl.when(q < 2)
    def _():
        top_near.wait_recv()
        finish([found[:2] for found in apply(unpack(top_rcv[...]))])

        for host, i in hosts:
            scatter = send(mom.at[block(i)], rs_buf.at[core, me], rs_s, rs_r.at[core], at(host, 1))

            @pl.when(jnp.logical_or(me != host, core == 0))
            def _():
                scatter.start()

    @pl.when(q >= 2)
    def _():
        finish([(own[t, :width], own[t, width:lean]) for t in range(steps)])

        @pl.when(jnp.logical_and(q == 3, digit < 2))
        def _():
            near_sym.wait_send()
            far_sym.wait_send()

        for step in (dx + dy, dx, dy):
            to = digit + step
            theirs = pl.ds(pl.multiple_of(lax.rem(to, 3) * rows, PAD), rows)
            part_sum = send(mom.at[theirs], pre_buf.at[lax.rem(4 - step, 4)], rs_s, pre_r, at(me + step, core))
            pl.when(to < 3)(part_sum.start)

        @pl.when(digit < 3)
        def _():
            landed(pre_buf.at[pl.ds(1, 3)], pre_r)
            pre_buf[0] = (mom[mine, :] + pre_buf[1]) + (pre_buf[2] + pre_buf[3])
            for to, wanted in ((digit, digit > 0), (4 + digit, digit < 3)):
                upward = send(pre_buf.at[0], rs_buf.at[core, 6 + q], rs_s, rs_r.at[core], at(to, 1))
                pl.when(wanted)(upward.start)

    @pl.when(is_host)
    def _():
        rs_buf[1, me] = mom[mine, :]
        def gather(to, p):
            copy = send(red.at[p], mom_rcv.at[mine], ag_s, ag_r, at(to, p))
            if to == 0:
                pl.when(me < 5)(copy.start)
            elif p == 0 or to not in (4, 5, 6):
                copy.start()
            else:
                pl.when(me != to)(copy.start)

        for p in (0, 1):
            landed(rs_buf.at[p, pl.ds(0, 10 - p)], rs_r.at[p])
            parts = [rs_buf[p, j] for j in range(10)]
            while len(parts) > 1:
                parts = [u + v for u, v in zip(parts[::2], parts[1::2])] + parts[len(parts) & ~1 :]
            red[p] = parts[0]
            gather(0, p)
            if p == 1:
                @pl.when(is_wide)
                def _():
                    mom_rcv[mine, :] = parts[0]

        @pl.when(is_wide)
        def _():
            for some in (range(1, 8), range(8, n)):
                for p in (0, 1):
                    for to in some:
                        gather(to, p)

    @pl.when(is_wide)
    def _():
        landed(mom_rcv.at[pl.ds(0, 2 * rows)], ag_r)

    @pl.when(jnp.logical_not(is_wide))
    def _():
        landed(mom_rcv, ag_r)

    mom_out[...] = unpack(mom_rcv[...])[:width]

    def sent_blocks(count, sem):
        while count:
            some = min(count, 10)
            sent(rs_buf.at[0, pl.ds(0, some)], sem)
            count -= some

    @pl.when(is_near)
    def _():
        sent_blocks(2, ag_s)

    @pl.when(is_wide)
    def _():
        sent_blocks(29, ag_s)

        @pl.when(me == 4)
        def _():
            sent_blocks(2, ag_s)

    sent_blocks(3, rs_s)

    @pl.when(jnp.where(q < 2, 1, lax.rem(digit, 3)) > 0)
    def _():
        sent_blocks(1, rs_s)

    @pl.when(jnp.logical_and(q < 2, jnp.logical_not(is_host)))
    def _():
        sent_blocks(1, rs_s)

    @pl.when(q < 3)
    def _():
        sent(sym_rcv.at[pl.ds(1, 3)], ring_s)
        sent(ring.at[pl.ds(1, 3), psi], ring_s)

    @pl.when(q == 3)
    def _():
        @pl.when(digit < 3)
        def _():
            sent(ring.at[1, pl.ds(0, packed + width)], ring_s)

        @pl.when(digit == 2)
        def _():
            sent(ring.at[1, pl.ds(0, packed + width)], ring_s)

        @pl.when(digit == 3)
        def _():
            sent(sym_rcv.at[pl.ds(1, 3)], ring_s)

    @pl.when(q == 1)
    def _():
        near_sym.wait_send()
        near_psi.wait_send()

    @pl.when(q == 2)
    def _():
        top_far.wait_send()
        top_near.wait_send()


def write_out(a, b, c, a_out, b_out, c_out, sems):
    copies = [
        pltpu.make_async_copy(x, y, sems.at[i])
        for i, (x, y) in enumerate(((b, b_out), (c, c_out), (a, a_out)))
    ]
    for copy in copies:
        copy.start()
    for copy in copies:
        copy.wait()


def local16(gains, offsets, cov_terms):
    steps, width = gains.shape[0], gains.shape[1]
    slab, packed = 2 * width + PAD, width // 2 + PAD
    rows = packed // 3
    assert packed == 3 * rows and rows % PAD == 0
    dma = pltpu.SemaphoreType.DMA
    vmem = pl.BlockSpec(memory_space=pltpu.VMEM)
    shapes = ((steps, width), (steps, width, width), (width, width))
    results = pl.pallas_call(
        kernel16,
        out_shape=tuple(pltpu.VMEM(s, F32) for s in shapes),
        in_specs=[pl.BlockSpec(memory_space=pltpu.HBM)] * 3,
        out_specs=(vmem,) * 3,
        scratch_shapes=[
            pltpu.VMEM((steps, width, width), F32),
            pltpu.VMEM((steps, width), F32),
            pltpu.VMEM((steps, width, width), F32),
            pltpu.VMEM((steps, slab, width), F32),
            pltpu.VMEM((steps - 1, width, width), F32),
            pltpu.VMEM((4, slab, width), F32),
            pltpu.VMEM((slab, width), F32),
            pltpu.VMEM((slab, width), F32),
            pltpu.VMEM((slab, width), F32),
            pltpu.VMEM((packed, width), F32),
            pltpu.VMEM((4, packed, width), F32),
            pltpu.VMEM((packed, width), F32),
            pltpu.VMEM((packed, width), F32),
            pltpu.VMEM((packed, width), F32),
            pltpu.VMEM((packed, width), F32),
            pltpu.VMEM((packed, width), F32),
            pltpu.VMEM((packed, width), F32),
            pltpu.VMEM((2, 10, rows, width), F32),
            pltpu.VMEM((4, rows, width), F32),
            pltpu.VMEM((2, rows, width), F32),
            pltpu.VMEM((2 * width, 2 * steps * width), BF16),
            pltpu.VMEM((steps, width, 2 * width), BF16),
            pltpu.VMEM((2 * width, 2 * width), BF16),
            pltpu.VMEM((width, 2 * width), BF16),
            dma((4,)), dma, dma((4,)), dma, dma((2,)), dma, dma((2,)), dma, dma, dma, pltpu.SemaphoreType.REGULAR,
        ],
        compiler_params=pltpu.CompilerParams(collective_id=0, has_side_effects=True),
    )(gains, offsets, cov_terms)
    results = [pltpu.with_memory_space_constraint(r, pltpu.VMEM) for r in results]
    return pl.pallas_call(
        write_out,
        out_shape=tuple(jax.ShapeDtypeStruct(s, F32) for s in shapes),
        in_specs=[vmem] * 3,
        out_specs=(pl.BlockSpec(memory_space=pl.ANY),) * 3,
        scratch_shapes=[dma((3,))],
    )(*results)


def solution(mesh):
    n = mesh.shape["tm"]
    in_specs = (P(("seq", "tm"), None, None), P(("seq", "tm"), None), P(("seq", "tm"), None, None))
    out_specs = (P(("seq", "tm"), None), P(("seq", "tm"), None, None), P("seq", None))
    return jax.shard_map(
        local16 if n == 16 and mesh.shape["seq"] == 2 else functools.partial(local, n), mesh=mesh, in_specs=in_specs, out_specs=out_specs, check_vma=False
    )
```

```python
import functools

import jax
import jax.numpy as jnp
from jax import lax
from jax.experimental import pallas as pl
from jax.experimental.pallas import tpu as pltpu
from jax.sharding import PartitionSpec as P

F32 = jnp.float32
BF16 = jnp.bfloat16
PAD = 8
GROUP = 16


def split(x):
    hi = x.astype(BF16)
    return hi, (x - hi.astype(F32)).astype(BF16)


def left(x):
    return jnp.concatenate(split(x), axis=1)


def right(w):
    both = jnp.concatenate(split(w), axis=1)
    return jnp.concatenate([both, both], axis=0)


def fold(x):
    half = x.shape[1] // 2
    return x[:, :half] + x[:, half:]


def mul(x, w):
    return fold(jnp.dot(x, w, preferred_element_type=F32))


def kernel(
    n, gains, offsets, covs, means_out, covs_out, mom_out,
    own, ring, suf, z_snd, z_near, top_snd, top_rcv,
    mom, rs_buf, bf_snd, bf_rcv, red, mom_all, mean_rows,
    ring_s, ring_r, z_s, z_r, rs_s, rs_r, bf_s, bf_r, ag_s, ag_r, out_s,
):
    steps, width = gains.shape[0], gains.shape[1]
    lean = width + PAD
    me = lax.axis_index("tm")
    levels = (n.bit_length() - 1) // 2
    quarter = n // 4
    rows = width // GROUP
    place = lax.rem(me, GROUP)
    base = me - place

    def flip(step):
        return me + step * (1 - 2 * lax.rem(lax.div(me, step), 2))

    def digit_of(stride):
        return lax.rem(lax.div(me, stride), 4)

    def peer(stride, j):
        digit = digit_of(stride)
        return me + stride * (lax.rem(digit + j, 4) - digit)

    peers = [base + lax.rem(place + j, GROUP) for j in range(1, GROUP)]
    peers += [peer(4**l, j) for l in range(2, levels) for j in (1, 2, 3)]
    barrier = pltpu.get_barrier_semaphore()
    for to in peers:
        pl.semaphore_signal(barrier, inc=1, device_id={"tm": to}, device_id_type=pl.DeviceIdType.MESH)

    def send(src, dst, s, r, to):
        return pltpu.make_async_remote_copy(
            src_ref=src, dst_ref=dst, send_sem=s, recv_sem=r,
            device_id={"tm": to}, device_id_type=pl.DeviceIdType.MESH,
        )

    def compose(e, f):
        e_psi = e[lean:]
        x = mul(left(f), right(e_psi))
        p = e[:width] + mul(left(e_psi.T), right(x[:width]))
        out = [p, e[width:lean] + x[width:lean]]
        if f.shape[0] > lean:
            out.append(x[lean:])
        return jnp.concatenate(out, axis=0)

    for t in reversed(range(steps)):
        gain = gains[t]
        if t == steps - 1:
            gain = jnp.where(me == n - 1, jnp.zeros_like(gain), gain)
        offset = jnp.broadcast_to(offsets[t : t + 1, :], (PAD, width))
        element = jnp.concatenate([covs[t], offset, gain.T], axis=0)
        own[t] = element if t == steps - 1 else compose(element, own[t + 1])

    def absorb(f):
        for t in range(steps):
            own[t, : f.shape[0]] = compose(own[t], f)

    pl.semaphore_wait(barrier, len(peers))

    def deferred(l):
        digit = digit_of(4**l)

        @pl.when(digit == 0)
        def _():
            suf[...] = compose(ring[l, 1], suf[...])

        @pl.when(digit == 2)
        def _():
            suf[...] = ring[l, 3]

        @pl.when(digit < 3)
        def _():
            absorb(suf[...])

    sends = []
    total = own[0]
    for l in range(levels - 1):
        digit = digit_of(4**l)
        ring[l, digit] = total
        started = []
        for j in (2, 1, 3):
            c = send(
                ring.at[l, digit], ring.at[l, digit], ring_s.at[l, j - 1], ring_r.at[l, j - 1], peer(4**l, j)
            )
            c.start()
            started.append(c)
        if l:
            deferred(l - 1)
        for j in (1, 2, 3):
            came = lax.rem(digit + 4 - j, 4)
            send(
                ring.at[l, came], ring.at[l, came], ring_s.at[l, j - 1], ring_r.at[l, j - 1], peer(4**l, j)
            ).wait_recv()
        sends += started
        high = compose(ring[l, 2], ring[l, 3])
        total = compose(compose(ring[l, 0], ring[l, 1]), high)
        suf[...] = high
    z_snd[...] = total

    q = lax.div(me, quarter)
    down, down2 = lax.rem(me + n - quarter, n), lax.rem(me + n - 2 * quarter, n)
    part = pl.ds(0, lean)
    near_full = send(z_snd, z_near, z_s.at[0], z_r.at[0], down)
    near_lean = send(z_snd.at[part], z_near.at[part], z_s.at[0], z_r.at[0], down)
    top_far = send(top_snd, top_rcv, z_s.at[1], z_r.at[1], down2)
    top_near = send(top_snd, top_rcv, z_s.at[2], z_r.at[1], down)

    @pl.when(q == 3)
    def _():
        near_lean.start()

    @pl.when(q == 1)
    def _():
        near_full.start()

    deferred(levels - 2)

    @pl.when(q == 3)
    def _():
        near_lean.wait_send()

    @pl.when(q == 2)
    def _():
        near_lean.wait_recv()
        top_snd[...] = compose(z_snd[...], z_near[part, :])
        top_far.start()
        top_near.start()
        absorb(z_near[part, :])
        top_far.wait_send()
        top_near.wait_send()

    @pl.when(q == 0)
    def _():
        near_full.wait_recv()
        absorb(z_near[...])

    @pl.when(q < 2)
    def _():
        top_near.wait_recv()
        absorb(top_rcv[...])

    @pl.when(q == 1)
    def _():
        near_full.wait_send()

    out_copies = []
    for t in range(steps):
        out_copies.append(pltpu.make_async_copy(own.at[t, pl.ds(0, width)], covs_out.at[t], out_s.at[t]))
    means = jnp.concatenate([own[t, width : width + 1] for t in range(steps)], axis=0)
    mean_rows[...] = means
    out_copies.append(pltpu.make_async_copy(mean_rows, means_out, out_s.at[steps]))
    sums = own[0, :width]
    for t in range(1, steps):
        sums = sums + own[t, :width]
    m_hi, m_lo = split(means)
    outer = lambda u, v: lax.dot_general(u, v, (((0,), (0,)), ((), ())), preferred_element_type=F32)
    sums = sums + (outer(m_hi, m_hi) + (outer(m_hi, m_lo) + outer(m_lo, m_hi)))
    mom[...] = sums * (1.0 / (steps * n))

    def group_rows(k):
        return pl.ds(pl.multiple_of(k * rows, rows), rows)

    for j in range(1, GROUP):
        to = lax.rem(place + j, GROUP)
        c = send(mom.at[group_rows(to)], rs_buf.at[j - 1], rs_s.at[j - 1], rs_r.at[j - 1], base + to)
        c.start()
        sends.append(c)
    for c in out_copies:
        c.start()
    acc = mom[group_rows(place), :]
    for c, j in zip(sends[1 - GROUP :], range(1, GROUP)):
        c.wait_recv()
        acc = acc + rs_buf[j - 1]
    k = 0
    while GROUP << k < n:
        bf_snd[k] = acc
        c = send(bf_snd.at[k], bf_rcv.at[k], bf_s.at[k], bf_r.at[k], flip(GROUP << k))
        c.start()
        c.wait()
        acc = acc + bf_rcv[k]
        k += 1
    red[...] = acc
    gather = []
    for j in range(1, GROUP):
        to = lax.rem(place + j, GROUP)
        c = send(red, mom_all.at[group_rows(place)], ag_s.at[j - 1], ag_r.at[j - 1], base + to)
        c.start()
        gather.append(c)
    mom_all[group_rows(place), :] = acc
    for c in sends + gather:
        c.wait_send()
    for c in out_copies:
        c.wait()
    for c in gather:
        c.wait_recv()
    last = pltpu.make_async_copy(mom_all, mom_out, out_s.at[steps + 1])
    last.start()
    last.wait()


def hand_over(a, b, c, a_out, b_out, c_out, sems):
    copies = [
        pltpu.make_async_copy(x, y, sems.at[i])
        for i, (x, y) in enumerate(((b, b_out), (c, c_out), (a, a_out)))
    ]
    for copy in copies:
        copy.start()
    for copy in copies:
        copy.wait()


def local(n, gains, offsets, cov_terms):
    steps, width = gains.shape[0], gains.shape[1]
    levels = (n.bit_length() - 1) // 2
    assert n == 4**levels and levels > 1
    slab, lean, rows = 2 * width + PAD, width + PAD, width // GROUP
    far = max(1, (n // GROUP).bit_length() - 1)
    dma = pltpu.SemaphoreType.DMA
    vmem = pl.BlockSpec(memory_space=pltpu.VMEM)
    any_space = pl.BlockSpec(memory_space=pl.ANY)
    shapes = (
        jax.ShapeDtypeStruct((steps, width), F32),
        jax.ShapeDtypeStruct((steps, width, width), F32),
        jax.ShapeDtypeStruct((width, width), F32),
    )
    results = pl.pallas_call(
        functools.partial(kernel, n),
        out_shape=shapes,
        in_specs=[vmem] * 3,
        out_specs=(any_space,) * 3,
        scratch_shapes=[
            pltpu.VMEM((steps, slab, width), F32),
            pltpu.VMEM((levels - 1, 4, slab, width), F32),
            pltpu.VMEM((slab, width), F32),
            pltpu.VMEM((slab, width), F32),
            pltpu.VMEM((slab, width), F32),
            pltpu.VMEM((lean, width), F32),
            pltpu.VMEM((lean, width), F32),
            pltpu.VMEM((width, width), F32),
            pltpu.VMEM((GROUP - 1, rows, width), F32),
            pltpu.VMEM((far, rows, width), F32),
            pltpu.VMEM((far, rows, width), F32),
            pltpu.VMEM((rows, width), F32),
            pltpu.VMEM((width, width), F32),
            pltpu.VMEM((steps, width), F32),
            dma((levels - 1, 3)), dma((levels - 1, 3)),
            dma((3,)), dma((2,)),
            dma((GROUP - 1,)), dma((GROUP - 1,)),
            dma((far,)), dma((far,)),
            dma((GROUP - 1,)), dma((GROUP - 1,)),
            dma((steps + 2,)),
        ],
        compiler_params=pltpu.CompilerParams(collective_id=0, has_side_effects=True),
    )(gains, offsets, cov_terms)
    return pl.pallas_call(
        hand_over,
        out_shape=shapes,
        in_specs=[vmem] * 3,
        out_specs=(any_space,) * 3,
        scratch_shapes=[dma((3,))],
    )(*results)


def pack(s):
    half = s.shape[1] // 2
    row = lax.broadcasted_iota(jnp.int32, (half, 2 * half), 0)
    col = lax.broadcasted_iota(jnp.int32, (half, 2 * half), 1)
    low = s[half : 2 * half]
    both = jnp.where(jnp.logical_or(col >= half, row >= col), s[:half], pltpu.roll(low, half, 1))
    diag = jnp.sum(jnp.where(col - half == row, low, 0.0), axis=0, keepdims=True)
    first = lax.broadcasted_iota(jnp.int32, (PAD, 2 * half), 0) == 0
    return jnp.concatenate([both, jnp.where(first, s[2 * half :], diag)], axis=0)


def unpack(p):
    half = p.shape[1] // 2
    row = lax.broadcasted_iota(jnp.int32, (half, 2 * half), 0)
    col = lax.broadcasted_iota(jnp.int32, (half, 2 * half), 1)
    m = p[:half]
    turned = jnp.concatenate([m, m], axis=0).T
    top = jnp.where(jnp.logical_or(col >= half, row >= col), m, turned[:half])
    k = col - half
    right_low = jnp.where(row < k, pltpu.roll(m, half, 1), jnp.where(row == k, p[half + 1 : half + 2], turned[:half]))
    low = jnp.where(col < half, turned[half:], right_low)
    mean = jnp.broadcast_to(p[half : half + 1], (PAD, 2 * half))
    return jnp.concatenate([top, low, mean], axis=0)


def kernel16(
    gains_in, offsets_in, covs_in, means_out, covs_out, mom_out,
    gains, offsets, covs, own, held, ring, acc, suf, z_near, sym_snd, sym_rcv, z_sym, z_sym_rcv, top_snd, top_rcv, mom, mom_rcv, rs_buf, pre_buf, red,
    own_right, own_both, z_right, z_both,
    in_s, ring_s, ring_r, z_s, z_r, rs_s, rs_r, pre_r, ag_s, ag_r, pace,
):
    steps, width = gains.shape[0], gains.shape[1]
    lean = width + PAD
    n = 16
    me, core = lax.axis_index("tm"), lax.axis_index("seq")
    digit, q = lax.rem(me, 4), lax.div(me, 4)
    rows = (width // 2 + PAD) // 3
    central = [4 + i for i in range(4)]
    hosts = [(4, 0), (5, 1), (6, 2), (1, 1), (2, 2)]
    is_central = jnp.logical_and(q == 1, core == 1)
    is_wide = jnp.logical_and(is_central, digit < 3)
    is_near = jnp.logical_and(core == 1, jnp.logical_or(me == 1, me == 2))
    is_host = jnp.logical_or(is_wide, is_near)
    is_last = me == n - 1
    part, psi = pl.ds(0, lean), pl.ds(lean, width)
    packed = width // 2 + PAD
    dx, dy = 1 - 2 * lax.rem(digit, 2), 2 - 4 * lax.div(digit, 2)

    def at(tm, seq):
        return {"tm": tm, "seq": seq}

    def send(src, dst, s, r, to):
        return pltpu.make_async_remote_copy(
            src_ref=src, dst_ref=dst, send_sem=s, recv_sem=r,
            device_id=to, device_id_type=pl.DeviceIdType.MESH,
        )

    def landed(ref, sem):
        send(ref, ref, sem, sem, at(lax.rem(me + 1, n), core)).wait_recv()

    def sent(ref, sem):
        send(ref, ref, sem, sem, at(lax.rem(me + 1, n), core)).wait_send()

    barrier = pltpu.get_barrier_semaphore()

    def greet(tm, seq):
        pl.semaphore_signal(barrier, inc=1, device_id=at(tm, seq), device_id_type=pl.DeviceIdType.MESH)

    @pl.when(is_central)
    def _():
        for j in range(1, n):
            greet(lax.rem(me + j, n), core)
        for j in range(n):
            greet(j, 0)

    @pl.when(jnp.logical_not(is_central))
    def _():
        @pl.when(jnp.logical_or(q < 3, digit < 2))
        def _():
            for step in (dx, dy, dx + dy):
                greet(me + step, core)

        @pl.when(jnp.logical_and(q == 3, digit == 2))
        def _():
            greet(me + 1, core)

        for host in central:
            greet(host, 1)

        @pl.when(core == 1)
        def _():
            greet(me - digit + 2, 0)

        @pl.when(q == 0)
        def _():
            greet(8 + digit, core)

        @pl.when(is_near)
        def _():
            for j in range(8):
                greet(j, 0)
            for j in range(1, 4):
                greet(lax.rem(me + j, 4), 1)
            for seq in (0, 1):
                greet(8 + me, seq)
                greet(12 + me, seq)

        @pl.when(q == 2)
        def _():
            greet(12 + lax.rem(digit, 2), core)

        @pl.when(jnp.logical_and(q < 2, core == 0))
        def _():
            greet(me + 4, core)

    early, late = pl.ds(0, 2), pl.ds(2, steps - 2)
    fetch = [
        pltpu.make_async_copy(gains_in.at[early], gains.at[early], in_s.at[0]),
        pltpu.make_async_copy(gains_in.at[late], gains.at[late], in_s.at[1]),
        pltpu.make_async_copy(covs_in, covs, in_s.at[2]),
        pltpu.make_async_copy(offsets_in, offsets, in_s.at[3]),
    ]
    for c in fetch:
        c.start()

    def compose(e, f):
        e_psi = e[lean:]
        x = mul(left(f), right(e_psi))
        p = e[:width] + mul(left(e_psi.T), right(x[:width]))
        out = [p, e[width:lean] + x[width:lean]]
        if f.shape[0] > lean:
            out.append(x[lean:])
        return jnp.concatenate(out, axis=0)

    def slot(d):
        return lax.rem(d + 4 - digit, 4)

    def total_of(d):
        return ring[slot(d)]

    def exchange(src, dst):
        upper, lower = jnp.logical_or(q < 3, digit >= 2), jnp.logical_or(q < 3, digit != 2)
        for step, needed in ((dx + dy, upper), (dy, upper), (dx, lower)):
            there = lax.rem(4 - step, 4)
            pl.when(needed)(send(src, dst(there), ring_s, ring_r.at[there], at(me + step, core)).start)

    def exchange_psi():
        exchange(ring.at[0, psi], lambda there: ring.at[there, psi])

    fetch[0].wait()
    ready = jnp.where(q == 0, 7, jnp.where(q == 1, 8, jnp.where(q == 2, 9 - core, jnp.where(digit < 2, 7, 4 + digit))))
    ready = ready + jnp.where(jnp.logical_and(core == 0, jnp.logical_and(digit == 2, q != 1)), 4, 0)
    ready = ready + jnp.where(q < 2, 2, jnp.where(lax.rem(digit, 3) == 0, 0, 1)) - jnp.where(is_near, 1, 0)
    ready = jnp.where(is_central, 2 * n - 1, ready)

    def local_total(reach):
        cov, mean = covs[0], offset[0]
        for t in range(1, steps):
            e = reach[t - 1]
            x = mul(left(jnp.concatenate([covs[t], offset[t]], axis=0)), right(e.T))
            cov = cov + mul(left(e), right(x[:width]))
            mean = mean + x[width:]
        ring[0, part] = jnp.concatenate([cov, mean], axis=0)
        sym_snd[...] = pack(jnp.concatenate([cov, mean], axis=0))

    def reached():
        reach = [gains[0]]
        for t in range(1, steps - 1):
            reach.append(mul(left(reach[-1]), right(gains[t])))
        return reach

    fetch[1].wait()

    @pl.when(jnp.logical_not(is_last))
    def _():
        reach = reached()
        for t, e in enumerate(reach):
            held[t] = e
        ring[0, psi] = mul(left(reach[-1]), right(gains[steps - 1])).T

    fetch[2].wait()
    fetch[3].wait()
    offset = [jnp.broadcast_to(offsets[t : t + 1, :], (PAD, width)) for t in range(steps)]

    @pl.when(is_last)
    def _():
        ring[0, psi] = jnp.zeros((width, width), F32)
        local_total(reached())

    pl.semaphore_wait(barrier, ready)

    @pl.when(jnp.logical_and(jnp.logical_not(is_last), core == 0))
    def _():
        exchange_psi()

    @pl.when(jnp.logical_not(is_last))
    def _():
        local_total([held[t] for t in range(steps - 1)])

    @pl.when(jnp.logical_or(core == 0, is_last))
    def _():
        exchange(sym_snd, lambda there: sym_rcv.at[there])

        @pl.when(jnp.logical_and(core == 0, digit == 3))
        def _():
            pl.semaphore_signal(pace, inc=1, device_id=at(me - 1, 0), device_id_type=pl.DeviceIdType.MESH)

    own[0] = ring[0]
    run = jnp.where(is_last, jnp.zeros_like(gains[0]), gains[steps - 1])
    run = jnp.concatenate([covs[steps - 1], offset[steps - 1], run.T], axis=0)
    own[steps - 1] = run
    for t in reversed(range(1, steps - 1)):
        run = compose(jnp.concatenate([covs[t], offset[t], gains[t].T], axis=0), run)
        own[t] = run

    @pl.when(jnp.logical_and(core == 0, digit == 2))
    def _():
        pl.semaphore_wait(pace, 1)
        for j in range(4):
            pl.semaphore_signal(pace, inc=1, device_id=at(me - 2 + j, 1), device_id_type=pl.DeviceIdType.MESH)

    @pl.when(core == 1)
    def _():
        pl.semaphore_wait(pace, 1)

        @pl.when(jnp.logical_not(is_last))
        def _():
            exchange_psi()
            exchange(sym_snd, lambda there: sym_rcv.at[there])

    def prepare():
        for t in range(steps):
            e = own[t, psi]
            own_right[:, pl.ds(2 * t * width, 2 * width)] = right(e)
            own_both[t] = left(e.T)

    def apply(f):
        x = jnp.dot(left(f), own_right[...], preferred_element_type=F32)
        out = []
        for t in range(steps):
            xt = fold(x[:, 2 * t * width : 2 * (t + 1) * width])
            cov = own[t, :width] + mul(own_both[t], right(xt[:width]))
            out.append((cov, own[t, width:lean] + xt[width:lean], xt[lean:]))
        return out

    def absorb(f):
        for t, (cov, mean, rest) in enumerate(apply(f)):
            own[t, :width] = cov
            own[t, width:lean] = mean
            if f.shape[0] > lean:
                own[t, psi] = rest

    def finish(found):
        means = jnp.concatenate([mean[:1] for _, mean in found], axis=0)
        sums = found[0][0]
        for cov, _ in found[1:]:
            sums = sums + cov
        m_hi, m_lo = split(means)
        outer = lambda u, v: lax.dot_general(u, v, (((0,), (0,)), ((), ())), preferred_element_type=F32)
        sums = sums + (outer(m_hi, m_hi) + (outer(m_hi, m_lo) + outer(m_lo, m_hi)))
        mom[...] = pack(jnp.concatenate([sums * (1.0 / (steps * n)), jnp.zeros((PAD, width), F32)], axis=0))
        means_out[...] = means
        for t, (cov, _) in enumerate(found):
            covs_out[t] = cov

    def block(i):
        return pl.ds(i * rows, rows)

    mine = pl.ds(pl.multiple_of(lax.rem(digit, 3) * rows, PAD), rows)

    def arrive(d):
        here = slot(d)

        @pl.when(digit != d)
        def _():
            landed(ring.at[here, pl.ds(0, packed + width)], ring_r.at[here])
            ring[here, part] = unpack(sym_rcv[here])

    def state_of(base, f, after, before):
        x = mul(left(f), after)
        cov = base[:width] + mul(before, right(x[:width]))
        return jnp.concatenate([cov, base[width:lean] + x[width:]], axis=0)

    def hold(e):
        z_right[...] = right(e)
        z_both[...] = left(e.T)

    down, down2 = lax.rem(me + n - 4, n), lax.rem(me + n - 8, n)
    near_sym = send(z_sym, z_sym_rcv, z_s, z_r.at[0], at(down, core))
    near_psi = send(acc.at[psi], z_near.at[psi], z_s, z_r.at[0], at(down, core))
    top_far = send(top_snd, top_rcv, z_s, z_r.at[1], at(down2, core))
    top_near = send(top_snd, top_rcv, z_s, z_r.at[1], at(down, core))
    far_sym = send(z_sym, z_sym_rcv, z_s, z_r.at[0], at(lax.rem(me + n - 2, n), core))

    @pl.when(jnp.logical_and(q == 3, digit < 2))
    def _():
        arrive(0)
        arrive(1)
        acc[...] = compose(total_of(0), total_of(1))
        hold(acc[psi, :])
        arrive(2)
        e = total_of(2)[lean:]
        own_right[:, pl.ds(0, 2 * width)] = right(e)
        own_both[0] = left(e.T)
        landed(sym_rcv.at[slot(3)], ring_r.at[slot(3)])
        newest = unpack(sym_rcv[slot(3)])
        state = state_of(total_of(2)[:lean], newest, own_right[:, pl.ds(0, 2 * width)], own_both[0])
        suf[part, :] = state
        z_sym[...] = pack(state_of(acc[part, :], state, z_right[...], z_both[...]))
        far_sym.start()
        near_sym.start()

        @pl.when(digit == 0)
        def _():
            suf[part, :] = compose(total_of(1), suf[part, :])

    @pl.when(jnp.logical_and(q == 3, digit == 2))
    def _():
        landed(sym_rcv.at[slot(3)], ring_r.at[slot(3)])
        suf[part, :] = unpack(sym_rcv[slot(3)])

    @pl.when(q < 3)
    def _():
        arrive(3)
        acc[...] = total_of(3)
        for d in (2, 1, 0):
            @pl.when(digit == d)
            def _():
                suf[...] = acc[...]

            arrive(d)
            acc[...] = compose(total_of(d), acc[...])

    @pl.when(q == 1)
    def _():
        z_sym[...] = pack(acc[part, :])
        near_sym.start()
        near_psi.start()

    @pl.when(q == 2)
    def _():
        hold(acc[psi, :])

    prepare()

    @pl.when(digit < 3)
    def _():
        @pl.when(q == 3)
        def _():
            absorb(suf[part, :])

        @pl.when(q < 3)
        def _():
            absorb(suf[...])
            prepare()

    @pl.when(q == 2)
    def _():
        near_sym.wait_recv()
        near = unpack(z_sym_rcv[...])
        top_snd[...] = pack(state_of(acc[part, :], near, z_right[...], z_both[...]))
        top_far.start()
        top_near.start()
        absorb(near)

    @pl.when(q == 0)
    def _():
        landed(z_near.at[pl.ds(0, packed + width)], z_r.at[0])
        z_near[part, :] = unpack(z_sym_rcv[...])
        absorb(z_near[...])
        prepare()

    @pl.when(q < 2)
    def _():
        top_near.wait_recv()
        finish([found[:2] for found in apply(unpack(top_rcv[...]))])

        for host, i in hosts:
            scatter = send(mom.at[block(i)], rs_buf.at[core, me], rs_s, rs_r.at[core], at(host, 1))

            @pl.when(jnp.logical_or(me != host, core == 0))
            def _():
                scatter.start()

    @pl.when(q >= 2)
    def _():
        finish([(own[t, :width], own[t, width:lean]) for t in range(steps)])

        @pl.when(jnp.logical_and(q == 3, digit < 2))
        def _():
            near_sym.wait_send()
            far_sym.wait_send()

        for step in (dx + dy, dx, dy):
            to = digit + step
            theirs = pl.ds(pl.multiple_of(lax.rem(to, 3) * rows, PAD), rows)
            part_sum = send(mom.at[theirs], pre_buf.at[lax.rem(4 - step, 4)], rs_s, pre_r, at(me + step, core))
            pl.when(to < 3)(part_sum.start)

        @pl.when(digit < 3)
        def _():
            landed(pre_buf.at[pl.ds(1, 3)], pre_r)
            pre_buf[0] = (mom[mine, :] + pre_buf[1]) + (pre_buf[2] + pre_buf[3])
            for to, wanted in ((digit, digit > 0), (4 + digit, digit < 3)):
                upward = send(pre_buf.at[0], rs_buf.at[core, 6 + q], rs_s, rs_r.at[core], at(to, 1))
                pl.when(wanted)(upward.start)

    @pl.when(is_host)
    def _():
        rs_buf[1, me] = mom[mine, :]
        def gather(to, p):
            copy = send(red.at[p], mom_rcv.at[mine], ag_s, ag_r, at(to, p))
            if to == 0:
                pl.when(me < 5)(copy.start)
            elif p == 0 or to not in (4, 5, 6):
                copy.start()
            else:
                pl.when(me != to)(copy.start)

        for p in (0, 1):
            landed(rs_buf.at[p, pl.ds(0, 10 - p)], rs_r.at[p])
            parts = [rs_buf[p, j] for j in range(10)]
            while len(parts) > 1:
                parts = [u + v for u, v in zip(parts[::2], parts[1::2])] + parts[len(parts) & ~1 :]
            red[p] = parts[0]
            gather(0, p)
            if p == 1:
                @pl.when(is_wide)
                def _():
                    mom_rcv[mine, :] = parts[0]

        @pl.when(is_wide)
        def _():
            for some in (range(1, 8), range(8, n)):
                for p in (0, 1):
                    for to in some:
                        gather(to, p)

    @pl.when(is_wide)
    def _():
        landed(mom_rcv.at[pl.ds(0, 2 * rows)], ag_r)

    @pl.when(jnp.logical_not(is_wide))
    def _():
        landed(mom_rcv, ag_r)

    mom_out[...] = unpack(mom_rcv[...])[:width]

    def sent_blocks(count, sem):
        while count:
            some = min(count, 10)
            sent(rs_buf.at[0, pl.ds(0, some)], sem)
            count -= some

    @pl.when(is_near)
    def _():
        sent_blocks(2, ag_s)

    @pl.when(is_wide)
    def _():
        sent_blocks(29, ag_s)

        @pl.when(me == 4)
        def _():
            sent_blocks(2, ag_s)

    sent_blocks(3, rs_s)

    @pl.when(jnp.where(q < 2, 1, lax.rem(digit, 3)) > 0)
    def _():
        sent_blocks(1, rs_s)

    @pl.when(jnp.logical_and(q < 2, jnp.logical_not(is_host)))
    def _():
        sent_blocks(1, rs_s)

    @pl.when(q < 3)
    def _():
        sent(sym_rcv.at[pl.ds(1, 3)], ring_s)
        sent(ring.at[pl.ds(1, 3), psi], ring_s)

    @pl.when(q == 3)
    def _():
        @pl.when(digit < 3)
        def _():
            sent(ring.at[1, pl.ds(0, packed + width)], ring_s)

        @pl.when(digit == 2)
        def _():
            sent(ring.at[1, pl.ds(0, packed + width)], ring_s)

        @pl.when(digit == 3)
        def _():
            sent(sym_rcv.at[pl.ds(1, 3)], ring_s)

    @pl.when(q == 1)
    def _():
        near_sym.wait_send()
        near_psi.wait_send()

    @pl.when(q == 2)
    def _():
        top_far.wait_send()
        top_near.wait_send()


def write_out(a, b, c, a_out, b_out, c_out, sems):
    copies = [
        pltpu.make_async_copy(x, y, sems.at[i])
        for i, (x, y) in enumerate(((b, b_out), (c, c_out), (a, a_out)))
    ]
    for copy in copies:
        copy.start()
    for copy in copies:
        copy.wait()


def local16(gains, offsets, cov_terms):
    steps, width = gains.shape[0], gains.shape[1]
    slab, packed = 2 * width + PAD, width // 2 + PAD
    rows = packed // 3
    assert packed == 3 * rows and rows % PAD == 0
    dma = pltpu.SemaphoreType.DMA
    vmem = pl.BlockSpec(memory_space=pltpu.VMEM)
    shapes = ((steps, width), (steps, width, width), (width, width))
    results = pl.pallas_call(
        kernel16,
        out_shape=tuple(pltpu.VMEM(s, F32) for s in shapes),
        in_specs=[pl.BlockSpec(memory_space=pltpu.HBM)] * 3,
        out_specs=(vmem,) * 3,
        scratch_shapes=[
            pltpu.VMEM((steps, width, width), F32),
            pltpu.VMEM((steps, width), F32),
            pltpu.VMEM((steps, width, width), F32),
            pltpu.VMEM((steps, slab, width), F32),
            pltpu.VMEM((steps - 1, width, width), F32),
            pltpu.VMEM((4, slab, width), F32),
            pltpu.VMEM((slab, width), F32),
            pltpu.VMEM((slab, width), F32),
            pltpu.VMEM((slab, width), F32),
            pltpu.VMEM((packed, width), F32),
            pltpu.VMEM((4, packed, width), F32),
            pltpu.VMEM((packed, width), F32),
            pltpu.VMEM((packed, width), F32),
            pltpu.VMEM((packed, width), F32),
            pltpu.VMEM((packed, width), F32),
            pltpu.VMEM((packed, width), F32),
            pltpu.VMEM((packed, width), F32),
            pltpu.VMEM((2, 10, rows, width), F32),
            pltpu.VMEM((4, rows, width), F32),
            pltpu.VMEM((2, rows, width), F32),
            pltpu.VMEM((2 * width, 2 * steps * width), BF16),
            pltpu.VMEM((steps, width, 2 * width), BF16),
            pltpu.VMEM((2 * width, 2 * width), BF16),
            pltpu.VMEM((width, 2 * width), BF16),
            dma((4,)), dma, dma((4,)), dma, dma((2,)), dma, dma((2,)), dma, dma, dma, pltpu.SemaphoreType.REGULAR,
        ],
        compiler_params=pltpu.CompilerParams(collective_id=0, has_side_effects=True),
    )(gains, offsets, cov_terms)
    results = [pltpu.with_memory_space_constraint(r, pltpu.VMEM) for r in results]
    return pl.pallas_call(
        write_out,
        out_shape=tuple(jax.ShapeDtypeStruct(s, F32) for s in shapes),
        in_specs=[vmem] * 3,
        out_specs=(pl.BlockSpec(memory_space=pl.ANY),) * 3,
        scratch_shapes=[dma((3,))],
    )(*results)


def solution(mesh):
    n = mesh.shape["tm"]
    in_specs = (P(("seq", "tm"), None, None), P(("seq", "tm"), None), P(("seq", "tm"), None, None))
    out_specs = (P(("seq", "tm"), None), P(("seq", "tm"), None, None), P("seq", None))
    return jax.shard_map(
        local16 if n == 16 and mesh.shape["seq"] == 2 else functools.partial(local, n), mesh=mesh, in_specs=in_specs, out_specs=out_specs, check_vma=False
    )
```

```python
import functools

import jax
import jax.numpy as jnp
from jax import lax
from jax.experimental import pallas as pl
from jax.experimental.pallas import tpu as pltpu
from jax.sharding import PartitionSpec as P

F32 = jnp.float32
BF16 = jnp.bfloat16
PAD = 8
GROUP = 16


def split(x):
    hi = x.astype(BF16)
    return hi, (x - hi.astype(F32)).astype(BF16)


def left(x):
    return jnp.concatenate(split(x), axis=1)


def right(w):
    both = jnp.concatenate(split(w), axis=1)
    return jnp.concatenate([both, both], axis=0)


def fold(x):
    half = x.shape[1] // 2
    return x[:, :half] + x[:, half:]


def mul(x, w):
    return fold(jnp.dot(x, w, preferred_element_type=F32))


def kernel(
    n, gains, offsets, covs, means_out, covs_out, mom_out,
    own, ring, suf, z_snd, z_near, top_snd, top_rcv,
    mom, rs_buf, bf_snd, bf_rcv, red, mom_all, mean_rows,
    ring_s, ring_r, z_s, z_r, rs_s, rs_r, bf_s, bf_r, ag_s, ag_r, out_s,
):
    steps, width = gains.shape[0], gains.shape[1]
    lean = width + PAD
    me = lax.axis_index("tm")
    levels = (n.bit_length() - 1) // 2
    quarter = n // 4
    rows = width // GROUP
    place = lax.rem(me, GROUP)
    base = me - place

    def flip(step):
        return me + step * (1 - 2 * lax.rem(lax.div(me, step), 2))

    def digit_of(stride):
        return lax.rem(lax.div(me, stride), 4)

    def peer(stride, j):
        digit = digit_of(stride)
        return me + stride * (lax.rem(digit + j, 4) - digit)

    peers = [base + lax.rem(place + j, GROUP) for j in range(1, GROUP)]
    peers += [peer(4**l, j) for l in range(2, levels) for j in (1, 2, 3)]
    barrier = pltpu.get_barrier_semaphore()
    for to in peers:
        pl.semaphore_signal(barrier, inc=1, device_id={"tm": to}, device_id_type=pl.DeviceIdType.MESH)

    def send(src, dst, s, r, to):
        return pltpu.make_async_remote_copy(
            src_ref=src, dst_ref=dst, send_sem=s, recv_sem=r,
            device_id={"tm": to}, device_id_type=pl.DeviceIdType.MESH,
        )

    def compose(e, f):
        e_psi = e[lean:]
        x = mul(left(f), right(e_psi))
        p = e[:width] + mul(left(e_psi.T), right(x[:width]))
        out = [p, e[width:lean] + x[width:lean]]
        if f.shape[0] > lean:
            out.append(x[lean:])
        return jnp.concatenate(out, axis=0)

    for t in reversed(range(steps)):
        gain = gains[t]
        if t == steps - 1:
            gain = jnp.where(me == n - 1, jnp.zeros_like(gain), gain)
        offset = jnp.broadcast_to(offsets[t : t + 1, :], (PAD, width))
        element = jnp.concatenate([covs[t], offset, gain.T], axis=0)
        own[t] = element if t == steps - 1 else compose(element, own[t + 1])

    def absorb(f):
        for t in range(steps):
            own[t, : f.shape[0]] = compose(own[t], f)

    pl.semaphore_wait(barrier, len(peers))

    def deferred(l):
        digit = digit_of(4**l)

        @pl.when(digit == 0)
        def _():
            suf[...] = compose(ring[l, 1], suf[...])

        @pl.when(digit == 2)
        def _():
            suf[...] = ring[l, 3]

        @pl.when(digit < 3)
        def _():
            absorb(suf[...])

    sends = []
    total = own[0]
    for l in range(levels - 1):
        digit = digit_of(4**l)
        ring[l, digit] = total
        started = []
        for j in (2, 1, 3):
            c = send(
                ring.at[l, digit], ring.at[l, digit], ring_s.at[l, j - 1], ring_r.at[l, j - 1], peer(4**l, j)
            )
            c.start()
            started.append(c)
        if l:
            deferred(l - 1)
        for j in (1, 2, 3):
            came = lax.rem(digit + 4 - j, 4)
            send(
                ring.at[l, came], ring.at[l, came], ring_s.at[l, j - 1], ring_r.at[l, j - 1], peer(4**l, j)
            ).wait_recv()
        sends += started
        high = compose(ring[l, 2], ring[l, 3])
        total = compose(compose(ring[l, 0], ring[l, 1]), high)
        suf[...] = high
    z_snd[...] = total

    q = lax.div(me, quarter)
    down, down2 = lax.rem(me + n - quarter, n), lax.rem(me + n - 2 * quarter, n)
    part = pl.ds(0, lean)
    near_full = send(z_snd, z_near, z_s.at[0], z_r.at[0], down)
    near_lean = send(z_snd.at[part], z_near.at[part], z_s.at[0], z_r.at[0], down)
    top_far = send(top_snd, top_rcv, z_s.at[1], z_r.at[1], down2)
    top_near = send(top_snd, top_rcv, z_s.at[2], z_r.at[1], down)

    @pl.when(q == 3)
    def _():
        near_lean.start()

    @pl.when(q == 1)
    def _():
        near_full.start()

    deferred(levels - 2)

    @pl.when(q == 3)
    def _():
        near_lean.wait_send()

    @pl.when(q == 2)
    def _():
        near_lean.wait_recv()
        top_snd[...] = compose(z_snd[...], z_near[part, :])
        top_far.start()
        top_near.start()
        absorb(z_near[part, :])
        top_far.wait_send()
        top_near.wait_send()

    @pl.when(q == 0)
    def _():
        near_full.wait_recv()
        absorb(z_near[...])

    @pl.when(q < 2)
    def _():
        top_near.wait_recv()
        absorb(top_rcv[...])

    @pl.when(q == 1)
    def _():
        near_full.wait_send()

    out_copies = []
    for t in range(steps):
        out_copies.append(pltpu.make_async_copy(own.at[t, pl.ds(0, width)], covs_out.at[t], out_s.at[t]))
    means = jnp.concatenate([own[t, width : width + 1] for t in range(steps)], axis=0)
    mean_rows[...] = means
    out_copies.append(pltpu.make_async_copy(mean_rows, means_out, out_s.at[steps]))
    sums = own[0, :width]
    for t in range(1, steps):
        sums = sums + own[t, :width]
    m_hi, m_lo = split(means)
    outer = lambda u, v: lax.dot_general(u, v, (((0,), (0,)), ((), ())), preferred_element_type=F32)
    sums = sums + (outer(m_hi, m_hi) + (outer(m_hi, m_lo) + outer(m_lo, m_hi)))
    mom[...] = sums * (1.0 / (steps * n))

    def group_rows(k):
        return pl.ds(pl.multiple_of(k * rows, rows), rows)

    for j in range(1, GROUP):
        to = lax.rem(place + j, GROUP)
        c = send(mom.at[group_rows(to)], rs_buf.at[j - 1], rs_s.at[j - 1], rs_r.at[j - 1], base + to)
        c.start()
        sends.append(c)
    for c in out_copies:
        c.start()
    acc = mom[group_rows(place), :]
    for c, j in zip(sends[1 - GROUP :], range(1, GROUP)):
        c.wait_recv()
        acc = acc + rs_buf[j - 1]
    k = 0
    while GROUP << k < n:
        bf_snd[k] = acc
        c = send(bf_snd.at[k], bf_rcv.at[k], bf_s.at[k], bf_r.at[k], flip(GROUP << k))
        c.start()
        c.wait()
        acc = acc + bf_rcv[k]
        k += 1
    red[...] = acc
    gather = []
    for j in range(1, GROUP):
        to = lax.rem(place + j, GROUP)
        c = send(red, mom_all.at[group_rows(place)], ag_s.at[j - 1], ag_r.at[j - 1], base + to)
        c.start()
        gather.append(c)
    mom_all[group_rows(place), :] = acc
    for c in sends + gather:
        c.wait_send()
    for c in out_copies:
        c.wait()
    for c in gather:
        c.wait_recv()
    last = pltpu.make_async_copy(mom_all, mom_out, out_s.at[steps + 1])
    last.start()
    last.wait()


def hand_over(a, b, c, a_out, b_out, c_out, sems):
    copies = [
        pltpu.make_async_copy(x, y, sems.at[i])
        for i, (x, y) in enumerate(((b, b_out), (c, c_out), (a, a_out)))
    ]
    for copy in copies:
        copy.start()
    for copy in copies:
        copy.wait()


def local(n, gains, offsets, cov_terms):
    steps, width = gains.shape[0], gains.shape[1]
    levels = (n.bit_length() - 1) // 2
    assert n == 4**levels and levels > 1
    slab, lean, rows = 2 * width + PAD, width + PAD, width // GROUP
    far = max(1, (n // GROUP).bit_length() - 1)
    dma = pltpu.SemaphoreType.DMA
    vmem = pl.BlockSpec(memory_space=pltpu.VMEM)
    any_space = pl.BlockSpec(memory_space=pl.ANY)
    shapes = (
        jax.ShapeDtypeStruct((steps, width), F32),
        jax.ShapeDtypeStruct((steps, width, width), F32),
        jax.ShapeDtypeStruct((width, width), F32),
    )
    results = pl.pallas_call(
        functools.partial(kernel, n),
        out_shape=shapes,
        in_specs=[vmem] * 3,
        out_specs=(any_space,) * 3,
        scratch_shapes=[
            pltpu.VMEM((steps, slab, width), F32),
            pltpu.VMEM((levels - 1, 4, slab, width), F32),
            pltpu.VMEM((slab, width), F32),
            pltpu.VMEM((slab, width), F32),
            pltpu.VMEM((slab, width), F32),
            pltpu.VMEM((lean, width), F32),
            pltpu.VMEM((lean, width), F32),
            pltpu.VMEM((width, width), F32),
            pltpu.VMEM((GROUP - 1, rows, width), F32),
            pltpu.VMEM((far, rows, width), F32),
            pltpu.VMEM((far, rows, width), F32),
            pltpu.VMEM((rows, width), F32),
            pltpu.VMEM((width, width), F32),
            pltpu.VMEM((steps, width), F32),
            dma((levels - 1, 3)), dma((levels - 1, 3)),
            dma((3,)), dma((2,)),
            dma((GROUP - 1,)), dma((GROUP - 1,)),
            dma((far,)), dma((far,)),
            dma((GROUP - 1,)), dma((GROUP - 1,)),
            dma((steps + 2,)),
        ],
        compiler_params=pltpu.CompilerParams(collective_id=0, has_side_effects=True),
    )(gains, offsets, cov_terms)
    return pl.pallas_call(
        hand_over,
        out_shape=shapes,
        in_specs=[vmem] * 3,
        out_specs=(any_space,) * 3,
        scratch_shapes=[dma((3,))],
    )(*results)


def pack(s):
    half = s.shape[1] // 2
    row = lax.broadcasted_iota(jnp.int32, (half, 2 * half), 0)
    col = lax.broadcasted_iota(jnp.int32, (half, 2 * half), 1)
    low = s[half : 2 * half]
    both = jnp.where(jnp.logical_or(col >= half, row >= col), s[:half], pltpu.roll(low, half, 1))
    diag = jnp.sum(jnp.where(col - half == row, low, 0.0), axis=0, keepdims=True)
    first = lax.broadcasted_iota(jnp.int32, (PAD, 2 * half), 0) == 0
    return jnp.concatenate([both, jnp.where(first, s[2 * half :], diag)], axis=0)


def unpack(p):
    half = p.shape[1] // 2
    row = lax.broadcasted_iota(jnp.int32, (half, 2 * half), 0)
    col = lax.broadcasted_iota(jnp.int32, (half, 2 * half), 1)
    m = p[:half]
    turned = jnp.concatenate([m, m], axis=0).T
    top = jnp.where(jnp.logical_or(col >= half, row >= col), m, turned[:half])
    k = col - half
    right_low = jnp.where(row < k, pltpu.roll(m, half, 1), jnp.where(row == k, p[half + 1 : half + 2], turned[:half]))
    low = jnp.where(col < half, turned[half:], right_low)
    mean = jnp.broadcast_to(p[half : half + 1], (PAD, 2 * half))
    return jnp.concatenate([top, low, mean], axis=0)


def kernel16(
    gains_in, offsets_in, covs_in, means_out, covs_out, mom_out,
    gains, offsets, covs, own, held, ring, acc, suf, z_near, sym_snd, sym_rcv, z_sym, z_sym_rcv, top_snd, top_rcv, mom, mom_rcv, rs_buf, pre_buf, red,
    own_right, own_both, z_right, z_both,
    in_s, ring_s, ring_r, z_s, z_r, rs_s, rs_r, pre_r, ag_s, ag_r, pace,
):
    steps, width = gains.shape[0], gains.shape[1]
    lean = width + PAD
    n = 16
    me, core = lax.axis_index("tm"), lax.axis_index("seq")
    digit, q = lax.rem(me, 4), lax.div(me, 4)
    rows = (width // 2 + PAD) // 3
    central = [4 + i for i in range(4)]
    hosts = [(4, 0), (5, 1), (6, 2), (1, 1), (2, 2)]
    is_central = jnp.logical_and(q == 1, core == 1)
    is_wide = jnp.logical_and(is_central, digit < 3)
    is_near = jnp.logical_and(core == 1, jnp.logical_or(me == 1, me == 2))
    is_host = jnp.logical_or(is_wide, is_near)
    is_last = me == n - 1
    part, psi = pl.ds(0, lean), pl.ds(lean, width)
    packed = width // 2 + PAD
    dx, dy = 1 - 2 * lax.rem(digit, 2), 2 - 4 * lax.div(digit, 2)

    def at(tm, seq):
        return {"tm": tm, "seq": seq}

    def send(src, dst, s, r, to):
        return pltpu.make_async_remote_copy(
            src_ref=src, dst_ref=dst, send_sem=s, recv_sem=r,
            device_id=to, device_id_type=pl.DeviceIdType.MESH,
        )

    def landed(ref, sem):
        send(ref, ref, sem, sem, at(lax.rem(me + 1, n), core)).wait_recv()

    def sent(ref, sem):
        send(ref, ref, sem, sem, at(lax.rem(me + 1, n), core)).wait_send()

    barrier = pltpu.get_barrier_semaphore()

    def greet(tm, seq):
        pl.semaphore_signal(barrier, inc=1, device_id=at(tm, seq), device_id_type=pl.DeviceIdType.MESH)

    @pl.when(is_central)
    def _():
        for j in range(1, n):
            greet(lax.rem(me + j, n), core)
        for j in range(n):
            greet(j, 0)

    @pl.when(jnp.logical_not(is_central))
    def _():
        @pl.when(jnp.logical_or(q < 3, digit < 2))
        def _():
            for step in (dx, dy, dx + dy):
                greet(me + step, core)

        @pl.when(jnp.logical_and(q == 3, digit == 2))
        def _():
            greet(me + 1, core)

        for host in central:
            greet(host, 1)

        @pl.when(core == 1)
        def _():
            greet(me - digit + 2, 0)

        @pl.when(q == 0)
        def _():
            greet(8 + digit, core)

        @pl.when(is_near)
        def _():
            for j in range(8):
                greet(j, 0)
            for j in range(1, 4):
                greet(lax.rem(me + j, 4), 1)
            for seq in (0, 1):
                greet(8 + me, seq)
                greet(12 + me, seq)

        @pl.when(q == 2)
        def _():
            greet(12 + lax.rem(digit, 2), core)

        @pl.when(jnp.logical_and(q < 2, core == 0))
        def _():
            greet(me + 4, core)

    early, late = pl.ds(0, 2), pl.ds(2, steps - 2)
    fetch = [
        pltpu.make_async_copy(gains_in.at[early], gains.at[early], in_s.at[0]),
        pltpu.make_async_copy(gains_in.at[late], gains.at[late], in_s.at[1]),
        pltpu.make_async_copy(covs_in, covs, in_s.at[2]),
        pltpu.make_async_copy(offsets_in, offsets, in_s.at[3]),
    ]
    for c in fetch:
        c.start()

    def compose(e, f):
        e_psi = e[lean:]
        x = mul(left(f), right(e_psi))
        p = e[:width] + mul(left(e_psi.T), right(x[:width]))
        out = [p, e[width:lean] + x[width:lean]]
        if f.shape[0] > lean:
            out.append(x[lean:])
        return jnp.concatenate(out, axis=0)

    def slot(d):
        return lax.rem(d + 4 - digit, 4)

    def total_of(d):
        return ring[slot(d)]

    def exchange(src, dst):
        upper, lower = jnp.logical_or(q < 3, digit >= 2), jnp.logical_or(q < 3, digit != 2)
        for step, needed in ((dx + dy, upper), (dy, upper), (dx, lower)):
            there = lax.rem(4 - step, 4)
            pl.when(needed)(send(src, dst(there), ring_s, ring_r.at[there], at(me + step, core)).start)

    def exchange_psi():
        exchange(ring.at[0, psi], lambda there: ring.at[there, psi])

    fetch[0].wait()
    ready = jnp.where(q == 0, 7, jnp.where(q == 1, 8, jnp.where(q == 2, 9 - core, jnp.where(digit < 2, 7, 4 + digit))))
    ready = ready + jnp.where(jnp.logical_and(core == 0, jnp.logical_and(digit == 2, q != 1)), 4, 0)
    ready = ready + jnp.where(q < 2, 2, jnp.where(lax.rem(digit, 3) == 0, 0, 1)) - jnp.where(is_near, 1, 0)
    ready = jnp.where(is_central, 2 * n - 1, ready)

    def local_total(reach):
        cov, mean = covs[0], offset[0]
        for t in range(1, steps):
            e = reach[t - 1]
            x = mul(left(jnp.concatenate([covs[t], offset[t]], axis=0)), right(e.T))
            cov = cov + mul(left(e), right(x[:width]))
            mean = mean + x[width:]
        ring[0, part] = jnp.concatenate([cov, mean], axis=0)
        sym_snd[...] = pack(jnp.concatenate([cov, mean], axis=0))

    def reached():
        reach = [gains[0]]
        for t in range(1, steps - 1):
            reach.append(mul(left(reach[-1]), right(gains[t])))
        return reach

    fetch[1].wait()

    @pl.when(jnp.logical_not(is_last))
    def _():
        reach = reached()
        for t, e in enumerate(reach):
            held[t] = e
        ring[0, psi] = mul(left(reach[-1]), right(gains[steps - 1])).T

    fetch[2].wait()
    fetch[3].wait()
    offset = [jnp.broadcast_to(offsets[t : t + 1, :], (PAD, width)) for t in range(steps)]

    @pl.when(is_last)
    def _():
        ring[0, psi] = jnp.zeros((width, width), F32)
        local_total(reached())

    pl.semaphore_wait(barrier, ready)

    @pl.when(jnp.logical_and(jnp.logical_not(is_last), core == 0))
    def _():
        exchange_psi()

    @pl.when(jnp.logical_not(is_last))
    def _():
        local_total([held[t] for t in range(steps - 1)])

    @pl.when(jnp.logical_or(core == 0, is_last))
    def _():
        exchange(sym_snd, lambda there: sym_rcv.at[there])

        @pl.when(jnp.logical_and(core == 0, digit == 3))
        def _():
            pl.semaphore_signal(pace, inc=1, device_id=at(me - 1, 0), device_id_type=pl.DeviceIdType.MESH)

    own[0] = ring[0]
    run = jnp.where(is_last, jnp.zeros_like(gains[0]), gains[steps - 1])
    run = jnp.concatenate([covs[steps - 1], offset[steps - 1], run.T], axis=0)
    own[steps - 1] = run
    for t in reversed(range(1, steps - 1)):
        run = compose(jnp.concatenate([covs[t], offset[t], gains[t].T], axis=0), run)
        own[t] = run

    @pl.when(jnp.logical_and(core == 0, digit == 2))
    def _():
        pl.semaphore_wait(pace, 1)
        for j in range(4):
            pl.semaphore_signal(pace, inc=1, device_id=at(me - 2 + j, 1), device_id_type=pl.DeviceIdType.MESH)

    @pl.when(core == 1)
    def _():
        pl.semaphore_wait(pace, 1)

        @pl.when(jnp.logical_not(is_last))
        def _():
            exchange_psi()
            exchange(sym_snd, lambda there: sym_rcv.at[there])

    def prepare():
        for t in range(steps):
            e = own[t, psi]
            own_right[:, pl.ds(2 * t * width, 2 * width)] = right(e)
            own_both[t] = left(e.T)

    def apply(f):
        x = jnp.dot(left(f), own_right[...], preferred_element_type=F32)
        out = []
        for t in range(steps):
            xt = fold(x[:, 2 * t * width : 2 * (t + 1) * width])
            cov = own[t, :width] + mul(own_both[t], right(xt[:width]))
            out.append((cov, own[t, width:lean] + xt[width:lean], xt[lean:]))
        return out

    def absorb(f):
        for t, (cov, mean, rest) in enumerate(apply(f)):
            own[t, :width] = cov
            own[t, width:lean] = mean
            if f.shape[0] > lean:
                own[t, psi] = rest

    def finish(found):
        means = jnp.concatenate([mean[:1] for _, mean in found], axis=0)
        sums = found[0][0]
        for cov, _ in found[1:]:
            sums = sums + cov
        m_hi, m_lo = split(means)
        outer = lambda u, v: lax.dot_general(u, v, (((0,), (0,)), ((), ())), preferred_element_type=F32)
        sums = sums + (outer(m_hi, m_hi) + (outer(m_hi, m_lo) + outer(m_lo, m_hi)))
        mom[...] = pack(jnp.concatenate([sums * (1.0 / (steps * n)), jnp.zeros((PAD, width), F32)], axis=0))
        means_out[...] = means
        for t, (cov, _) in enumerate(found):
            covs_out[t] = cov

    def block(i):
        return pl.ds(i * rows, rows)

    mine = pl.ds(pl.multiple_of(lax.rem(digit, 3) * rows, PAD), rows)

    def arrive(d):
        here = slot(d)

        @pl.when(digit != d)
        def _():
            landed(ring.at[here, pl.ds(0, packed + width)], ring_r.at[here])
            ring[here, part] = unpack(sym_rcv[here])

    def state_of(base, f, after, before):
        x = mul(left(f), after)
        cov = base[:width] + mul(before, right(x[:width]))
        return jnp.concatenate([cov, base[width:lean] + x[width:]], axis=0)

    def hold(e):
        z_right[...] = right(e)
        z_both[...] = left(e.T)

    down, down2 = lax.rem(me + n - 4, n), lax.rem(me + n - 8, n)
    near_sym = send(z_sym, z_sym_rcv, z_s, z_r.at[0], at(down, core))
    near_psi = send(acc.at[psi], z_near.at[psi], z_s, z_r.at[0], at(down, core))
    top_far = send(top_snd, top_rcv, z_s, z_r.at[1], at(down2, core))
    top_near = send(top_snd, top_rcv, z_s, z_r.at[1], at(down, core))
    far_sym = send(z_sym, z_sym_rcv, z_s, z_r.at[0], at(lax.rem(me + n - 2, n), core))

    @pl.when(jnp.logical_and(q == 3, digit < 2))
    def _():
        arrive(0)
        arrive(1)
        acc[...] = compose(total_of(0), total_of(1))
        hold(acc[psi, :])
        arrive(2)
        e = total_of(2)[lean:]
        own_right[:, pl.ds(0, 2 * width)] = right(e)
        own_both[0] = left(e.T)
        landed(sym_rcv.at[slot(3)], ring_r.at[slot(3)])
        newest = unpack(sym_rcv[slot(3)])
        state = state_of(total_of(2)[:lean], newest, own_right[:, pl.ds(0, 2 * width)], own_both[0])
        suf[part, :] = state
        z_sym[...] = pack(state_of(acc[part, :], state, z_right[...], z_both[...]))
        far_sym.start()
        near_sym.start()

        @pl.when(digit == 0)
        def _():
            suf[part, :] = compose(total_of(1), suf[part, :])

    @pl.when(jnp.logical_and(q == 3, digit == 2))
    def _():
        landed(sym_rcv.at[slot(3)], ring_r.at[slot(3)])
        suf[part, :] = unpack(sym_rcv[slot(3)])

    @pl.when(q < 3)
    def _():
        arrive(3)
        acc[...] = total_of(3)
        for d in (2, 1, 0):
            @pl.when(digit == d)
            def _():
                suf[...] = acc[...]

            arrive(d)
            acc[...] = compose(total_of(d), acc[...])

    @pl.when(q == 1)
    def _():
        z_sym[...] = pack(acc[part, :])
        near_sym.start()
        near_psi.start()

    @pl.when(q == 2)
    def _():
        hold(acc[psi, :])

    prepare()

    @pl.when(digit < 3)
    def _():
        @pl.when(q == 3)
        def _():
            absorb(suf[part, :])

        @pl.when(q < 3)
        def _():
            absorb(suf[...])
            prepare()

    @pl.when(q == 2)
    def _():
        near_sym.wait_recv()
        near = unpack(z_sym_rcv[...])
        top_snd[...] = pack(state_of(acc[part, :], near, z_right[...], z_both[...]))
        top_far.start()
        top_near.start()
        absorb(near)

    @pl.when(q == 0)
    def _():
        landed(z_near.at[pl.ds(0, packed + width)], z_r.at[0])
        z_near[part, :] = unpack(z_sym_rcv[...])
        absorb(z_near[...])
        prepare()

    @pl.when(q < 2)
    def _():
        top_near.wait_recv()
        finish([found[:2] for found in apply(unpack(top_rcv[...]))])

        def scatter(host, at_block):
            send(mom.at[at_block], rs_buf.at[core, me], rs_s, rs_r.at[core], at(host, 1)).start()

        across_host = 7 - me
        theirs = pl.ds(pl.multiple_of(lax.rem(lax.rem(across_host, 4), 3) * rows, PAD), rows)

        @pl.when(lax.rem(across_host, 4) * lax.rem(me, 4) * across_host + jnp.where(me == 3, 1, 0) > 0)
        def _():
            scatter(across_host, theirs)

        for host, i in hosts:
            @pl.when(jnp.logical_and(across_host != host, jnp.logical_or(me != host, core == 0)))
            def _():
                scatter(host, block(i))

    @pl.when(q >= 2)
    def _():
        finish([(own[t, :width], own[t, width:lean]) for t in range(steps)])

        @pl.when(jnp.logical_and(q == 3, digit < 2))
        def _():
            near_sym.wait_send()
            far_sym.wait_send()

        for step in (dx + dy, dx, dy):
            to = digit + step
            theirs = pl.ds(pl.multiple_of(lax.rem(to, 3) * rows, PAD), rows)
            part_sum = send(mom.at[theirs], pre_buf.at[lax.rem(4 - step, 4)], rs_s, pre_r, at(me + step, core))
            pl.when(to < 3)(part_sum.start)

        @pl.when(digit < 3)
        def _():
            landed(pre_buf.at[pl.ds(1, 3)], pre_r)
            pre_buf[0] = (mom[mine, :] + pre_buf[1]) + (pre_buf[2] + pre_buf[3])
            for to, wanted in ((digit, digit > 0), (4 + digit, digit < 3)):
                upward = send(pre_buf.at[0], rs_buf.at[core, 6 + q], rs_s, rs_r.at[core], at(to, 1))
                pl.when(wanted)(upward.start)

    @pl.when(is_host)
    def _():
        rs_buf[1, me] = mom[mine, :]
        def gather(to, p):
            copy = send(red.at[p], mom_rcv.at[mine], ag_s, ag_r, at(to, p))
            if to == 0:
                pl.when(me < 5)(copy.start)
            elif p == 0 or to not in (4, 5, 6):
                copy.start()
            else:
                pl.when(me != to)(copy.start)

        for p in (0, 1):
            landed(rs_buf.at[p, pl.ds(0, 10 - p)], rs_r.at[p])
            parts = [rs_buf[p, j] for j in range(10)]
            while len(parts) > 1:
                parts = [u + v for u, v in zip(parts[::2], parts[1::2])] + parts[len(parts) & ~1 :]
            red[p] = parts[0]
            gather(0, p)
            if p == 1:
                @pl.when(is_wide)
                def _():
                    mom_rcv[mine, :] = parts[0]

        @pl.when(is_wide)
        def _():
            for some in (range(1, 8), range(8, n)):
                for p in (0, 1):
                    for to in some:
                        gather(to, p)

    @pl.when(is_wide)
    def _():
        landed(mom_rcv.at[pl.ds(0, 2 * rows)], ag_r)

    @pl.when(jnp.logical_not(is_wide))
    def _():
        landed(mom_rcv, ag_r)

    mom_out[...] = unpack(mom_rcv[...])[:width]

    def sent_blocks(count, sem):
        while count:
            some = min(count, 10)
            sent(rs_buf.at[0, pl.ds(0, some)], sem)
            count -= some

    @pl.when(is_near)
    def _():
        sent_blocks(2, ag_s)

    @pl.when(is_wide)
    def _():
        sent_blocks(29, ag_s)

        @pl.when(me == 4)
        def _():
            sent_blocks(2, ag_s)

    sent_blocks(3, rs_s)

    @pl.when(jnp.where(q < 2, 1, lax.rem(digit, 3)) > 0)
    def _():
        sent_blocks(1, rs_s)

    @pl.when(jnp.logical_and(q < 2, jnp.logical_not(is_host)))
    def _():
        sent_blocks(1, rs_s)

    @pl.when(q < 3)
    def _():
        sent(sym_rcv.at[pl.ds(1, 3)], ring_s)
        sent(ring.at[pl.ds(1, 3), psi], ring_s)

    @pl.when(q == 3)
    def _():
        @pl.when(digit < 3)
        def _():
            sent(ring.at[1, pl.ds(0, packed + width)], ring_s)

        @pl.when(digit == 2)
        def _():
            sent(ring.at[1, pl.ds(0, packed + width)], ring_s)

        @pl.when(digit == 3)
        def _():
            sent(sym_rcv.at[pl.ds(1, 3)], ring_s)

    @pl.when(q == 1)
    def _():
        near_sym.wait_send()
        near_psi.wait_send()

    @pl.when(q == 2)
    def _():
        top_far.wait_send()
        top_near.wait_send()


def write_out(a, b, c, a_out, b_out, c_out, sems):
    copies = [
        pltpu.make_async_copy(x, y, sems.at[i])
        for i, (x, y) in enumerate(((b, b_out), (c, c_out), (a, a_out)))
    ]
    for copy in copies:
        copy.start()
    for copy in copies:
        copy.wait()


def local16(gains, offsets, cov_terms):
    steps, width = gains.shape[0], gains.shape[1]
    slab, packed = 2 * width + PAD, width // 2 + PAD
    rows = packed // 3
    assert packed == 3 * rows and rows % PAD == 0
    dma = pltpu.SemaphoreType.DMA
    vmem = pl.BlockSpec(memory_space=pltpu.VMEM)
    shapes = ((steps, width), (steps, width, width), (width, width))
    results = pl.pallas_call(
        kernel16,
        out_shape=tuple(pltpu.VMEM(s, F32) for s in shapes),
        in_specs=[pl.BlockSpec(memory_space=pltpu.HBM)] * 3,
        out_specs=(vmem,) * 3,
        scratch_shapes=[
            pltpu.VMEM((steps, width, width), F32),
            pltpu.VMEM((steps, width), F32),
            pltpu.VMEM((steps, width, width), F32),
            pltpu.VMEM((steps, slab, width), F32),
            pltpu.VMEM((steps - 1, width, width), F32),
            pltpu.VMEM((4, slab, width), F32),
            pltpu.VMEM((slab, width), F32),
            pltpu.VMEM((slab, width), F32),
            pltpu.VMEM((slab, width), F32),
            pltpu.VMEM((packed, width), F32),
            pltpu.VMEM((4, packed, width), F32),
            pltpu.VMEM((packed, width), F32),
            pltpu.VMEM((packed, width), F32),
            pltpu.VMEM((packed, width), F32),
            pltpu.VMEM((packed, width), F32),
            pltpu.VMEM((packed, width), F32),
            pltpu.VMEM((packed, width), F32),
            pltpu.VMEM((2, 10, rows, width), F32),
            pltpu.VMEM((4, rows, width), F32),
            pltpu.VMEM((2, rows, width), F32),
            pltpu.VMEM((2 * width, 2 * steps * width), BF16),
            pltpu.VMEM((steps, width, 2 * width), BF16),
            pltpu.VMEM((2 * width, 2 * width), BF16),
            pltpu.VMEM((width, 2 * width), BF16),
            dma((4,)), dma, dma((4,)), dma, dma((2,)), dma, dma((2,)), dma, dma, dma, pltpu.SemaphoreType.REGULAR,
        ],
        compiler_params=pltpu.CompilerParams(collective_id=0, has_side_effects=True),
    )(gains, offsets, cov_terms)
    results = [pltpu.with_memory_space_constraint(r, pltpu.VMEM) for r in results]
    return pl.pallas_call(
        write_out,
        out_shape=tuple(jax.ShapeDtypeStruct(s, F32) for s in shapes),
        in_specs=[vmem] * 3,
        out_specs=(pl.BlockSpec(memory_space=pl.ANY),) * 3,
        scratch_shapes=[dma((3,))],
    )(*results)


def solution(mesh):
    n = mesh.shape["tm"]
    in_specs = (P(("seq", "tm"), None, None), P(("seq", "tm"), None), P(("seq", "tm"), None, None))
    out_specs = (P(("seq", "tm"), None), P(("seq", "tm"), None, None), P("seq", None))
    return jax.shard_map(
        local16 if n == 16 and mesh.shape["seq"] == 2 else functools.partial(local, n), mesh=mesh, in_specs=in_specs, out_specs=out_specs, check_vma=False
    )
```

```python
import functools

import jax
import jax.numpy as jnp
from jax import lax
from jax.experimental import pallas as pl
from jax.experimental.pallas import tpu as pltpu
from jax.sharding import PartitionSpec as P

F32 = jnp.float32
BF16 = jnp.bfloat16
PAD = 8
GROUP = 16


def split(x):
    hi = x.astype(BF16)
    return hi, (x - hi.astype(F32)).astype(BF16)


def left(x):
    return jnp.concatenate(split(x), axis=1)


def right(w):
    both = jnp.concatenate(split(w), axis=1)
    return jnp.concatenate([both, both], axis=0)


def fold(x):
    half = x.shape[1] // 2
    return x[:, :half] + x[:, half:]


def mul(x, w):
    return fold(jnp.dot(x, w, preferred_element_type=F32))


def kernel(
    n, gains, offsets, covs, means_out, covs_out, mom_out,
    own, ring, suf, z_snd, z_near, top_snd, top_rcv,
    mom, rs_buf, bf_snd, bf_rcv, red, mom_all, mean_rows,
    ring_s, ring_r, z_s, z_r, rs_s, rs_r, bf_s, bf_r, ag_s, ag_r, out_s,
):
    steps, width = gains.shape[0], gains.shape[1]
    lean = width + PAD
    me = lax.axis_index("tm")
    levels = (n.bit_length() - 1) // 2
    quarter = n // 4
    rows = width // GROUP
    place = lax.rem(me, GROUP)
    base = me - place

    def flip(step):
        return me + step * (1 - 2 * lax.rem(lax.div(me, step), 2))

    def digit_of(stride):
        return lax.rem(lax.div(me, stride), 4)

    def peer(stride, j):
        digit = digit_of(stride)
        return me + stride * (lax.rem(digit + j, 4) - digit)

    peers = [base + lax.rem(place + j, GROUP) for j in range(1, GROUP)]
    peers += [peer(4**l, j) for l in range(2, levels) for j in (1, 2, 3)]
    barrier = pltpu.get_barrier_semaphore()
    for to in peers:
        pl.semaphore_signal(barrier, inc=1, device_id={"tm": to}, device_id_type=pl.DeviceIdType.MESH)

    def send(src, dst, s, r, to):
        return pltpu.make_async_remote_copy(
            src_ref=src, dst_ref=dst, send_sem=s, recv_sem=r,
            device_id={"tm": to}, device_id_type=pl.DeviceIdType.MESH,
        )

    def compose(e, f):
        e_psi = e[lean:]
        x = mul(left(f), right(e_psi))
        p = e[:width] + mul(left(e_psi.T), right(x[:width]))
        out = [p, e[width:lean] + x[width:lean]]
        if f.shape[0] > lean:
            out.append(x[lean:])
        return jnp.concatenate(out, axis=0)

    for t in reversed(range(steps)):
        gain = gains[t]
        if t == steps - 1:
            gain = jnp.where(me == n - 1, jnp.zeros_like(gain), gain)
        offset = jnp.broadcast_to(offsets[t : t + 1, :], (PAD, width))
        element = jnp.concatenate([covs[t], offset, gain.T], axis=0)
        own[t] = element if t == steps - 1 else compose(element, own[t + 1])

    def absorb(f):
        for t in range(steps):
            own[t, : f.shape[0]] = compose(own[t], f)

    pl.semaphore_wait(barrier, len(peers))

    def deferred(l):
        digit = digit_of(4**l)

        @pl.when(digit == 0)
        def _():
            suf[...] = compose(ring[l, 1], suf[...])

        @pl.when(digit == 2)
        def _():
            suf[...] = ring[l, 3]

        @pl.when(digit < 3)
        def _():
            absorb(suf[...])

    sends = []
    total = own[0]
    for l in range(levels - 1):
        digit = digit_of(4**l)
        ring[l, digit] = total
        started = []
        for j in (2, 1, 3):
            c = send(
                ring.at[l, digit], ring.at[l, digit], ring_s.at[l, j - 1], ring_r.at[l, j - 1], peer(4**l, j)
            )
            c.start()
            started.append(c)
        if l:
            deferred(l - 1)
        for j in (1, 2, 3):
            came = lax.rem(digit + 4 - j, 4)
            send(
                ring.at[l, came], ring.at[l, came], ring_s.at[l, j - 1], ring_r.at[l, j - 1], peer(4**l, j)
            ).wait_recv()
        sends += started
        high = compose(ring[l, 2], ring[l, 3])
        total = compose(compose(ring[l, 0], ring[l, 1]), high)
        suf[...] = high
    z_snd[...] = total

    q = lax.div(me, quarter)
    down, down2 = lax.rem(me + n - quarter, n), lax.rem(me + n - 2 * quarter, n)
    part = pl.ds(0, lean)
    near_full = send(z_snd, z_near, z_s.at[0], z_r.at[0], down)
    near_lean = send(z_snd.at[part], z_near.at[part], z_s.at[0], z_r.at[0], down)
    top_far = send(top_snd, top_rcv, z_s.at[1], z_r.at[1], down2)
    top_near = send(top_snd, top_rcv, z_s.at[2], z_r.at[1], down)

    @pl.when(q == 3)
    def _():
        near_lean.start()

    @pl.when(q == 1)
    def _():
        near_full.start()

    deferred(levels - 2)

    @pl.when(q == 3)
    def _():
        near_lean.wait_send()

    @pl.when(q == 2)
    def _():
        near_lean.wait_recv()
        top_snd[...] = compose(z_snd[...], z_near[part, :])
        top_far.start()
        top_near.start()
        absorb(z_near[part, :])
        top_far.wait_send()
        top_near.wait_send()

    @pl.when(q == 0)
    def _():
        near_full.wait_recv()
        absorb(z_near[...])

    @pl.when(q < 2)
    def _():
        top_near.wait_recv()
        absorb(top_rcv[...])

    @pl.when(q == 1)
    def _():
        near_full.wait_send()

    out_copies = []
    for t in range(steps):
        out_copies.append(pltpu.make_async_copy(own.at[t, pl.ds(0, width)], covs_out.at[t], out_s.at[t]))
    means = jnp.concatenate([own[t, width : width + 1] for t in range(steps)], axis=0)
    mean_rows[...] = means
    out_copies.append(pltpu.make_async_copy(mean_rows, means_out, out_s.at[steps]))
    sums = own[0, :width]
    for t in range(1, steps):
        sums = sums + own[t, :width]
    m_hi, m_lo = split(means)
    outer = lambda u, v: lax.dot_general(u, v, (((0,), (0,)), ((), ())), preferred_element_type=F32)
    sums = sums + (outer(m_hi, m_hi) + (outer(m_hi, m_lo) + outer(m_lo, m_hi)))
    mom[...] = sums * (1.0 / (steps * n))

    def group_rows(k):
        return pl.ds(pl.multiple_of(k * rows, rows), rows)

    for j in range(1, GROUP):
        to = lax.rem(place + j, GROUP)
        c = send(mom.at[group_rows(to)], rs_buf.at[j - 1], rs_s.at[j - 1], rs_r.at[j - 1], base + to)
        c.start()
        sends.append(c)
    for c in out_copies:
        c.start()
    acc = mom[group_rows(place), :]
    for c, j in zip(sends[1 - GROUP :], range(1, GROUP)):
        c.wait_recv()
        acc = acc + rs_buf[j - 1]
    k = 0
    while GROUP << k < n:
        bf_snd[k] = acc
        c = send(bf_snd.at[k], bf_rcv.at[k], bf_s.at[k], bf_r.at[k], flip(GROUP << k))
        c.start()
        c.wait()
        acc = acc + bf_rcv[k]
        k += 1
    red[...] = acc
    gather = []
    for j in range(1, GROUP):
        to = lax.rem(place + j, GROUP)
        c = send(red, mom_all.at[group_rows(place)], ag_s.at[j - 1], ag_r.at[j - 1], base + to)
        c.start()
        gather.append(c)
    mom_all[group_rows(place), :] = acc
    for c in sends + gather:
        c.wait_send()
    for c in out_copies:
        c.wait()
    for c in gather:
        c.wait_recv()
    last = pltpu.make_async_copy(mom_all, mom_out, out_s.at[steps + 1])
    last.start()
    last.wait()


def hand_over(a, b, c, a_out, b_out, c_out, sems):
    copies = [
        pltpu.make_async_copy(x, y, sems.at[i])
        for i, (x, y) in enumerate(((b, b_out), (c, c_out), (a, a_out)))
    ]
    for copy in copies:
        copy.start()
    for copy in copies:
        copy.wait()


def local(n, gains, offsets, cov_terms):
    steps, width = gains.shape[0], gains.shape[1]
    levels = (n.bit_length() - 1) // 2
    assert n == 4**levels and levels > 1
    slab, lean, rows = 2 * width + PAD, width + PAD, width // GROUP
    far = max(1, (n // GROUP).bit_length() - 1)
    dma = pltpu.SemaphoreType.DMA
    vmem = pl.BlockSpec(memory_space=pltpu.VMEM)
    any_space = pl.BlockSpec(memory_space=pl.ANY)
    shapes = (
        jax.ShapeDtypeStruct((steps, width), F32),
        jax.ShapeDtypeStruct((steps, width, width), F32),
        jax.ShapeDtypeStruct((width, width), F32),
    )
    results = pl.pallas_call(
        functools.partial(kernel, n),
        out_shape=shapes,
        in_specs=[vmem] * 3,
        out_specs=(any_space,) * 3,
        scratch_shapes=[
            pltpu.VMEM((steps, slab, width), F32),
            pltpu.VMEM((levels - 1, 4, slab, width), F32),
            pltpu.VMEM((slab, width), F32),
            pltpu.VMEM((slab, width), F32),
            pltpu.VMEM((slab, width), F32),
            pltpu.VMEM((lean, width), F32),
            pltpu.VMEM((lean, width), F32),
            pltpu.VMEM((width, width), F32),
            pltpu.VMEM((GROUP - 1, rows, width), F32),
            pltpu.VMEM((far, rows, width), F32),
            pltpu.VMEM((far, rows, width), F32),
            pltpu.VMEM((rows, width), F32),
            pltpu.VMEM((width, width), F32),
            pltpu.VMEM((steps, width), F32),
            dma((levels - 1, 3)), dma((levels - 1, 3)),
            dma((3,)), dma((2,)),
            dma((GROUP - 1,)), dma((GROUP - 1,)),
            dma((far,)), dma((far,)),
            dma((GROUP - 1,)), dma((GROUP - 1,)),
            dma((steps + 2,)),
        ],
        compiler_params=pltpu.CompilerParams(collective_id=0, has_side_effects=True),
    )(gains, offsets, cov_terms)
    return pl.pallas_call(
        hand_over,
        out_shape=shapes,
        in_specs=[vmem] * 3,
        out_specs=(any_space,) * 3,
        scratch_shapes=[dma((3,))],
    )(*results)


def pack(s):
    half = s.shape[1] // 2
    row = lax.broadcasted_iota(jnp.int32, (half, 2 * half), 0)
    col = lax.broadcasted_iota(jnp.int32, (half, 2 * half), 1)
    low = s[half : 2 * half]
    both = jnp.where(jnp.logical_or(col >= half, row >= col), s[:half], pltpu.roll(low, half, 1))
    diag = jnp.sum(jnp.where(col - half == row, low, 0.0), axis=0, keepdims=True)
    first = lax.broadcasted_iota(jnp.int32, (PAD, 2 * half), 0) == 0
    return jnp.concatenate([both, jnp.where(first, s[2 * half :], diag)], axis=0)


def unpack(p):
    half = p.shape[1] // 2
    row = lax.broadcasted_iota(jnp.int32, (half, 2 * half), 0)
    col = lax.broadcasted_iota(jnp.int32, (half, 2 * half), 1)
    m = p[:half]
    turned = jnp.concatenate([m, m], axis=0).T
    top = jnp.where(jnp.logical_or(col >= half, row >= col), m, turned[:half])
    k = col - half
    right_low = jnp.where(row < k, pltpu.roll(m, half, 1), jnp.where(row == k, p[half + 1 : half + 2], turned[:half]))
    low = jnp.where(col < half, turned[half:], right_low)
    mean = jnp.broadcast_to(p[half : half + 1], (PAD, 2 * half))
    return jnp.concatenate([top, low, mean], axis=0)


def kernel16(
    gains_in, offsets_in, covs_in, means_out, covs_out, mom_out,
    gains, offsets, covs, own, held, ring, acc, suf, z_near, sym_snd, sym_rcv, z_sym, z_sym_rcv, top_snd, top_rcv, mom, mom_rcv, rs_buf, pre_buf, red,
    own_right, own_both, z_right, z_both,
    in_s, ring_s, ring_r, z_s, z_r, rs_s, rs_r, pre_r, ag_s, ag_r, pace,
):
    steps, width = gains.shape[0], gains.shape[1]
    lean = width + PAD
    n = 16
    me, core = lax.axis_index("tm"), lax.axis_index("seq")
    digit, q = lax.rem(me, 4), lax.div(me, 4)
    rows = (width // 2 + PAD) // 3
    central = [4 + i for i in range(4)]
    hosts = [(4, 0), (5, 1), (6, 2), (1, 1), (2, 2)]
    is_central = jnp.logical_and(q == 1, core == 1)
    is_wide = jnp.logical_and(is_central, digit < 3)
    is_near = jnp.logical_and(core == 1, jnp.logical_or(me == 1, me == 2))
    is_host = jnp.logical_or(is_wide, is_near)
    is_last = me == n - 1
    part, psi = pl.ds(0, lean), pl.ds(lean, width)
    packed = width // 2 + PAD
    dx, dy = 1 - 2 * lax.rem(digit, 2), 2 - 4 * lax.div(digit, 2)

    def at(tm, seq):
        return {"tm": tm, "seq": seq}

    def send(src, dst, s, r, to):
        return pltpu.make_async_remote_copy(
            src_ref=src, dst_ref=dst, send_sem=s, recv_sem=r,
            device_id=to, device_id_type=pl.DeviceIdType.MESH,
        )

    def landed(ref, sem):
        send(ref, ref, sem, sem, at(lax.rem(me + 1, n), core)).wait_recv()

    def sent(ref, sem):
        send(ref, ref, sem, sem, at(lax.rem(me + 1, n), core)).wait_send()

    barrier = pltpu.get_barrier_semaphore()

    def greet(tm, seq):
        pl.semaphore_signal(barrier, inc=1, device_id=at(tm, seq), device_id_type=pl.DeviceIdType.MESH)

    @pl.when(is_central)
    def _():
        for j in range(1, n):
            greet(lax.rem(me + j, n), core)
        for j in range(n):
            greet(j, 0)

    @pl.when(jnp.logical_not(is_central))
    def _():
        @pl.when(jnp.logical_or(q < 3, digit < 2))
        def _():
            for step in (dx, dy, dx + dy):
                greet(me + step, core)

        @pl.when(jnp.logical_and(q == 3, digit == 2))
        def _():
            greet(me + 1, core)

        for host in central:
            greet(host, 1)

        @pl.when(core == 1)
        def _():
            greet(me - digit + 2, 0)

        @pl.when(q == 0)
        def _():
            greet(8 + digit, core)

        @pl.when(is_near)
        def _():
            for j in range(8):
                greet(j, 0)
            for j in range(1, 4):
                greet(lax.rem(me + j, 4), 1)
            for seq in (0, 1):
                greet(8 + me, seq)
                greet(12 + me, seq)

        @pl.when(q == 2)
        def _():
            greet(12 + lax.rem(digit, 2), core)

        @pl.when(jnp.logical_and(q < 2, core == 0))
        def _():
            greet(me + 4, core)

    fetch = []
    for t in range(steps):
        fetch.append(pltpu.make_async_copy(gains_in.at[t], gains.at[t], in_s.at[t]))
    for t in range(steps):
        fetch.append(pltpu.make_async_copy(covs_in.at[t], covs.at[t], in_s.at[steps + t]))
    fetch.append(pltpu.make_async_copy(offsets_in, offsets, in_s.at[2 * steps]))
    for c in fetch:
        c.start()

    def compose(e, f):
        e_psi = e[lean:]
        x = mul(left(f), right(e_psi))
        p = e[:width] + mul(left(e_psi.T), right(x[:width]))
        out = [p, e[width:lean] + x[width:lean]]
        if f.shape[0] > lean:
            out.append(x[lean:])
        return jnp.concatenate(out, axis=0)

    def slot(d):
        return lax.rem(d + 4 - digit, 4)

    def total_of(d):
        return ring[slot(d)]

    def exchange(src, dst):
        upper, lower = jnp.logical_or(q < 3, digit >= 2), jnp.logical_or(q < 3, digit != 2)
        for step, needed in ((dx + dy, upper), (dy, upper), (dx, lower)):
            there = lax.rem(4 - step, 4)
            pl.when(needed)(send(src, dst(there), ring_s, ring_r.at[there], at(me + step, core)).start)

    def exchange_psi():
        exchange(ring.at[0, psi], lambda there: ring.at[there, psi])

    for c in fetch[:steps]:
        c.wait()
    ready = jnp.where(q == 0, 7, jnp.where(q == 1, 8, jnp.where(q == 2, 9 - core, jnp.where(digit < 2, 7, 4 + digit))))
    ready = ready + jnp.where(jnp.logical_and(core == 0, jnp.logical_and(digit == 2, q != 1)), 4, 0)
    ready = ready + jnp.where(q < 2, 2, jnp.where(lax.rem(digit, 3) == 0, 0, 1)) - jnp.where(is_near, 1, 0)
    ready = jnp.where(is_central, 2 * n - 1, ready)

    def local_total(reach):
        cov, mean = covs[0], offset[0]
        for t in range(1, steps):
            e = reach[t - 1]
            x = mul(left(jnp.concatenate([covs[t], offset[t]], axis=0)), right(e.T))
            cov = cov + mul(left(e), right(x[:width]))
            mean = mean + x[width:]
        ring[0, part] = jnp.concatenate([cov, mean], axis=0)
        sym_snd[...] = pack(jnp.concatenate([cov, mean], axis=0))

    def reached():
        reach = [gains[0]]
        for t in range(1, steps - 1):
            reach.append(mul(left(reach[-1]), right(gains[t])))
        return reach

    @pl.when(jnp.logical_not(is_last))
    def _():
        reach = reached()
        for t, e in enumerate(reach):
            held[t] = e
        ring[0, psi] = mul(left(reach[-1]), right(gains[steps - 1])).T

    for c in fetch[steps:]:
        c.wait()
    offset = [jnp.broadcast_to(offsets[t : t + 1, :], (PAD, width)) for t in range(steps)]

    @pl.when(is_last)
    def _():
        ring[0, psi] = jnp.zeros((width, width), F32)
        local_total(reached())

    pl.semaphore_wait(barrier, ready)

    @pl.when(jnp.logical_and(jnp.logical_not(is_last), core == 0))
    def _():
        exchange_psi()

    @pl.when(jnp.logical_not(is_last))
    def _():
        local_total([held[t] for t in range(steps - 1)])

    @pl.when(jnp.logical_or(core == 0, is_last))
    def _():
        exchange(sym_snd, lambda there: sym_rcv.at[there])

        @pl.when(jnp.logical_and(core == 0, digit == 3))
        def _():
            pl.semaphore_signal(pace, inc=1, device_id=at(me - 1, 0), device_id_type=pl.DeviceIdType.MESH)

    own[0] = ring[0]
    run = jnp.where(is_last, jnp.zeros_like(gains[0]), gains[steps - 1])
    run = jnp.concatenate([covs[steps - 1], offset[steps - 1], run.T], axis=0)
    own[steps - 1] = run
    for t in reversed(range(1, steps - 1)):
        run = compose(jnp.concatenate([covs[t], offset[t], gains[t].T], axis=0), run)
        own[t] = run

    @pl.when(jnp.logical_and(core == 0, digit == 2))
    def _():
        pl.semaphore_wait(pace, 1)
        for j in range(4):
            pl.semaphore_signal(pace, inc=1, device_id=at(me - 2 + j, 1), device_id_type=pl.DeviceIdType.MESH)

    @pl.when(core == 1)
    def _():
        pl.semaphore_wait(pace, 1)

        @pl.when(jnp.logical_not(is_last))
        def _():
            exchange_psi()
            exchange(sym_snd, lambda there: sym_rcv.at[there])

    def prepare():
        for t in range(steps):
            e = own[t, psi]
            own_right[:, pl.ds(2 * t * width, 2 * width)] = right(e)
            own_both[t] = left(e.T)

    def apply(f):
        x = jnp.dot(left(f), own_right[...], preferred_element_type=F32)
        out = []
        for t in range(steps):
            xt = fold(x[:, 2 * t * width : 2 * (t + 1) * width])
            cov = own[t, :width] + mul(own_both[t], right(xt[:width]))
            out.append((cov, own[t, width:lean] + xt[width:lean], xt[lean:]))
        return out

    def absorb(f):
        for t, (cov, mean, rest) in enumerate(apply(f)):
            own[t, :width] = cov
            own[t, width:lean] = mean
            if f.shape[0] > lean:
                own[t, psi] = rest

    def finish(found):
        means = jnp.concatenate([mean[:1] for _, mean in found], axis=0)
        sums = found[0][0]
        for cov, _ in found[1:]:
            sums = sums + cov
        m_hi, m_lo = split(means)
        outer = lambda u, v: lax.dot_general(u, v, (((0,), (0,)), ((), ())), preferred_element_type=F32)
        sums = sums + (outer(m_hi, m_hi) + (outer(m_hi, m_lo) + outer(m_lo, m_hi)))
        mom[...] = pack(jnp.concatenate([sums * (1.0 / (steps * n)), jnp.zeros((PAD, width), F32)], axis=0))
        means_out[...] = means
        for t, (cov, _) in enumerate(found):
            covs_out[t] = cov

    def block(i):
        return pl.ds(i * rows, rows)

    mine = pl.ds(pl.multiple_of(lax.rem(digit, 3) * rows, PAD), rows)

    def arrive(d):
        here = slot(d)

        @pl.when(digit != d)
        def _():
            landed(ring.at[here, pl.ds(0, packed + width)], ring_r.at[here])
            ring[here, part] = unpack(sym_rcv[here])

    def state_of(base, f, after, before):
        x = mul(left(f), after)
        cov = base[:width] + mul(before, right(x[:width]))
        return jnp.concatenate([cov, base[width:lean] + x[width:]], axis=0)

    def hold(e):
        z_right[...] = right(e)
        z_both[...] = left(e.T)

    down, down2 = lax.rem(me + n - 4, n), lax.rem(me + n - 8, n)
    near_sym = send(z_sym, z_sym_rcv, z_s, z_r.at[0], at(down, core))
    near_psi = send(acc.at[psi], z_near.at[psi], z_s, z_r.at[0], at(down, core))
    top_far = send(top_snd, top_rcv, z_s, z_r.at[1], at(down2, core))
    top_near = send(top_snd, top_rcv, z_s, z_r.at[1], at(down, core))
    far_sym = send(z_sym, z_sym_rcv, z_s, z_r.at[0], at(lax.rem(me + n - 2, n), core))

    @pl.when(jnp.logical_and(q == 3, digit < 2))
    def _():
        arrive(0)
        arrive(1)
        acc[...] = compose(total_of(0), total_of(1))
        hold(acc[psi, :])
        arrive(2)
        e = total_of(2)[lean:]
        own_right[:, pl.ds(0, 2 * width)] = right(e)
        own_both[0] = left(e.T)
        landed(sym_rcv.at[slot(3)], ring_r.at[slot(3)])
        newest = unpack(sym_rcv[slot(3)])
        state = state_of(total_of(2)[:lean], newest, own_right[:, pl.ds(0, 2 * width)], own_both[0])
        suf[part, :] = state
        z_sym[...] = pack(state_of(acc[part, :], state, z_right[...], z_both[...]))
        far_sym.start()
        near_sym.start()

        @pl.when(digit == 0)
        def _():
            suf[part, :] = compose(total_of(1), suf[part, :])

    @pl.when(jnp.logical_and(q == 3, digit == 2))
    def _():
        landed(sym_rcv.at[slot(3)], ring_r.at[slot(3)])
        suf[part, :] = unpack(sym_rcv[slot(3)])

    @pl.when(q < 3)
    def _():
        arrive(3)
        acc[...] = total_of(3)
        for d in (2, 1, 0):
            @pl.when(digit == d)
            def _():
                suf[...] = acc[...]

            arrive(d)
            acc[...] = compose(total_of(d), acc[...])

    @pl.when(q == 1)
    def _():
        z_sym[...] = pack(acc[part, :])
        near_sym.start()
        near_psi.start()

    @pl.when(q == 2)
    def _():
        hold(acc[psi, :])

    prepare()

    @pl.when(digit < 3)
    def _():
        @pl.when(q == 3)
        def _():
            absorb(suf[part, :])

        @pl.when(q < 3)
        def _():
            absorb(suf[...])
            prepare()

    @pl.when(q == 2)
    def _():
        near_sym.wait_recv()
        near = unpack(z_sym_rcv[...])
        top_snd[...] = pack(state_of(acc[part, :], near, z_right[...], z_both[...]))
        top_far.start()
        top_near.start()
        absorb(near)

    @pl.when(q == 0)
    def _():
        landed(z_near.at[pl.ds(0, packed + width)], z_r.at[0])
        z_near[part, :] = unpack(z_sym_rcv[...])
        absorb(z_near[...])
        prepare()

    @pl.when(q < 2)
    def _():
        top_near.wait_recv()
        finish([found[:2] for found in apply(unpack(top_rcv[...]))])

        def scatter(host, at_block):
            send(mom.at[at_block], rs_buf.at[core, me], rs_s, rs_r.at[core], at(host, 1)).start()

        across_host = 7 - me
        theirs = pl.ds(pl.multiple_of(lax.rem(lax.rem(across_host, 4), 3) * rows, PAD), rows)

        @pl.when(lax.rem(across_host, 4) * lax.rem(me, 4) * across_host + jnp.where(me == 3, 1, 0) > 0)
        def _():
            scatter(across_host, theirs)

        for host, i in hosts:
            @pl.when(jnp.logical_and(across_host != host, jnp.logical_or(me != host, core == 0)))
            def _():
                scatter(host, block(i))

    @pl.when(q >= 2)
    def _():
        finish([(own[t, :width], own[t, width:lean]) for t in range(steps)])

        @pl.when(jnp.logical_and(q == 3, digit < 2))
        def _():
            near_sym.wait_send()
            far_sym.wait_send()

        for step in (dx + dy, dx, dy):
            to = digit + step
            theirs = pl.ds(pl.multiple_of(lax.rem(to, 3) * rows, PAD), rows)
            part_sum = send(mom.at[theirs], pre_buf.at[lax.rem(4 - step, 4)], rs_s, pre_r, at(me + step, core))
            pl.when(to < 3)(part_sum.start)

        @pl.when(digit < 3)
        def _():
            landed(pre_buf.at[pl.ds(1, 3)], pre_r)
            pre_buf[0] = (mom[mine, :] + pre_buf[1]) + (pre_buf[2] + pre_buf[3])
            for to, wanted in ((digit, digit > 0), (4 + digit, digit < 3)):
                upward = send(pre_buf.at[0], rs_buf.at[core, 6 + q], rs_s, rs_r.at[core], at(to, 1))
                pl.when(wanted)(upward.start)

    @pl.when(is_host)
    def _():
        rs_buf[1, me] = mom[mine, :]
        def gather(to, p):
            copy = send(red.at[p], mom_rcv.at[mine], ag_s, ag_r, at(to, p))
            if to == 0:
                pl.when(me < 5)(copy.start)
            elif p == 0 or to not in (4, 5, 6):
                copy.start()
            else:
                pl.when(me != to)(copy.start)

        for p in (0, 1):
            landed(rs_buf.at[p, pl.ds(0, 10 - p)], rs_r.at[p])
            parts = [rs_buf[p, j] for j in range(10)]
            while len(parts) > 1:
                parts = [u + v for u, v in zip(parts[::2], parts[1::2])] + parts[len(parts) & ~1 :]
            red[p] = parts[0]
            gather(0, p)
            if p == 1:
                @pl.when(is_wide)
                def _():
                    mom_rcv[mine, :] = parts[0]

        @pl.when(is_wide)
        def _():
            for some in (range(1, 8), range(8, n)):
                for p in (0, 1):
                    for to in some:
                        gather(to, p)

    @pl.when(is_wide)
    def _():
        landed(mom_rcv.at[pl.ds(0, 2 * rows)], ag_r)

    @pl.when(jnp.logical_not(is_wide))
    def _():
        landed(mom_rcv, ag_r)

    mom_out[...] = unpack(mom_rcv[...])[:width]

    def sent_blocks(count, sem):
        while count:
            some = min(count, 10)
            sent(rs_buf.at[0, pl.ds(0, some)], sem)
            count -= some

    @pl.when(is_near)
    def _():
        sent_blocks(2, ag_s)

    @pl.when(is_wide)
    def _():
        sent_blocks(29, ag_s)

        @pl.when(me == 4)
        def _():
            sent_blocks(2, ag_s)

    sent_blocks(3, rs_s)

    @pl.when(jnp.where(q < 2, 1, lax.rem(digit, 3)) > 0)
    def _():
        sent_blocks(1, rs_s)

    @pl.when(jnp.logical_and(q < 2, jnp.logical_not(is_host)))
    def _():
        sent_blocks(1, rs_s)

    @pl.when(q < 3)
    def _():
        sent(sym_rcv.at[pl.ds(1, 3)], ring_s)
        sent(ring.at[pl.ds(1, 3), psi], ring_s)

    @pl.when(q == 3)
    def _():
        @pl.when(digit < 3)
        def _():
            sent(ring.at[1, pl.ds(0, packed + width)], ring_s)

        @pl.when(digit == 2)
        def _():
            sent(ring.at[1, pl.ds(0, packed + width)], ring_s)

        @pl.when(digit == 3)
        def _():
            sent(sym_rcv.at[pl.ds(1, 3)], ring_s)

    @pl.when(q == 1)
    def _():
        near_sym.wait_send()
        near_psi.wait_send()

    @pl.when(q == 2)
    def _():
        top_far.wait_send()
        top_near.wait_send()


def write_out(a, b, c, a_out, b_out, c_out, sems):
    copies = [
        pltpu.make_async_copy(x, y, sems.at[i])
        for i, (x, y) in enumerate(((b, b_out), (c, c_out), (a, a_out)))
    ]
    for copy in copies:
        copy.start()
    for copy in copies:
        copy.wait()


def local16(gains, offsets, cov_terms):
    steps, width = gains.shape[0], gains.shape[1]
    slab, packed = 2 * width + PAD, width // 2 + PAD
    rows = packed // 3
    assert packed == 3 * rows and rows % PAD == 0
    dma = pltpu.SemaphoreType.DMA
    vmem = pl.BlockSpec(memory_space=pltpu.VMEM)
    shapes = ((steps, width), (steps, width, width), (width, width))
    results = pl.pallas_call(
        kernel16,
        out_shape=tuple(pltpu.VMEM(s, F32) for s in shapes),
        in_specs=[pl.BlockSpec(memory_space=pltpu.HBM)] * 3,
        out_specs=(vmem,) * 3,
        scratch_shapes=[
            pltpu.VMEM((steps, width, width), F32),
            pltpu.VMEM((steps, width), F32),
            pltpu.VMEM((steps, width, width), F32),
            pltpu.VMEM((steps, slab, width), F32),
            pltpu.VMEM((steps - 1, width, width), F32),
            pltpu.VMEM((4, slab, width), F32),
            pltpu.VMEM((slab, width), F32),
            pltpu.VMEM((slab, width), F32),
            pltpu.VMEM((slab, width), F32),
            pltpu.VMEM((packed, width), F32),
            pltpu.VMEM((4, packed, width), F32),
            pltpu.VMEM((packed, width), F32),
            pltpu.VMEM((packed, width), F32),
            pltpu.VMEM((packed, width), F32),
            pltpu.VMEM((packed, width), F32),
            pltpu.VMEM((packed, width), F32),
            pltpu.VMEM((packed, width), F32),
            pltpu.VMEM((2, 10, rows, width), F32),
            pltpu.VMEM((4, rows, width), F32),
            pltpu.VMEM((2, rows, width), F32),
            pltpu.VMEM((2 * width, 2 * steps * width), BF16),
            pltpu.VMEM((steps, width, 2 * width), BF16),
            pltpu.VMEM((2 * width, 2 * width), BF16),
            pltpu.VMEM((width, 2 * width), BF16),
            dma((2 * steps + 1,)), dma, dma((4,)), dma, dma((2,)), dma, dma((2,)), dma, dma, dma, pltpu.SemaphoreType.REGULAR,
        ],
        compiler_params=pltpu.CompilerParams(collective_id=0, has_side_effects=True),
    )(gains, offsets, cov_terms)
    results = [pltpu.with_memory_space_constraint(r, pltpu.VMEM) for r in results]
    return pl.pallas_call(
        write_out,
        out_shape=tuple(jax.ShapeDtypeStruct(s, F32) for s in shapes),
        in_specs=[vmem] * 3,
        out_specs=(pl.BlockSpec(memory_space=pl.ANY),) * 3,
        scratch_shapes=[dma((3,))],
    )(*results)


def solution(mesh):
    n = mesh.shape["tm"]
    in_specs = (P(("seq", "tm"), None, None), P(("seq", "tm"), None), P(("seq", "tm"), None, None))
    out_specs = (P(("seq", "tm"), None), P(("seq", "tm"), None, None), P("seq", None))
    return jax.shard_map(
        local16 if n == 16 and mesh.shape["seq"] == 2 else functools.partial(local, n), mesh=mesh, in_specs=in_specs, out_specs=out_specs, check_vma=False
    )
```
